512 devices in a mesh: expert: 16 (over z, core), tensor: 32 (over x, y).
Axes of the slice: x: 4, y: 8, z: 8, core: 2. Of those that a mesh axis runs over, the one named last changes fastest.
Arguments:
- tokens: bfloat16 [2048, 5120], P('expert', 'tensor'), may hold values from -6 to 6
- routes: int32 [2048, 6], P('expert'), may hold values from 0 to 15, all different within a row; in each aligned block of 128 rows (0 to 127, 128 to 255, ...) at most 64 rows name the same one
- gates: float32 [2048, 6], P('expert'), may hold values from 0.05 to 0.35
- w_gate: bfloat16 [16, 1536, 5120], P('expert', 'tensor'), may hold values from -0.078125 to 0.078125
- w_up: bfloat16 [16, 1536, 5120], P('expert', 'tensor'), may hold values from -0.078125 to 0.078125
- w_down: bfloat16 [16, 1536, 5120], P('expert', None, 'tensor'), may hold values from -0.15625 to 0.15625
- shared_gate: bfloat16 [1536, 5120], P('tensor'), may hold values from -0.078125 to 0.078125
- shared_up: bfloat16 [1536, 5120], P('tensor'), may hold values from -0.078125 to 0.078125
- shared_down: bfloat16 [1536, 5120], P(None, 'tensor'), may hold values from -0.15625 to 0.15625
- vocab: bfloat16 [65536, 5120], P(('expert', 'tensor'))
- targets: int32 [64], replicated, may hold values from 0 to 65535
Outputs:
- layer_out: bfloat16 [2048, 5120], P('expert', 'tensor')
- loglik: float32 [64], replicated
The draws below stay inside these ranges and needn't reach their ends.
Inputs may be any that keep to these rules, and one draw needn't show every extreme that they name: `routes`: the tokens of one group name one expert at most 64 times; in every draw some group names some expert exactly 64 times.
All inputs are finite; a program needn't handle non-finite values.
Results may differ from the reference program's by a relative error of at most 0.0041.
Values may be sent and summed in bfloat16 or wider, within the bound.
No kernel may reach another device: no remote copies, remote signals or barrier semaphores. Data moves between devices by JAX's collectives and lax.ppermute only.
A program may use at most 64 MiB of HBM per device.

```python
import math
import jax
import jax.numpy as jnp
import numpy as np
from jax import lax

D = 5120
FF = 1536
TOPK = 6
EXPERTS = 16
TOK_E = 128
SCORE_E = 4
CAP = 64
TOKENS = 2048
SCORED = 64
V = 65536
N_EXPERT = 16


def draw_vocab(key, part):
    first, second = jax.random.split(key)
    position = jnp.arange(V, dtype=jnp.float32)[:, None] / V
    spread = jnp.exp(jax.random.uniform(second, (V, 1), jnp.float32, 0.0, math.log(3.0)))
    base = jax.random.normal(first, (V, D), jnp.float32)
    scale = 1.1 * spread * (1.0 + 0.6 * position)
    return (base * scale / math.sqrt(D)).astype(jnp.bfloat16)


def with_ends(values, rng, smallest, high):
    dims = values.shape
    spot = [jax.random.randint(jax.random.fold_in(rng, axis), (), 0, dims[axis]) for axis in range(len(dims))]
    values = values.at[tuple(spot)].set(smallest)
    longest = dims.index(max(dims))
    spot[longest] = (spot[longest] + 1) % dims[longest]
    return values.at[tuple(spot)].set(high)


def level_of(key, dims, cuts, low, high):
    def one(axis_at, blocks):
        heights = jax.random.uniform(jax.random.fold_in(jax.random.fold_in(key, 6), axis_at), (blocks,), jnp.float32, low / len(cuts), high / len(cuts))
        return jnp.repeat(jnp.exp(heights), dims[axis_at] // blocks).reshape((-1,) + (1,) * (len(dims) - axis_at - 1))

    loudness = one(*cuts[0])
    for cut in cuts[1:]:
        loudness = loudness * one(*cut)
    return loudness


def routed_block(rng, own, number, rows, number_of, top, limit, lean):
    sequence = jax.random.permutation(rng, number_of)
    heavy_load, common = shares(number_of, rows * top, limit, lean, True), shares(number_of, rows * top, limit, lean, False)
    places = jnp.arange(number_of)

    def named(lengths, offset_by):
        used = int((lengths > 0).sum())
        fixed = max(1, used // 4)
        moved = fixed + (places - fixed + offset_by * (used - fixed)) % max(1, number_of - fixed)
        return jnp.zeros((number_of,), jnp.int32).at[sequence[jnp.where(places < fixed, places, moved)]].set(jnp.asarray(lengths, jnp.int32))

    lengths = jnp.where(number % 4 == 0, named(heavy_load, number // 4), named(common, number - number // 4 - 1))
    mixed = jax.random.permutation(jax.random.fold_in(own, 3), number_of)
    source_of, receiver = mixed[0:number_of // 2 * 2:2], mixed[1:number_of // 2 * 2:2]
    slack = jnp.minimum(lengths[source_of] - 1, limit - lengths[receiver]) // 2
    slack = jnp.where((source_of == sequence[0]) | (receiver == sequence[0]) | (lengths[receiver] == 0), 0, jnp.maximum(slack, 0))
    moved = jax.random.randint(jax.random.fold_in(own, 4), (number_of // 2,), 0, 1 << 20) % (slack + 1)
    lengths = lengths.at[source_of].add(-moved).at[receiver].add(moved)
    labels = jnp.searchsorted(jnp.cumsum(lengths), jnp.arange(rows * top), side="right").astype(jnp.int32)
    table = labels.reshape(top, rows).T
    table = table[jax.random.permutation(jax.random.fold_in(own, 1), rows)]
    offset_by = jax.random.randint(jax.random.fold_in(own, 2), (rows, 1), 0, top)
    return jnp.take_along_axis(table, (jnp.arange(top)[None, :] + offset_by) % top, axis=1)


def shares(amount, total, reach, lean, full):
    weights = [(1 << 20) // math.isqrt(rank ** lean) + 1 for rank in range(1, amount + 1)]
    largest = reach if full else min(reach, max(-(-total // amount), total * weights[0] // sum(weights)))
    least = 1 if total - largest >= amount - 1 else 0
    counts, rest = [largest] + [least] * (amount - 1), total - largest - least * (amount - 1)
    while rest > 0:
        candidates = [i for i in range(1, amount) if counts[i] < largest] or [i for i in range(1, amount) if counts[i] < reach]
        mass, left = sum([weights[i] for i in candidates]), rest
        for i in candidates:
            addition = min(reach - counts[i], max(1, left * weights[i] // mass), rest)
            counts[i] = counts[i] + addition
            rest = rest - addition
    return np.array(counts)


def centred(stream_key, extent, width, reach, shards=(), kind=jnp.bfloat16):
    values = width * jax.random.normal(stream_key, extent, jnp.float32)
    if shards:
        values = values * level_of(stream_key, extent, shards, -0.22, 0.18)
    return jnp.clip(values, -reach, reach).astype(kind)


def setup_inputs(seed: int = 0) -> dict:
    keys = jax.random.split(jax.random.key(seed), 12)
    tokens = centred(keys[0], (TOKENS, D), 1.0, 6.0, ((0, 16), (1, 32)))
    routes_keys = jax.random.split(jax.random.fold_in(keys[1], 1), TOKENS // TOK_E)
    routes_turns = jax.random.permutation(jax.random.fold_in(keys[1], 3), TOKENS // TOK_E)
    routes = jax.vmap(lambda own, number: routed_block(jax.random.fold_in(keys[1], 2), own, number, TOK_E, EXPERTS, TOPK, CAP, 2))(routes_keys, routes_turns).reshape((TOKENS, TOPK))
    gates = jnp.clip(0.05 + 0.29999999 * jax.random.uniform(keys[2], (TOKENS, TOPK), jnp.float32) ** level_of(keys[2], (TOKENS, TOPK), ((0, 16),), -0.2, 0.2), 0.05, 0.35)
    w_gate = centred(keys[3], (EXPERTS, FF, D), D ** -0.5, 0.078125, ((0, 16), (1, 32)))
    w_up = centred(keys[4], (EXPERTS, FF, D), D ** -0.5, 0.078125, ((0, 16), (1, 32)))
    w_down = centred(keys[5], (EXPERTS, FF, D), FF ** -0.5, 0.15625, ((0, 16), (2, 32)))
    shared_gate = centred(keys[6], (FF, D), D ** -0.5, 0.078125, ((0, 32),))
    shared_up = centred(keys[7], (FF, D), D ** -0.5, 0.078125, ((0, 32),))
    shared_down = centred(keys[8], (FF, D), FF ** -0.5, 0.15625, ((1, 32),))
    vocab = draw_vocab(jax.random.fold_in(keys[11], 71), 0)
    targets = with_ends(jax.random.randint(keys[10], (SCORED,), 0, V), jax.random.fold_in(keys[10], 1), 0, V - 1).astype(jnp.int32)
    return {"tokens": tokens, "routes": routes, "gates": gates, "w_gate": w_gate, "w_up": w_up, "w_down": w_down, "shared_gate": shared_gate, "shared_up": shared_up, "shared_down": shared_down, "vocab": vocab, "targets": targets}


def slot_tables(routes, gates):
    picks = (routes[:, :, None] == jnp.arange(EXPERTS, dtype=jnp.int32)[None, None, :]).astype(jnp.int32)
    per_token = jnp.sum(picks, axis=1)
    earlier = jnp.cumsum(per_token, axis=0) - per_token
    slots = jnp.sum(picks * earlier[:, None, :], axis=2)
    places = (slots[:, :, None] == jnp.arange(CAP, dtype=jnp.int32)[None, None, :]).astype(jnp.float32)
    picked = picks.astype(jnp.float32)
    select = jnp.einsum("ikr,iks->rsi", picked, places, precision=lax.Precision.HIGHEST)
    weigh = jnp.einsum("ikr,iks,ik->rsi", picked, places, gates.astype(jnp.float32), precision=lax.Precision.HIGHEST)
    return select, weigh


def expert_block(operands):
    rows, weight_gate, weight_up, weight_down = operands
    gate = jnp.dot(rows, weight_gate.T, preferred_element_type=jnp.float32)
    upper = jnp.dot(rows, weight_up.T, preferred_element_type=jnp.float32)
    hidden = (jax.nn.silu(gate) * upper).astype(jnp.bfloat16)
    return jnp.dot(hidden, weight_down, preferred_element_type=jnp.float32).astype(jnp.bfloat16)


def reference(tokens, routes, gates, w_gate, w_up, w_down, shared_gate, shared_up, shared_down, vocab, targets):
    grouped = tokens.reshape(N_EXPERT, TOK_E, D)
    select, weigh = jax.vmap(slot_tables)(routes.reshape(N_EXPERT, TOK_E, TOPK), gates.reshape(N_EXPERT, TOK_E, TOPK))
    outgoing = jnp.einsum("grsi,gid->rgsd", select, grouped.astype(jnp.float32), precision=lax.Precision.HIGHEST).astype(jnp.bfloat16)
    rows = outgoing.reshape(EXPERTS, N_EXPERT * CAP, D)
    outputs = lax.map(expert_block, (rows, w_gate, w_up, w_down))
    back = outputs.reshape(EXPERTS, N_EXPERT, CAP, D).astype(jnp.float32)
    routed = jnp.einsum("grsi,rgsd->gid", weigh, back, precision=lax.Precision.HIGHEST).reshape(TOKENS, D)
    shared_g = jnp.dot(tokens, shared_gate.T, preferred_element_type=jnp.float32)
    shared_u = jnp.dot(tokens, shared_up.T, preferred_element_type=jnp.float32)
    shared_hidden = (jax.nn.silu(shared_g) * shared_u).astype(jnp.bfloat16)
    shared_out = jnp.dot(shared_hidden, shared_down, preferred_element_type=jnp.float32)
    layer_out = (tokens.astype(jnp.float32) + shared_out + routed).astype(jnp.bfloat16)
    scored = layer_out.reshape(N_EXPERT, TOK_E, D)[:, TOK_E - SCORE_E:, :].reshape(SCORED, D)
    logits = jnp.dot(scored, vocab.T, preferred_element_type=jnp.float32)
    totals = jnp.sum(jnp.exp(logits), axis=1)
    target_logit = jnp.take_along_axis(logits, targets[:, None].astype(jnp.int32), axis=1)[:, 0]
    return layer_out, target_logit - jnp.log(totals)
```

```python
import jax
import jax.numpy as jnp
from jax import lax
from jax.experimental import pallas as pl
from jax.experimental.pallas import tpu as pltpu
from jax.sharding import Mesh
from jax.sharding import PartitionSpec as P

SCORE_E = 4
F32 = jnp.float32
BF16 = jnp.bfloat16
LINE = ("z", "core")
PLANE = ("x", "y")
VMEM_LIMIT = 48 << 20


def call(body, outs, args, scalars=0, scratch=(), flops=0):
    specs = [
        pl.BlockSpec(memory_space=pltpu.SMEM if n < scalars else pltpu.VMEM) for n in range(len(args))
    ]
    moved = sum(a.size * a.dtype.itemsize for a in args)
    moved += sum(o.size * o.dtype.itemsize for o in outs)
    return pl.pallas_call(
        body,
        out_shape=outs,
        in_specs=specs,
        out_specs=[pl.BlockSpec(memory_space=pltpu.VMEM) for _ in outs],
        scratch_shapes=list(scratch),
        cost_estimate=pl.CostEstimate(flops=flops, bytes_accessed=moved, transcendentals=0),
        compiler_params=pltpu.CompilerParams(vmem_limit_bytes=VMEM_LIMIT),
    )(*args)


def shape(dims, dtype=BF16):
    return jax.ShapeDtypeStruct(dims, dtype)


def nn(a, b):
    return lax.dot_general(a, b, (((1,), (0,)), ((), ())), preferred_element_type=F32)


def nt(a, b):
    return lax.dot_general(a, b, (((1,), (1,)), ((), ())), preferred_element_type=F32)


def iota(dims, axis):
    return lax.broadcasted_iota(jnp.int32, dims, axis)


def pair_low(a, b, half):
    lane = iota(a.shape, 1)
    return jnp.where(lane < half, a, pltpu.roll(b, half, 1))


def pair_high(a, b, half):
    lane = iota(a.shape, 1)
    return jnp.where(lane < half, pltpu.roll(a, half, 1), b)


def routing(routes_ref, gates_ref, experts):
    top, rows = routes_ref.shape
    expert = iota((experts, rows), 0)
    named = jnp.zeros((experts, rows), F32)
    gate = jnp.zeros((experts, rows), F32)
    for k in range(top):
        hit = expert == routes_ref[k : k + 1, :]
        named = named + jnp.where(hit, 1.0, 0.0)
        gate = gate + jnp.where(hit, gates_ref[k : k + 1, :], 0.0)
    before = jnp.where(iota((rows, rows), 0) < iota((rows, rows), 1), 1.0, 0.0).astype(BF16)
    earlier = nn(named.astype(BF16), before)
    return jnp.where(named > 0.0, earlier, -1.0).astype(jnp.int32), gate


def dispatch_body(routes_ref, gates_ref, tok_ref, out_ref, slot_ref, gate_ref):
    experts, half, lanes = out_ref.shape
    rows = tok_ref.shape[1]
    cap = lanes // 2
    slot, gate = routing(routes_ref, gates_ref, experts)
    slot_ref[...] = slot
    gate_ref[...] = gate
    tok = jnp.concatenate([tok_ref[:half, :], tok_ref[half:, :]], axis=1)
    place = iota((lanes, rows), 0)
    place = jnp.where(place < cap, place, place - cap)
    low = iota((lanes, rows), 0) < cap
    for e in range(experts):
        sel = jnp.where(slot[e : e + 1, :] == place, 1.0, 0.0)
        sel = jnp.concatenate([jnp.where(low, sel, 0.0), jnp.where(low, 0.0, sel)], axis=1)
        out_ref[e] = nt(tok, sel.astype(BF16)).astype(BF16)


def spread_body(in_ref, out_ref):
    lanes_x, groups, half, lanes = in_ref.shape
    cap = lanes // 2
    for x in range(lanes_x):
        for q in range(groups // 2):
            a = in_ref[x, 2 * q].astype(F32)
            b = in_ref[x, 2 * q + 1].astype(F32)
            cols = slice(q * lanes, (q + 1) * lanes)
            out_ref[2 * half * x : 2 * half * x + half, cols] = pair_low(a, b, cap).astype(BF16)
            out_ref[2 * half * x + half : 2 * half * (x + 1), cols] = pair_high(a, b, cap).astype(BF16)


def glu(gate, up):
    return (gate / (1.0 + jnp.exp(-gate)) * up).astype(BF16)


def hidden_body(rows_ref, *refs):
    *weights, out_ref, flat_ref = refs
    ny, block, _ = rows_ref.shape
    nx = len(weights) // 2
    width = block // nx
    for y in range(ny):
        for x in range(nx):
            at = (x * ny + y) * width
            flat_ref[at : at + width, :] = rows_ref[y, x * width : (x + 1) * width, :]
    units = weights[0].shape[0]
    rows = flat_ref[...]
    for x in range(nx):
        gate = nn(weights[2 * x][...], rows)
        up = nn(weights[2 * x + 1][...], rows)
        out_ref[x * units : (x + 1) * units, :] = glu(gate, up)


def shared_body(tok_ref, gate_ref, up_ref, out_ref):
    tok = tok_ref[...]
    out_ref[...] = glu(nn(gate_ref[...], tok), nn(up_ref[...], tok))


def down_body(x_ref, hidden_ref, *refs):
    *weights, out_ref, flat_ref = refs
    nx = len(weights)
    ny = hidden_ref.shape[0]
    units = hidden_ref.shape[1] // nx
    _, groups, half, lanes = out_ref.shape
    cap = lanes // 2
    own = [lax.rem(x_ref[0] + shift, nx) for shift in SHIFTS]
    for n in range(nx):
        for y in range(ny):
            at = pl.multiple_of((own[n] * ny + y) * units, units)
            flat_ref[pl.ds(at, units), :] = hidden_ref[y, n * units : (n + 1) * units, :]
    rows = flat_ref[...]
    for n in range(nx):
        out = nn(weights[n][...], rows)
        for q in range(groups // 2):
            cols = slice(q * lanes, (q + 1) * lanes)
            a, b = out[:half, cols], out[half:, cols]
            out_ref[own[n], 2 * q] = pair_low(a, b, cap).astype(BF16)
            out_ref[own[n], 2 * q + 1] = pair_high(a, b, cap).astype(BF16)


def combine_body(slot_ref, gate_ref, back_ref, tok_ref, hidden_ref, down_ref, out_ref, scored_ref):
    experts, half, lanes = back_ref.shape
    rows = tok_ref.shape[1]
    cap = lanes // 2
    place = iota((lanes, rows), 0)
    place = jnp.where(place < cap, place, place - cap)
    low = iota((lanes, rows), 0) < cap
    routed = jnp.zeros((half, 2 * rows), F32)
    for e in range(experts):
        mix = jnp.where(slot_ref[e : e + 1, :] == place, gate_ref[e : e + 1, :], 0.0)
        mix = jnp.concatenate([jnp.where(low, mix, 0.0), jnp.where(low, 0.0, mix)], axis=1)
        head = mix.astype(BF16)
        tail = (mix - head.astype(F32)).astype(BF16)
        routed = routed + nn(back_ref[e], head) + nn(back_ref[e], tail)
    shared = nn(down_ref[...], hidden_ref[...])
    routed = jnp.concatenate([routed[:, :rows], routed[:, rows:]], axis=0)
    out = (tok_ref[...].astype(F32) + shared + routed).astype(BF16)
    out_ref[...] = out
    take = iota((scored_ref.shape[0], rows), 1) == rows - SCORE_E + iota((scored_ref.shape[0], rows), 0)
    scored_ref[...] = nt(jnp.where(take, 1.0, 0.0).astype(BF16), out).astype(BF16)


def pack_body(rows_ref, out_ref):
    count, width = rows_ref.shape
    half = width // 2
    eye = jnp.where(iota((count, count), 0) == iota((count, count), 1), 1.0, 0.0).astype(BF16)
    flip = lax.dot_general(
        rows_ref[...], eye, (((0,), (0,)), ((), ())), preferred_element_type=F32
    )
    out_ref[...] = jnp.concatenate([flip[:half], flip[half:]], axis=1).astype(BF16)


def score_body(offset_ref, rows_ref, vocab_ref, targets_ref, out_ref, flat_ref):
    blocks, half, lanes = rows_ref.shape
    count = lanes // 2
    for b in range(blocks):
        both = rows_ref[b].astype(F32)
        flat_ref[2 * half * b : 2 * half * b + half, :] = rows_ref[b]
        flat_ref[2 * half * b + half : 2 * half * (b + 1), :] = pltpu.roll(both, count, 1).astype(BF16)
    logits = nn(vocab_ref[...], flat_ref[...])
    entry = iota(logits.shape, 0) + offset_ref[0]
    sums = jnp.sum(jnp.exp(logits), axis=0, keepdims=True)
    hits = jnp.sum(jnp.where(entry == targets_ref[0:1, :], logits, 0.0), axis=0, keepdims=True)
    lane = iota(sums.shape, 1)
    out_ref[...] = jnp.broadcast_to(jnp.where(lane < count, sums, pltpu.roll(hits, count, 1)), out_ref.shape)


SHIFTS = (0, 1, 3, 2)


def spread_all(value, axes, count):
    return lax.all_to_all(
        jnp.broadcast_to(value[None], (count, *value.shape)), axes, 0, 0, tiled=True
    )


def nearby(value, axis):
    count = lax.axis_size(axis)
    return [
        value
        if shift == 0
        else lax.ppermute(value, axis, [((i + shift) % count, i) for i in range(count)])
        for shift in SHIFTS
    ]


def shards(tokens, routes, gates, w_gate, w_up, w_down, shared_gate, shared_up, shared_down, vocab, targets):
    nx, ny = lax.axis_size("x"), lax.axis_size("y")
    nz, nc = lax.axis_size("z"), lax.axis_size("core")
    groups, lanes = nz * nc, nx * ny
    rows, width = tokens.shape
    half, cap = width // 2, rows // 2
    near = groups // nx
    units = w_gate.shape[1]
    tok = tokens.T
    x_at = lax.axis_index("x").astype(jnp.int32).reshape(1)

    gates_near = nearby(w_gate[0], "x")
    ups_near = nearby(w_up[0], "x")
    downs_near = nearby(w_down[0].T, "x")

    outgoing, slot, gate = call(
        dispatch_body,
        [
            shape((groups, half, 2 * cap)),
            shape((groups, rows), jnp.int32),
            shape((groups, rows), F32),
        ],
        [routes.T, gates.T, tok],
    )
    arrived = lax.all_to_all(outgoing, LINE, 0, 0, tiled=True)
    plane_tok = spread_all(tok, PLANE, lanes).reshape(lanes * width, rows)
    quarter = lax.all_to_all(arrived.reshape(nx, near, half, 2 * cap), "x", 0, 0, tiled=True)
    (spread,) = call(spread_body, [shape((nx * width, near * cap))], [quarter])
    gathered = spread_all(spread, "y", ny)
    (hidden,) = call(
        hidden_body,
        [shape((nx * units, near * cap))],
        [gathered, *[w for pair in zip(gates_near, ups_near) for w in pair]],
        scratch=[pltpu.VMEM((lanes * width, near * cap), BF16)],
    )
    (hidden_shared,) = call(shared_body, [shape((units, rows))], [plane_tok, shared_gate, shared_up])
    all_hidden = spread_all(hidden, "y", ny)
    all_shared = spread_all(hidden_shared, PLANE, lanes).reshape(lanes * units, rows)
    (returned,) = call(
        down_body,
        [shape((nx, near, half, 2 * cap))],
        [x_at, all_hidden, *downs_near],
        scalars=1,
        scratch=[pltpu.VMEM((lanes * units, near * cap), BF16)],
    )
    back = lax.all_to_all(returned, "x", 0, 0, tiled=True).reshape(groups, half, 2 * cap)
    back = lax.all_to_all(back, LINE, 0, 0, tiled=True)
    layer_out, scored = call(
        combine_body,
        [shape((width, rows)), shape((8, width))],
        [slot, gate, back, tok, all_shared, shared_down.T],
    )
    line_rows = spread_all(scored[:SCORE_E], LINE, groups).reshape(groups * SCORE_E, width)
    (packed,) = call(pack_body, [shape((half, 2 * groups * SCORE_E))], [line_rows])
    every = spread_all(packed, PLANE, lanes)
    offset = (
        (lax.axis_index("z") * nc + lax.axis_index("core")) * lanes
        + lax.axis_index("x") * ny
        + lax.axis_index("y")
    ) * vocab.shape[0]
    count = groups * SCORE_E
    (sums,) = call(
        score_body,
        [shape((8, 2 * count), F32)],
        [
            offset.astype(jnp.int32).reshape(1),
            every,
            vocab,
            jnp.concatenate([targets, targets]).reshape(1, 2 * count),
        ],
        scalars=1,
        scratch=[pltpu.VMEM((lanes * width, 2 * count), BF16)],
    )
    sums = jnp.sum(spread_all(sums[:1], PLANE, lanes), axis=0)
    sums = jnp.sum(spread_all(sums, LINE, groups), axis=0)[0]
    return layer_out.T, sums[count:] - jnp.log(sums[:count])


def solution(mesh):
    mesh = Mesh(mesh.devices.reshape(8, 2, 4, 8), ("z", "core", "x", "y"))
    placed = (
        P(LINE, PLANE),
        P(LINE, None),
        P(LINE, None),
        P(LINE, PLANE, None),
        P(LINE, PLANE, None),
        P(LINE, None, PLANE),
        P(PLANE, None),
        P(PLANE, None),
        P(None, PLANE),
        P((*LINE, *PLANE), None),
        P(),
    )
    return jax.shard_map(
        shards, mesh=mesh, in_specs=placed, out_specs=(P(LINE, PLANE), P()), check_vma=False
    )
```

```python
import jax
import jax.numpy as jnp
from jax import lax
from jax.experimental import pallas as pl
from jax.experimental.pallas import tpu as pltpu
from jax.sharding import Mesh
from jax.sharding import PartitionSpec as P

SCORE_E = 4
F32 = jnp.float32
BF16 = jnp.bfloat16
LINE = ("z", "core")
PLANE = ("x", "y")


def call(body, outs, args, scalars=0, far=(), scratch=(), limit=16):
    specs = [
        pl.BlockSpec(memory_space=pltpu.SMEM if n < scalars else pltpu.HBM if n in far else pltpu.VMEM)
        for n in range(len(args))
    ]
    moved = sum(a.size * a.dtype.itemsize for a in args)
    moved += sum(o.size * o.dtype.itemsize for o in outs)
    return pl.pallas_call(
        body,
        out_shape=outs,
        in_specs=specs,
        out_specs=[pl.BlockSpec(memory_space=pltpu.VMEM) for _ in outs],
        scratch_shapes=list(scratch),
        cost_estimate=pl.CostEstimate(flops=0, bytes_accessed=moved, transcendentals=0),
        compiler_params=pltpu.CompilerParams(vmem_limit_bytes=limit << 20),
    )(*args)


def fetch(pairs, sems):
    copies = [pltpu.make_async_copy(src, dst, sems.at[n]) for n, (src, dst) in enumerate(pairs)]
    for copy in copies:
        copy.start()
    return copies


def shape(dims, dtype=BF16):
    return jax.ShapeDtypeStruct(dims, dtype)


def nn(a, b):
    return lax.dot_general(a, b, (((1,), (0,)), ((), ())), preferred_element_type=F32)


def nt(a, b):
    return lax.dot_general(a, b, (((1,), (1,)), ((), ())), preferred_element_type=F32)


def iota(dims, axis):
    return lax.broadcasted_iota(jnp.int32, dims, axis)


def pair_low(a, b, half):
    lane = iota(a.shape, 1)
    return jnp.where(lane < half, a, pltpu.roll(b, half, 1))


def pair_high(a, b, half):
    lane = iota(a.shape, 1)
    return jnp.where(lane < half, pltpu.roll(a, half, 1), b)


def routing(routes_ref, gates_ref, experts):
    top, rows = routes_ref.shape
    expert = iota((experts, rows), 0)
    named = jnp.zeros((experts, rows), F32)
    gate = jnp.zeros((experts, rows), F32)
    for k in range(top):
        hit = expert == routes_ref[k : k + 1, :]
        named = named + jnp.where(hit, 1.0, 0.0)
        gate = gate + jnp.where(hit, gates_ref[k : k + 1, :], 0.0)
    before = jnp.where(iota((rows, rows), 0) < iota((rows, rows), 1), 1.0, 0.0).astype(BF16)
    earlier = nn(named.astype(BF16), before)
    return jnp.where(named > 0.0, earlier, -1.0).astype(jnp.int32), gate


def dispatch_body(routes_ref, gates_ref, tok_ref, out_ref, slot_ref, gate_ref):
    experts, half, lanes = out_ref.shape
    rows = tok_ref.shape[1]
    cap = lanes // 2
    slot, gate = routing(routes_ref, gates_ref, experts)
    slot_ref[...] = slot
    gate_ref[...] = gate
    tok = jnp.concatenate([tok_ref[:half, :], tok_ref[half:, :]], axis=1)
    place = iota((lanes, rows), 0)
    place = jnp.where(place < cap, place, place - cap)
    low = iota((lanes, rows), 0) < cap
    for e in range(experts):
        sel = jnp.where(slot[e : e + 1, :] == place, 1.0, 0.0)
        sel = jnp.concatenate([jnp.where(low, sel, 0.0), jnp.where(low, 0.0, sel)], axis=1)
        out_ref[e] = nt(tok, sel.astype(BF16)).astype(BF16)


def spread_body(in_ref, out_ref):
    lanes_x, _, lanes = in_ref.shape
    width = out_ref.shape[0] // lanes_x
    half, cap = width // 2, lanes // 2
    groups = (in_ref.shape[1] - width) // half
    for x in range(lanes_x):
        top, mid, end = x * width, x * width + half, (x + 1) * width
        for q in range(groups // 2):
            a = in_ref[x, 2 * q * half : (2 * q + 1) * half, :].astype(F32)
            b = in_ref[x, (2 * q + 1) * half : (2 * q + 2) * half, :].astype(F32)
            cols = slice(q * lanes, (q + 1) * lanes)
            out_ref[top:mid, cols] = pair_low(a, b, cap).astype(BF16)
            out_ref[mid:end, cols] = pair_high(a, b, cap).astype(BF16)
        out_ref[top:end, groups * cap :] = in_ref[x, groups * half :, :]


def glu(gate, up):
    return (gate / (1.0 + jnp.exp(-gate)) * up).astype(BF16)


def hidden_body(y_ref, *refs):
    blocks = refs[: len(RING)]
    out_ref, flat_ref, gates_ref, ups_ref, sems = refs[-5:]
    weights = refs[len(RING) : -5]
    nx = len(weights) // 2 - 1
    units = weights[0].shape[0]
    width = blocks[0].shape[0] // nx
    ny = flat_ref.shape[0] // (nx * width)
    pairs = []
    for n in range(nx + 1):
        for at, into in enumerate((gates_ref, ups_ref)):
            pairs.append((weights[2 * n + at], into.at[n * units : (n + 1) * units, :]))
    for block, (shift, first) in zip(blocks, RING):
        y = lax.rem(y_ref[0] + shift, ny)
        for n in range(block.shape[0] // width):
            at = pl.multiple_of(((first + n) * ny + y) * width, width)
            pairs.append((block.at[n * width : (n + 1) * width, :], flat_ref.at[pl.ds(at, width), :]))
    for copy in fetch(pairs, sems):
        copy.wait()
    cols = out_ref.shape[1]
    top = nx * units
    rows = flat_ref[:, :cols]
    out_ref[:top, :] = glu(nn(gates_ref[:top, :], rows), nn(ups_ref[:top, :], rows))
    toks = flat_ref[:, cols:]
    own = glu(nn(gates_ref[top:, :], toks), nn(ups_ref[top:, :], toks))
    fold = units // 2
    out_ref[top : top + fold, :] = jnp.concatenate([own[:fold], own[fold:]], axis=1)


def down_body(x_ref, hidden_ref, *refs):
    *weights, out_ref, flat_ref, down_ref, sems = refs
    nx = len(weights)
    copies = fetch([(weights[n], down_ref.at[n]) for n in range(nx)], sems)
    ny = hidden_ref.shape[0]
    units = flat_ref.shape[0] // (nx * ny)
    width, lanes = weights[0].shape[0], out_ref.shape[2]
    half, cap, fold = width // 2, lanes // 2, units // 2
    groups = (out_ref.shape[1] - ny * units) // half
    own = [lax.rem(x_ref[0] + shift, nx) for shift in SHIFTS]
    for n in range(nx):
        for y in range(ny):
            at = pl.multiple_of((own[n] * ny + y) * units, units)
            flat_ref[pl.ds(at, units), :] = hidden_ref[y, n * units : (n + 1) * units, :]
    rows = flat_ref[...]
    for n in range(nx):
        copies[n].wait()
        out = nn(down_ref[n], rows)
        for q in range(groups // 2):
            cols = slice(q * lanes, (q + 1) * lanes)
            a, b = out[:half, cols], out[half:, cols]
            out_ref[own[n], 2 * q * half : (2 * q + 1) * half, :] = pair_low(a, b, cap).astype(BF16)
            out_ref[own[n], (2 * q + 1) * half : (2 * q + 2) * half, :] = pair_high(a, b, cap).astype(BF16)
        for y in range(ny):
            at = groups * half + y * units
            both = hidden_ref[y, nx * units : nx * units + fold, :]
            out_ref[n, at : at + fold, :] = both[:, :lanes]
            out_ref[n, at + fold : at + units, :] = both[:, lanes:]


def combine_body(slot_ref, gate_ref, back_ref, tok_ref, hidden_ref, down_ref, out_ref, scored_ref):
    experts, half, lanes = back_ref.shape
    rows = tok_ref.shape[1]
    cap = lanes // 2
    place = iota((lanes, rows), 0)
    place = jnp.where(place < cap, place, place - cap)
    low = iota((lanes, rows), 0) < cap
    routed = jnp.zeros((half, 2 * rows), F32)
    for e in range(experts):
        mix = jnp.where(slot_ref[e : e + 1, :] == place, gate_ref[e : e + 1, :], 0.0)
        mix = jnp.concatenate([jnp.where(low, mix, 0.0), jnp.where(low, 0.0, mix)], axis=1)
        head = mix.astype(BF16)
        tail = (mix - head.astype(F32)).astype(BF16)
        routed = routed + nn(back_ref[e], head) + nn(back_ref[e], tail)
    depth = down_ref.shape[1] // hidden_ref.shape[0]
    skip = hidden_ref.shape[1] - depth
    shared = jnp.zeros((2 * half, rows), F32)
    for x in range(hidden_ref.shape[0]):
        shared = shared + nn(down_ref[:, x * depth : (x + 1) * depth], hidden_ref[x, skip:, :])
    routed = jnp.concatenate([routed[:, :rows], routed[:, rows:]], axis=0)
    out = (tok_ref[...].astype(F32) + shared + routed).astype(BF16)
    out_ref[...] = out
    take = iota((scored_ref.shape[0], rows), 1) == rows - SCORE_E + iota((scored_ref.shape[0], rows), 0)
    scored_ref[...] = nt(jnp.where(take, 1.0, 0.0).astype(BF16), out).astype(BF16)


def pack_body(rows_ref, out_ref):
    count, width = rows_ref.shape
    half = width // 2
    eye = jnp.where(iota((count, count), 0) == iota((count, count), 1), 1.0, 0.0).astype(BF16)
    flip = lax.dot_general(
        rows_ref[...], eye, (((0,), (0,)), ((), ())), preferred_element_type=F32
    )
    out_ref[...] = jnp.concatenate([flip[:half], flip[half:]], axis=1).astype(BF16)


def score_body(offset_ref, rows_ref, vocab_ref, targets_ref, out_ref, flat_ref):
    blocks, half, lanes = rows_ref.shape
    count = lanes // 2
    for b in range(blocks):
        both = rows_ref[b].astype(F32)
        flat_ref[2 * half * b : 2 * half * b + half, :] = rows_ref[b]
        flat_ref[2 * half * b + half : 2 * half * (b + 1), :] = pltpu.roll(both, count, 1).astype(BF16)
    logits = nn(vocab_ref[...], flat_ref[...])
    entry = iota(logits.shape, 0) + offset_ref[0]
    sums = jnp.sum(jnp.exp(logits), axis=0, keepdims=True)
    hits = jnp.sum(jnp.where(entry == targets_ref[0:1, :], logits, 0.0), axis=0, keepdims=True)
    lane = iota(sums.shape, 1)
    out_ref[...] = jnp.broadcast_to(jnp.where(lane < count, sums, pltpu.roll(hits, count, 1)), out_ref.shape)


SHIFTS = (0, 1, 3, 2)
RING = ((0, 0), (7, 0), (1, 0), (6, 0), (2, 0), (5, 0), (3, 0), (4, 0), (4, 2))


def spread_all(value, axes, count):
    return lax.all_to_all(
        jnp.broadcast_to(value[None], (count, *value.shape)), axes, 0, 0, tiled=True
    )


def from_shift(value, axis, shift):
    count = lax.axis_size(axis)
    return lax.ppermute(value, axis, [((i + shift) % count, i) for i in range(count)])


def around(value, axis, *due):
    count = lax.axis_size(axis)
    left = right = value
    got, kept = [value], []
    for hop in range(3):
        if hop and hop <= len(due):
            left, right, *had = lax.optimization_barrier((left, right, *due[hop - 1]))
            kept += had
        left = from_shift(left, axis, count - 1)
        right = from_shift(right, axis, 1)
        got += [left, right]
    part = value.shape[0] // 2
    return [*got, from_shift(left[:part], axis, count - 1), from_shift(right[part:], axis, 1)], kept


def shards(tokens, routes, gates, w_gate, w_up, w_down, shared_gate, shared_up, shared_down, vocab, targets):
    nx, ny = lax.axis_size("x"), lax.axis_size("y")
    nz, nc = lax.axis_size("z"), lax.axis_size("core")
    groups, lanes = nz * nc, nx * ny
    rows, width = tokens.shape
    half, cap = width // 2, rows // 2
    near = groups // nx
    units = w_gate.shape[1]
    tok = tokens.T
    x_at = lax.axis_index("x").astype(jnp.int32).reshape(1)
    y_at = lax.axis_index("y").astype(jnp.int32).reshape(1)

    own_gate, own_up, own_down = w_gate[0], w_up[0], w_down[0].T
    near_gate = [from_shift(own_gate, "x", shift) for shift in SHIFTS[1:]]
    near_up = [from_shift(own_up, "x", shift) for shift in SHIFTS[1:]]
    near_down = [from_shift(own_down, "x", shift) for shift in SHIFTS[1:]]

    outgoing, slot, gate = call(
        dispatch_body,
        [
            shape((groups, half, 2 * cap)),
            shape((groups, rows), jnp.int32),
            shape((groups, rows), F32),
        ],
        [routes.T, gates.T, tok],
    )
    arrived = lax.all_to_all(outgoing, LINE, 0, 0, tiled=True)
    arrived, g1, g3, u1, u3 = lax.optimization_barrier((arrived, *near_gate[:2], *near_up[:2]))
    leaving = jnp.concatenate(
        [arrived.reshape(nx, near * half, 2 * cap), jnp.broadcast_to(tok[None], (nx, width, rows))], axis=1
    )
    quarter = lax.all_to_all(leaving, "x", 0, 0, tiled=True)
    (spread,) = call(spread_body, [shape((nx * width, near * cap + rows))], [quarter])
    blocks, (g2, u2, d1, d3) = around(spread, "y", (near_gate[2], near_up[2]), near_down[:2])
    (hidden,) = call(
        hidden_body,
        [shape((nx * units + units // 2 + 8, near * cap))],
        [y_at, *blocks, own_gate, own_up, g1, u1, g3, u3, g2, u2, shared_gate, shared_up],
        scalars=1,
        far=range(1, 2 * nx + len(RING) + 3),
        scratch=[
            pltpu.VMEM((lanes * width, near * cap + rows), BF16),
            pltpu.VMEM(((nx + 1) * units, lanes * width), BF16),
            pltpu.VMEM(((nx + 1) * units, lanes * width), BF16),
            pltpu.SemaphoreType.DMA((2 * nx + 2 + lanes,)),
        ],
        limit=60,
    )
    all_hidden = spread_all(hidden, "y", ny)
    (returned,) = call(
        down_body,
        [shape((nx, near * half + ny * units, 2 * cap))],
        [x_at, all_hidden, own_down, d1, d3, near_down[2]],
        scalars=1,
        far=range(2, 2 + nx),
        scratch=[
            pltpu.VMEM((lanes * units, near * cap), BF16),
            pltpu.VMEM((nx, width, lanes * units), BF16),
            pltpu.SemaphoreType.DMA((nx,)),
        ],
        limit=60,
    )
    mixed = lax.all_to_all(returned, "x", 0, 0, tiled=True)
    back = mixed[:, : near * half].reshape(groups, half, 2 * cap)
    back = lax.all_to_all(back, LINE, 0, 0, tiled=True)
    layer_out, scored = call(
        combine_body,
        [shape((width, rows)), shape((8, width))],
        [slot, gate, back, tok, mixed, shared_down.T],
    )
    line_rows = spread_all(scored[:SCORE_E], LINE, groups).reshape(groups * SCORE_E, width)
    (packed,) = call(pack_body, [shape((half, 2 * groups * SCORE_E))], [line_rows])
    every = spread_all(packed, PLANE, lanes)
    offset = (
        (lax.axis_index("z") * nc + lax.axis_index("core")) * lanes
        + lax.axis_index("x") * ny
        + lax.axis_index("y")
    ) * vocab.shape[0]
    count = groups * SCORE_E
    (sums,) = call(
        score_body,
        [shape((8, 2 * count), F32)],
        [
            offset.astype(jnp.int32).reshape(1),
            every,
            vocab,
            jnp.concatenate([targets, targets]).reshape(1, 2 * count),
        ],
        scalars=1,
        scratch=[pltpu.VMEM((lanes * width, 2 * count), BF16)],
    )
    sums = jnp.sum(spread_all(sums[:1], PLANE, lanes), axis=0)
    sums = jnp.sum(spread_all(sums, LINE, groups), axis=0)[0]
    return layer_out.T, sums[count:] - jnp.log(sums[:count])


def solution(mesh):
    mesh = Mesh(mesh.devices.reshape(8, 2, 4, 8), ("z", "core", "x", "y"))
    placed = (
        P(LINE, PLANE),
        P(LINE, None),
        P(LINE, None),
        P(LINE, PLANE, None),
        P(LINE, PLANE, None),
        P(LINE, None, PLANE),
        P(PLANE, None),
        P(PLANE, None),
        P(None, PLANE),
        P((*LINE, *PLANE), None),
        P(),
    )
    return jax.shard_map(
        shards, mesh=mesh, in_specs=placed, out_specs=(P(LINE, PLANE), P()), check_vma=False
    )
```

```python
import jax
import jax.numpy as jnp
from jax import lax
from jax.experimental import pallas as pl
from jax.experimental.pallas import tpu as pltpu
from jax.sharding import Mesh
from jax.sharding import PartitionSpec as P

SCORE_E = 4
F32 = jnp.float32
BF16 = jnp.bfloat16
LINE = ("z", "core")
PLANE = ("x", "y")


def call(body, outs, args, scalars=0, far=(), scratch=(), limit=16):
    specs = [
        pl.BlockSpec(memory_space=pltpu.SMEM if n < scalars else pltpu.HBM if n in far else pltpu.VMEM)
        for n in range(len(args))
    ]
    moved = sum(a.size * a.dtype.itemsize for a in args)
    moved += sum(o.size * o.dtype.itemsize for o in outs)
    return pl.pallas_call(
        body,
        out_shape=outs,
        in_specs=specs,
        out_specs=[pl.BlockSpec(memory_space=pltpu.VMEM) for _ in outs],
        scratch_shapes=list(scratch),
        cost_estimate=pl.CostEstimate(flops=0, bytes_accessed=moved, transcendentals=0),
        compiler_params=pltpu.CompilerParams(vmem_limit_bytes=limit << 20),
    )(*args)


def fetch(pairs, sems):
    copies = [pltpu.make_async_copy(src, dst, sems.at[n]) for n, (src, dst) in enumerate(pairs)]
    for copy in copies:
        copy.start()
    return copies


def shape(dims, dtype=BF16):
    return jax.ShapeDtypeStruct(dims, dtype)


def nn(a, b):
    return lax.dot_general(a, b, (((1,), (0,)), ((), ())), preferred_element_type=F32)


def nt(a, b):
    return lax.dot_general(a, b, (((1,), (1,)), ((), ())), preferred_element_type=F32)


def iota(dims, axis):
    return lax.broadcasted_iota(jnp.int32, dims, axis)


def pair_low(a, b, half):
    lane = iota(a.shape, 1)
    return jnp.where(lane < half, a, pltpu.roll(b, half, 1))


def pair_high(a, b, half):
    lane = iota(a.shape, 1)
    return jnp.where(lane < half, pltpu.roll(a, half, 1), b)


def routing(routes_ref, gates_ref, experts):
    top, rows = routes_ref.shape
    expert = iota((experts, rows), 0)
    named = jnp.zeros((experts, rows), F32)
    gate = jnp.zeros((experts, rows), F32)
    for k in range(top):
        hit = expert == routes_ref[k : k + 1, :]
        named = named + jnp.where(hit, 1.0, 0.0)
        gate = gate + jnp.where(hit, gates_ref[k : k + 1, :], 0.0)
    before = jnp.where(iota((rows, rows), 0) < iota((rows, rows), 1), 1.0, 0.0).astype(BF16)
    earlier = nn(named.astype(BF16), before)
    return jnp.where(named > 0.0, earlier, -1.0).astype(jnp.int32), gate


def dispatch_body(routes_far, gates_far, tok_far, out_ref, slot_ref, gate_ref, routes_ref, gates_ref, tok_ref, sems):
    pairs = [(routes_far, routes_ref), (gates_far, gates_ref), (tok_far, tok_ref)]
    for copy in fetch(pairs, sems):
        copy.wait()
    experts, half, lanes = out_ref.shape
    rows = tok_ref.shape[1]
    cap = lanes // 2
    slot, gate = routing(routes_ref, gates_ref, experts)
    slot_ref[...] = slot
    gate_ref[...] = gate
    tok = jnp.concatenate([tok_ref[:half, :], tok_ref[half:, :]], axis=1)
    place = iota((lanes, rows), 0)
    place = jnp.where(place < cap, place, place - cap)
    low = iota((lanes, rows), 0) < cap
    for e in range(experts):
        sel = jnp.where(slot[e : e + 1, :] == place, 1.0, 0.0)
        sel = jnp.concatenate([jnp.where(low, sel, 0.0), jnp.where(low, 0.0, sel)], axis=1)
        out_ref[e] = nt(tok, sel.astype(BF16)).astype(BF16)


def spread_body(in_ref, out_ref):
    lanes_x, _, lanes = in_ref.shape
    width = out_ref.shape[0] // lanes_x
    half, cap = width // 2, lanes // 2
    groups = (in_ref.shape[1] - width) // half
    for x in range(lanes_x):
        top, mid, end = x * width, x * width + half, (x + 1) * width
        for q in range(groups // 2):
            a = in_ref[x, 2 * q * half : (2 * q + 1) * half, :].astype(F32)
            b = in_ref[x, (2 * q + 1) * half : (2 * q + 2) * half, :].astype(F32)
            cols = slice(q * lanes, (q + 1) * lanes)
            out_ref[top:mid, cols] = pair_low(a, b, cap).astype(BF16)
            out_ref[mid:end, cols] = pair_high(a, b, cap).astype(BF16)
        out_ref[top:end, groups * cap :] = in_ref[x, groups * half :, :]


def glu(gate, up):
    return (gate / (1.0 + jnp.exp(-gate)) * up).astype(BF16)


def hidden_body(y_ref, *refs):
    blocks = refs[: len(RING)]
    out_ref, flat_ref, gates_ref, ups_ref, sems = refs[-5:]
    weights = refs[len(RING) : -5]
    nx = len(weights) // 2 - 1
    units = weights[0].shape[0]
    width = blocks[0].shape[0] // nx
    ny = flat_ref.shape[0] // (nx * width)
    pairs = []
    for n in range(nx + 1):
        for at, into in enumerate((gates_ref, ups_ref)):
            pairs.append((weights[2 * n + at], into.at[n * units : (n + 1) * units, :]))
    for block, (shift, first) in zip(blocks, RING):
        y = lax.rem(y_ref[0] + shift, ny)
        for n in range(block.shape[0] // width):
            at = pl.multiple_of(((first + n) * ny + y) * width, width)
            pairs.append((block.at[n * width : (n + 1) * width, :], flat_ref.at[pl.ds(at, width), :]))
    for copy in fetch(pairs, sems):
        copy.wait()
    cols = out_ref.shape[1]
    top = nx * units
    rows = flat_ref[:, :cols]
    out_ref[:top, :] = glu(nn(gates_ref[:top, :], rows), nn(ups_ref[:top, :], rows))
    toks = flat_ref[:, cols:]
    own = glu(nn(gates_ref[top:, :], toks), nn(ups_ref[top:, :], toks))
    fold = units // 2
    out_ref[top : top + fold, :] = jnp.concatenate([own[:fold], own[fold:]], axis=1)


def down_body(x_ref, hidden_ref, *refs):
    *weights, out_ref, flat_ref, down_ref, sems = refs
    nx = out_ref.shape[0]
    width = weights[0].shape[0]
    copies, at = [], 0
    for n, weight in enumerate(weights):
        copies.append((weight, down_ref.at[at : at + weight.shape[0], :]))
        at += weight.shape[0]
    copies = fetch(copies, sems)
    ny = hidden_ref.shape[0]
    units = flat_ref.shape[0] // (nx * ny)
    lanes = out_ref.shape[2]
    half, cap, fold = width // 2, lanes // 2, units // 2
    groups = (out_ref.shape[1] - ny * units) // half
    own = [lax.rem(x_ref[0] + shift, nx) for shift in SHIFTS]
    for n in range(nx):
        for y in range(ny):
            at = pl.multiple_of((own[n] * ny + y) * units, units)
            flat_ref[pl.ds(at, units), :] = hidden_ref[y, n * units : (n + 1) * units, :]
    for copy in copies:
        copy.wait()
    outs = nn(down_ref[...], flat_ref[...])
    for n in range(nx):
        out = outs[n * width : (n + 1) * width]
        for q in range(groups // 2):
            cols = slice(q * lanes, (q + 1) * lanes)
            a, b = out[:half, cols], out[half:, cols]
            out_ref[own[n], 2 * q * half : (2 * q + 1) * half, :] = pair_low(a, b, cap).astype(BF16)
            out_ref[own[n], (2 * q + 1) * half : (2 * q + 2) * half, :] = pair_high(a, b, cap).astype(BF16)
        for y in range(ny):
            at = groups * half + y * units
            both = hidden_ref[y, nx * units : nx * units + fold, :]
            out_ref[n, at : at + fold, :] = both[:, :lanes]
            out_ref[n, at + fold : at + units, :] = both[:, lanes:]


def combine_body(slot_ref, gate_ref, back_ref, tok_ref, hidden_ref, down_ref, out_ref, scored_ref):
    experts, half, lanes = back_ref.shape
    rows = tok_ref.shape[1]
    cap = lanes // 2
    place = iota((lanes, rows), 0)
    place = jnp.where(place < cap, place, place - cap)
    low = iota((lanes, rows), 0) < cap
    routed = jnp.zeros((half, 2 * rows), F32)
    for e in range(experts):
        mix = jnp.where(slot_ref[e : e + 1, :] == place, gate_ref[e : e + 1, :], 0.0)
        mix = jnp.concatenate([jnp.where(low, mix, 0.0), jnp.where(low, 0.0, mix)], axis=1)
        head = mix.astype(BF16)
        tail = (mix - head.astype(F32)).astype(BF16)
        routed = routed + nn(back_ref[e], head) + nn(back_ref[e], tail)
    depth = down_ref.shape[1] // hidden_ref.shape[0]
    skip = hidden_ref.shape[1] - depth
    shared = jnp.zeros((2 * half, rows), F32)
    for x in range(hidden_ref.shape[0]):
        shared = shared + nn(down_ref[:, x * depth : (x + 1) * depth], hidden_ref[x, skip:, :])
    routed = jnp.concatenate([routed[:, :rows], routed[:, rows:]], axis=0)
    out = (tok_ref[...].astype(F32) + shared + routed).astype(BF16)
    out_ref[...] = out
    take = iota((scored_ref.shape[0], rows), 1) == rows - SCORE_E + iota((scored_ref.shape[0], rows), 0)
    scored_ref[...] = nt(jnp.where(take, 1.0, 0.0).astype(BF16), out).astype(BF16)


def pack_body(core_ref, rows_ref, out_ref):
    count, width = rows_ref.shape[0] // 2, rows_ref.shape[1]
    part = out_ref.shape[0]
    eye = jnp.where(iota((count, count), 0) == iota((count, count), 1), 1.0, 0.0).astype(BF16)
    mine = rows_ref[pl.ds(pl.multiple_of(core_ref[0] * count, count), count), :]
    flip = lax.dot_general(mine, eye, (((0,), (0,)), ((), ())), preferred_element_type=F32)
    out_ref[...] = jnp.concatenate([flip[n : n + part] for n in range(0, width, part)], axis=1).astype(BF16)


def score_body(at_ref, rows_ref, vocab_ref, other_ref, targets_ref, out_ref, flat_ref):
    blocks, part, lanes = rows_ref.shape
    parts = flat_ref.shape[0] // (blocks * part)
    count = lanes // parts
    for b in range(blocks):
        block = rows_ref[b].astype(F32)
        for n in range(parts):
            at = (b * parts + n) * part
            turned = block if n == 0 else pltpu.roll(block, lanes - n * count, 1)
            flat_ref[at : at + part, :] = turned.astype(BF16)
    target = targets_ref[pl.ds(at_ref[0], 1), :]
    sums = jnp.zeros((1, lanes), F32)
    hits = jnp.zeros((1, lanes), F32)
    for n, block in enumerate((vocab_ref, other_ref)):
        logits = nn(block[...], flat_ref[...])
        entry = iota(logits.shape, 0) + at_ref[1 + n]
        sums = sums + jnp.sum(jnp.exp(logits), axis=0, keepdims=True)
        hits = hits + jnp.sum(jnp.where(entry == target, logits, 0.0), axis=0, keepdims=True)
    lane = iota(sums.shape, 1)
    out_ref[...] = jnp.broadcast_to(jnp.where(lane < count, sums, pltpu.roll(hits, count, 1)), out_ref.shape)


SHIFTS = (0, 1, 3, 2)
RING = ((0, 0), (7, 0), (1, 0), (6, 0), (2, 0), (5, 0), (3, 0), (4, 0), (4, 2))


def spread_all(value, axes, count):
    return lax.all_to_all(
        jnp.broadcast_to(value[None], (count, *value.shape)), axes, 0, 0, tiled=True
    )


def from_shift(value, axis, shift):
    count = lax.axis_size(axis)
    return lax.ppermute(value, axis, [((i + shift) % count, i) for i in range(count)])


def around(value, axis, between):
    count = lax.axis_size(axis)
    left = right = value
    got = [value]
    for hop in range(3):
        if hop:
            left, right = between(hop, left, right)
        left = from_shift(left, axis, count - 1)
        right = from_shift(right, axis, 1)
        got += [left, right]
    left, right = between(3, left, right)
    part = value.shape[0] // 2
    return [*got, from_shift(left[:part], axis, count - 1), from_shift(right[part:], axis, 1)]


def shards(tokens, routes, gates, w_gate, w_up, w_down, shared_gate, shared_up, shared_down, vocab, targets):
    nx, ny = lax.axis_size("x"), lax.axis_size("y")
    nz, nc = lax.axis_size("z"), lax.axis_size("core")
    groups, lanes = nz * nc, nx * ny
    rows, width = tokens.shape
    half, cap = width // 2, rows // 2
    near = groups // nx
    units = w_gate.shape[1]
    tok = tokens.T
    x_at = lax.axis_index("x").astype(jnp.int32).reshape(1)
    y_at = lax.axis_index("y").astype(jnp.int32).reshape(1)

    own_gate, own_up = w_gate[0], w_up[0]
    g1, g3, u1, u3 = [from_shift(own, "x", shift) for own in (own_gate, own_up) for shift in SHIFTS[1:3]]

    outgoing, slot, gate = call(
        dispatch_body,
        [
            shape((groups, half, 2 * cap)),
            shape((groups, rows), jnp.int32),
            shape((groups, rows), F32),
        ],
        [routes.T, gates.T, tok],
        far=range(3),
        scratch=[
            pltpu.VMEM(routes.T.shape, jnp.int32),
            pltpu.VMEM(gates.T.shape, F32),
            pltpu.VMEM(tok.shape, BF16),
            pltpu.SemaphoreType.DMA((3,)),
        ],
        limit=60,
    )
    arrived = lax.all_to_all(outgoing, LINE, 0, 0, tiled=True)
    arrived, g1, u3 = lax.optimization_barrier((arrived, g1, u3))
    leaving = jnp.concatenate(
        [arrived.reshape(nx, near * half, 2 * cap), jnp.broadcast_to(tok[None], (nx, width, rows))], axis=1
    )
    quarter = lax.all_to_all(leaving, "x", 0, 0, tiled=True)
    (spread,) = call(spread_body, [shape((nx * width, near * cap + rows))], [quarter])
    held = {}

    def between(hop, left, right):
        if hop == 1:
            left, right, held["g3"], held["u1"] = lax.optimization_barrier((left, right, g3, u1))
        if hop == 2:
            left, right, held["down"] = lax.optimization_barrier((left, right, w_down[0].T))
            held["d1"] = from_shift(held["down"], "x", 1)
            held["d3"] = from_shift(held["down"], "x", nx - 1)
        if hop == 3:
            left, right, held["g2"], held["u2"] = lax.optimization_barrier((left, right, held["g2"], held["u2"]))
        return left, right

    spread, g1, u3 = lax.optimization_barrier((spread, g1, u3))
    held["g2"] = from_shift(g1, "x", 1)
    held["u2"] = from_shift(u3, "x", nx - 1)
    blocks = around(spread, "y", between)
    g3, u1, g2, u2 = held["g3"], held["u1"], held["g2"], held["u2"]
    (hidden,) = call(
        hidden_body,
        [shape((nx * units + units // 2 + 8, near * cap))],
        [y_at, *blocks, own_gate, own_up, g1, u1, g3, u3, g2, u2, shared_gate, shared_up],
        scalars=1,
        far=range(1, 2 * nx + len(RING) + 3),
        scratch=[
            pltpu.VMEM((lanes * width, near * cap + rows), BF16),
            pltpu.VMEM(((nx + 1) * units, lanes * width), BF16),
            pltpu.VMEM(((nx + 1) * units, lanes * width), BF16),
            pltpu.SemaphoreType.DMA((2 * nx + 2 + lanes,)),
        ],
        limit=60,
    )
    hidden, d1, d3 = lax.optimization_barrier((hidden, held["d1"], held["d3"]))
    d2 = [from_shift(d1[:half], "x", 1), from_shift(d3[half:], "x", nx - 1)]
    all_hidden = spread_all(hidden, "y", ny)
    (returned,) = call(
        down_body,
        [shape((nx, near * half + ny * units, 2 * cap))],
        [x_at, all_hidden, held["down"], d1, d3, *d2],
        scalars=1,
        far=range(2, 3 + nx),
        scratch=[
            pltpu.VMEM((lanes * units, near * cap), BF16),
            pltpu.VMEM((nx * width, lanes * units), BF16),
            pltpu.SemaphoreType.DMA((nx + 1,)),
        ],
        limit=40,
    )
    mixed = lax.all_to_all(returned, "x", 0, 0, tiled=True)
    back = mixed[:, : near * half].reshape(groups, half, 2 * cap)
    back = lax.all_to_all(back, LINE, 0, 0, tiled=True)
    layer_out, scored = call(
        combine_body,
        [shape((width, rows)), shape((8, width))],
        [slot, gate, back, tok, mixed, shared_down.T],
    )
    line_rows = spread_all(scored[:SCORE_E], LINE, groups).reshape(groups * SCORE_E, width)
    count = groups * SCORE_E // nc
    core = lax.axis_index("core").astype(jnp.int32)
    (packed,) = call(
        pack_body,
        [shape((width * count // (2 * cap), 2 * cap))],
        [core.reshape(1), line_rows],
        scalars=1,
    )
    every = spread_all(packed, PLANE, lanes)
    other_vocab = lax.ppermute(vocab, "core", [(0, 1), (1, 0)])
    place = lax.axis_index("x") * ny + lax.axis_index("y")
    first = [
        (((lax.axis_index("z") * nc + c) * lanes + place) * vocab.shape[0]).astype(jnp.int32)
        for c in (core, 1 - core)
    ]
    (sums,) = call(
        score_body,
        [shape((8, 2 * cap), F32)],
        [
            jnp.stack([core, *first]),
            every,
            vocab,
            other_vocab,
            jnp.tile(targets.reshape(nc, count), (1, 2 * cap // count)),
        ],
        scalars=1,
        scratch=[pltpu.VMEM((lanes * width, 2 * cap), BF16)],
    )
    sums = jnp.sum(spread_all(sums[:1], PLANE, lanes), axis=0)
    sums = jnp.sum(spread_all(sums, LINE, groups).reshape(nz, nc, 2 * cap), axis=0)
    return layer_out.T, (sums[:, count : 2 * count] - jnp.log(sums[:, :count])).reshape(-1)


def solution(mesh):
    mesh = Mesh(mesh.devices.reshape(8, 2, 4, 8), ("z", "core", "x", "y"))
    placed = (
        P(LINE, PLANE),
        P(LINE, None),
        P(LINE, None),
        P(LINE, PLANE, None),
        P(LINE, PLANE, None),
        P(LINE, None, PLANE),
        P(PLANE, None),
        P(PLANE, None),
        P(None, PLANE),
        P((*LINE, *PLANE), None),
        P(),
    )
    return jax.shard_map(
        shards, mesh=mesh, in_specs=placed, out_specs=(P(LINE, PLANE), P()), check_vma=False
    )
```

```python
import jax
import jax.numpy as jnp
from jax import lax
from jax.experimental import pallas as pl
from jax.experimental.pallas import tpu as pltpu
from jax.sharding import Mesh
from jax.sharding import PartitionSpec as P

SCORE_E = 4
F32 = jnp.float32
BF16 = jnp.bfloat16
LINE = ("z", "core")
PLANE = ("x", "y")


def call(body, outs, args, scalars=0, far=(), scratch=(), limit=16):
    specs = [
        pl.BlockSpec(memory_space=pltpu.SMEM if n < scalars else pltpu.HBM if n in far else pltpu.VMEM)
        for n in range(len(args))
    ]
    moved = sum(a.size * a.dtype.itemsize for a in args)
    moved += sum(o.size * o.dtype.itemsize for o in outs)
    return pl.pallas_call(
        body,
        out_shape=outs,
        in_specs=specs,
        out_specs=[pl.BlockSpec(memory_space=pltpu.VMEM) for _ in outs],
        scratch_shapes=list(scratch),
        cost_estimate=pl.CostEstimate(flops=0, bytes_accessed=moved, transcendentals=0),
        compiler_params=pltpu.CompilerParams(vmem_limit_bytes=limit << 20),
    )(*args)


def fetch(pairs, sems):
    copies = [pltpu.make_async_copy(src, dst, sems.at[n]) for n, (src, dst) in enumerate(pairs)]
    for copy in copies:
        copy.start()
    return copies


def shape(dims, dtype=BF16):
    return jax.ShapeDtypeStruct(dims, dtype)


def nn(a, b):
    return lax.dot_general(a, b, (((1,), (0,)), ((), ())), preferred_element_type=F32)


def nt(a, b):
    return lax.dot_general(a, b, (((1,), (1,)), ((), ())), preferred_element_type=F32)


def iota(dims, axis):
    return lax.broadcasted_iota(jnp.int32, dims, axis)


def pair_low(a, b, half):
    lane = iota(a.shape, 1)
    return jnp.where(lane < half, a, pltpu.roll(b, half, 1))


def pair_high(a, b, half):
    lane = iota(a.shape, 1)
    return jnp.where(lane < half, pltpu.roll(a, half, 1), b)


def routing(routes_ref, gates_ref, experts):
    top, rows = routes_ref.shape
    expert = iota((experts, rows), 0)
    named = jnp.zeros((experts, rows), F32)
    gate = jnp.zeros((experts, rows), F32)
    for k in range(top):
        hit = expert == routes_ref[k : k + 1, :]
        named = named + jnp.where(hit, 1.0, 0.0)
        gate = gate + jnp.where(hit, gates_ref[k : k + 1, :], 0.0)
    before = jnp.where(iota((rows, rows), 0) < iota((rows, rows), 1), 1.0, 0.0).astype(BF16)
    earlier = nn(named.astype(BF16), before)
    return jnp.where(named > 0.0, earlier, -1.0).astype(jnp.int32), gate


def dispatch_body(routes_far, gates_far, tok_far, out_ref, slot_ref, gate_ref, routes_ref, gates_ref, tok_ref, sems):
    pairs = [(routes_far, routes_ref), (gates_far, gates_ref), (tok_far, tok_ref)]
    for copy in fetch(pairs, sems):
        copy.wait()
    experts, half, lanes = out_ref.shape
    rows = tok_ref.shape[1]
    cap = lanes // 2
    slot, gate = routing(routes_ref, gates_ref, experts)
    slot_ref[...] = slot
    gate_ref[...] = gate
    tok = jnp.concatenate([tok_ref[:half, :], tok_ref[half:, :]], axis=1)
    place = iota((lanes, rows), 0)
    place = jnp.where(place < cap, place, place - cap)
    low = iota((lanes, rows), 0) < cap
    for e in range(experts):
        sel = jnp.where(slot[e : e + 1, :] == place, 1.0, 0.0)
        sel = jnp.concatenate([jnp.where(low, sel, 0.0), jnp.where(low, 0.0, sel)], axis=1)
        out_ref[e] = nt(tok, sel.astype(BF16)).astype(BF16)


def spread_body(x_ref, in_ref, *refs):
    *tokens, out_ref = refs
    lanes_x, _, lanes = in_ref.shape
    width = out_ref.shape[0] // lanes_x
    half, cap = width // 2, lanes // 2
    groups = in_ref.shape[1] // half
    for x in range(lanes_x):
        top, mid, end = x * width, x * width + half, (x + 1) * width
        for q in range(groups // 2):
            a = in_ref[x, 2 * q * half : (2 * q + 1) * half, :].astype(F32)
            b = in_ref[x, (2 * q + 1) * half : (2 * q + 2) * half, :].astype(F32)
            cols = slice(q * lanes, (q + 1) * lanes)
            out_ref[top:mid, cols] = pair_low(a, b, cap).astype(BF16)
            out_ref[mid:end, cols] = pair_high(a, b, cap).astype(BF16)
    for tok, shift in zip(tokens, SHIFTS):
        at = pl.multiple_of(lax.rem(x_ref[0] + shift, lanes_x) * width, width)
        out_ref[pl.ds(at, width), groups * cap :] = tok[...]


def glu(gate, up):
    return (gate / (1.0 + jnp.exp(-gate)) * up).astype(BF16)


def hidden_body(y_ref, *refs):
    blocks = refs[: len(RING)]
    out_ref, flat_ref, weight_ref, sems = refs[-4:]
    weights = refs[len(RING) : -4]
    nx = len(weights) // 2 - 1
    units = weights[0].shape[0]
    width = blocks[0].shape[0] // nx
    ny = flat_ref.shape[0] // (nx * width)
    top = nx * units
    pairs = []
    for n, weight in enumerate(weights):
        at = n // 2 * units + (n % 2) * top if n < 2 * nx else n * units
        pairs.append((weight, weight_ref.at[at : at + units, :]))
    for block, shift in zip(blocks, RING):
        y = lax.rem(y_ref[0] + shift, ny)
        for n in range(nx):
            at = pl.multiple_of((n * ny + y) * width, width)
            pairs.append((block.at[n * width : (n + 1) * width, :], flat_ref.at[pl.ds(at, width), :]))
    for copy in fetch(pairs, sems):
        copy.wait()
    cols = out_ref.shape[2]
    both = nn(weight_ref[: 2 * top, :], flat_ref[:, :cols])
    routed = glu(both[:top], both[top:])
    both = nn(weight_ref[2 * top :, :], flat_ref[:, cols:])
    own = glu(both[:units], both[units:])
    fold = units // 2
    folded = jnp.concatenate([own[:fold], own[fold:]], axis=1)
    for y in range(ny):
        out_ref[y, :top, :] = routed
        out_ref[y, top : top + fold, :] = folded


def down_body(x_ref, hidden_ref, *refs):
    *weights, out_ref, flat_ref, down_ref, sems = refs
    nx = out_ref.shape[0]
    width = weights[0].shape[0]
    copies, at = [], 0
    for n, weight in enumerate(weights):
        copies.append((weight, down_ref.at[at : at + weight.shape[0], :]))
        at += weight.shape[0]
    copies = fetch(copies, sems)
    ny = hidden_ref.shape[0]
    units = flat_ref.shape[0] // (nx * ny)
    lanes = out_ref.shape[2]
    half, cap, fold = width // 2, lanes // 2, units // 2
    groups = (out_ref.shape[1] - ny * units) // half
    own = [lax.rem(x_ref[0] + shift, nx) for shift in SHIFTS]
    for n in range(nx):
        for y in range(ny):
            at = pl.multiple_of((own[n] * ny + y) * units, units)
            flat_ref[pl.ds(at, units), :] = hidden_ref[y, n * units : (n + 1) * units, :]
    for copy in copies:
        copy.wait()
    outs = nn(down_ref[...], flat_ref[...])
    for n in range(nx):
        out = outs[n * width : (n + 1) * width]
        for q in range(groups // 2):
            cols = slice(q * lanes, (q + 1) * lanes)
            a, b = out[:half, cols], out[half:, cols]
            out_ref[own[n], 2 * q * half : (2 * q + 1) * half, :] = pair_low(a, b, cap).astype(BF16)
            out_ref[own[n], (2 * q + 1) * half : (2 * q + 2) * half, :] = pair_high(a, b, cap).astype(BF16)
        for y in range(ny):
            at = groups * half + y * units
            both = hidden_ref[y, nx * units : nx * units + fold, :]
            out_ref[n, at : at + fold, :] = both[:, :lanes]
            out_ref[n, at + fold : at + units, :] = both[:, lanes:]


def combine_body(slot_ref, gate_ref, back_ref, tok_ref, hidden_ref, down_ref, out_ref, scored_ref):
    experts, half, lanes = back_ref.shape
    rows = tok_ref.shape[1]
    cap = lanes // 2
    place = iota((lanes, rows), 0)
    place = jnp.where(place < cap, place, place - cap)
    low = iota((lanes, rows), 0) < cap
    routed = jnp.zeros((half, 2 * rows), F32)
    for e in range(experts):
        mix = jnp.where(slot_ref[e : e + 1, :] == place, gate_ref[e : e + 1, :], 0.0)
        mix = jnp.concatenate([jnp.where(low, mix, 0.0), jnp.where(low, 0.0, mix)], axis=1)
        head = mix.astype(BF16)
        tail = (mix - head.astype(F32)).astype(BF16)
        routed = routed + nn(back_ref[e], head) + nn(back_ref[e], tail)
    depth = down_ref.shape[1] // hidden_ref.shape[0]
    skip = hidden_ref.shape[1] - depth
    shared = jnp.zeros((2 * half, rows), F32)
    for x in range(hidden_ref.shape[0]):
        shared = shared + nn(down_ref[:, x * depth : (x + 1) * depth], hidden_ref[x, skip:, :])
    routed = jnp.concatenate([routed[:, :rows], routed[:, rows:]], axis=0)
    out = (tok_ref[...].astype(F32) + shared + routed).astype(BF16)
    out_ref[...] = out
    take = iota((2 * SCORE_E, rows), 1) == rows - SCORE_E + iota((2 * SCORE_E, rows), 0)
    scored = nt(jnp.where(take, 1.0, 0.0).astype(BF16), out).astype(BF16)
    for g in range(scored_ref.shape[0]):
        scored_ref[g] = scored[:SCORE_E]


def pack_body(core_ref, rows_ref, out_ref):
    count, width = rows_ref.shape[0] // 2, rows_ref.shape[1]
    part = out_ref.shape[1]
    eye = jnp.where(iota((count, count), 0) == iota((count, count), 1), 1.0, 0.0).astype(BF16)
    mine = rows_ref[pl.ds(pl.multiple_of(core_ref[0] * count, count), count), :]
    flip = lax.dot_general(mine, eye, (((0,), (0,)), ((), ())), preferred_element_type=F32)
    packed = jnp.concatenate([flip[n : n + part] for n in range(0, width, part)], axis=1).astype(BF16)
    for n in range(out_ref.shape[0]):
        out_ref[n] = packed


def score_body(at_ref, rows_ref, vocab_ref, other_ref, targets_ref, out_ref, flat_ref):
    blocks, part, lanes = rows_ref.shape
    parts = flat_ref.shape[0] // (blocks * part)
    count = lanes // parts
    for b in range(blocks):
        block = rows_ref[b].astype(F32)
        for n in range(parts):
            at = (b * parts + n) * part
            turned = block if n == 0 else pltpu.roll(block, lanes - n * count, 1)
            flat_ref[at : at + part, :] = turned.astype(BF16)
    target = targets_ref[pl.ds(at_ref[0], 1), :]
    sums = jnp.zeros((1, lanes), F32)
    hits = jnp.zeros((1, lanes), F32)
    for n, block in enumerate((vocab_ref, other_ref)):
        logits = nn(block[...], flat_ref[...])
        entry = iota(logits.shape, 0) + at_ref[1 + n]
        sums = sums + jnp.sum(jnp.exp(logits), axis=0, keepdims=True)
        hits = hits + jnp.sum(jnp.where(entry == target, logits, 0.0), axis=0, keepdims=True)
    lane = iota(sums.shape, 1)
    out_ref[...] = jnp.broadcast_to(jnp.where(lane < count, sums, pltpu.roll(hits, count, 1)), out_ref.shape)


SHIFTS = (0, 1, 3, 2)
RING = (0, 7, 1, 6, 2, 5, 3, 4)


def exchange(value, axes):
    return lax.all_to_all(value, axes, 0, 0, tiled=True)


def spread_all(value, axes, count):
    return lax.all_to_all(
        jnp.broadcast_to(value[None], (count, *value.shape)), axes, 0, 0, tiled=True
    )


def from_shift(value, axis, shift):
    count = lax.axis_size(axis)
    return lax.ppermute(value, axis, [((i + shift) % count, i) for i in range(count)])


def around(value, axis, between):
    count = lax.axis_size(axis)
    left = right = value
    got = [value]
    for hop in range(3):
        if hop:
            left, right = between(hop, left, right)
        left = from_shift(left, axis, count - 1)
        right = from_shift(right, axis, 1)
        got += [left, right]
    left, right = between(3, left, right)
    return [*got, from_shift(left, axis, count - 1)]


def shards(tokens, routes, gates, w_gate, w_up, w_down, shared_gate, shared_up, shared_down, vocab, targets):
    nx, ny = lax.axis_size("x"), lax.axis_size("y")
    nz, nc = lax.axis_size("z"), lax.axis_size("core")
    groups, lanes = nz * nc, nx * ny
    rows, width = tokens.shape
    half, cap = width // 2, rows // 2
    near = groups // nx
    units = w_gate.shape[1]
    tok = tokens.T
    x_at = lax.axis_index("x").astype(jnp.int32).reshape(1)
    y_at = lax.axis_index("y").astype(jnp.int32).reshape(1)

    outgoing, slot, gate = call(
        dispatch_body,
        [
            shape((groups, half, 2 * cap)),
            shape((groups, rows), jnp.int32),
            shape((groups, rows), F32),
        ],
        [routes.T, gates.T, tok],
        far=range(3),
        scratch=[
            pltpu.VMEM(routes.T.shape, jnp.int32),
            pltpu.VMEM(gates.T.shape, F32),
            pltpu.VMEM(tok.shape, BF16),
            pltpu.SemaphoreType.DMA((3,)),
        ],
        limit=60,
    )
    arrived = exchange(outgoing, LINE)
    arrived, t1, t3, t2 = lax.optimization_barrier((arrived, *[from_shift(tok, "x", shift) for shift in SHIFTS[1:]]))
    quarter = exchange(arrived.reshape(nx, near * half, 2 * cap), "x")
    (spread,) = call(
        spread_body,
        [shape((nx * width, near * cap + rows))],
        [x_at, quarter, tok, t1, t3, t2],
        scalars=1,
    )
    spread, own_gate, own_up = lax.optimization_barrier((spread, w_gate[0], w_up[0]))
    after = {"own_gate": own_gate, "own_up": own_up}
    after["g1"] = from_shift(own_gate, "x", 1)
    after["u3"] = from_shift(own_up, "x", nx - 1)

    def between(hop, left, right):
        if hop == 1:
            left, right, after["g1"], after["u3"] = lax.optimization_barrier((left, right, after["g1"], after["u3"]))
            after["g2"] = from_shift(after["g1"], "x", 1)
            after["u2"] = from_shift(after["u3"], "x", nx - 1)
        if hop == 2:
            names = ("g2", "u2", "own_gate", "own_up")
            left, right, *due = lax.optimization_barrier((left, right, *[after[n] for n in names]))
            after.update(zip(names, due))
            after["g3"] = from_shift(after["own_gate"], "x", nx - 1)
            after["u1"] = from_shift(after["own_up"], "x", 1)
        if hop == 3:
            names = ("g3", "u1", "down")
            after["down"] = w_down[0].T
            left, right, *due = lax.optimization_barrier((left, right, *[after[n] for n in names]))
            after.update(zip(names, due))
            after["d1"] = from_shift(after["down"], "x", 1)
            after["d3"] = from_shift(after["down"], "x", nx - 1)
        return left, right

    blocks = around(spread, "y", between)
    near_weights = [after[n] for n in ("own_gate", "own_up", "g1", "u1", "g3", "u3", "g2", "u2")]
    (hidden,) = call(
        hidden_body,
        [shape((ny, nx * units + units // 2 + 8, near * cap))],
        [y_at, *blocks, *near_weights, shared_gate, shared_up],
        scalars=1,
        far=(*range(1, len(RING)), *range(len(RING) + 1, len(RING) + 2 * nx + 3)),
        scratch=[
            pltpu.VMEM((lanes * width, near * cap + rows), BF16),
            pltpu.VMEM((2 * (nx + 1) * units, lanes * width), BF16),
            pltpu.SemaphoreType.DMA((2 * nx + 2 + lanes,)),
        ],
        limit=56,
    )
    hidden, d1, d3 = lax.optimization_barrier((hidden, after["d1"], after["d3"]))
    d2 = [from_shift(d1[:half], "x", 1), from_shift(d3[half:], "x", nx - 1)]
    all_hidden = exchange(hidden, "y")
    (returned,) = call(
        down_body,
        [shape((nx, near * half + ny * units, 2 * cap))],
        [x_at, all_hidden, after["down"], d1, d3, *d2],
        scalars=1,
        far=range(2, 3 + nx),
        scratch=[
            pltpu.VMEM((lanes * units, near * cap), BF16),
            pltpu.VMEM((nx * width, lanes * units), BF16),
            pltpu.SemaphoreType.DMA((nx + 1,)),
        ],
        limit=40,
    )
    mixed = lax.all_to_all(returned, "x", 0, 0, tiled=True)
    back = mixed[:, : near * half].reshape(groups, half, 2 * cap)
    back = lax.all_to_all(back, LINE, 0, 0, tiled=True)
    layer_out, scored = call(
        combine_body,
        [shape((width, rows)), shape((groups, SCORE_E, width))],
        [slot, gate, back, tok, mixed, shared_down.T],
    )
    line_rows = exchange(scored, LINE).reshape(groups * SCORE_E, width)
    count = groups * SCORE_E // nc
    core = lax.axis_index("core").astype(jnp.int32)
    (packed,) = call(
        pack_body,
        [shape((lanes, width * count // (2 * cap), 2 * cap))],
        [core.reshape(1), line_rows],
        scalars=1,
    )
    every = exchange(packed, PLANE)
    other_vocab = lax.ppermute(vocab, "core", [(0, 1), (1, 0)])
    place = lax.axis_index("x") * ny + lax.axis_index("y")
    first = [
        (((lax.axis_index("z") * nc + c) * lanes + place) * vocab.shape[0]).astype(jnp.int32)
        for c in (core, 1 - core)
    ]
    (sums,) = call(
        score_body,
        [shape((8, 2 * cap), F32)],
        [
            jnp.stack([core, *first]),
            every,
            vocab,
            other_vocab,
            jnp.tile(targets.reshape(nc, count), (1, 2 * cap // count)),
        ],
        scalars=1,
        scratch=[pltpu.VMEM((lanes * width, 2 * cap), BF16)],
    )
    sums = jnp.sum(spread_all(sums[:1], PLANE, lanes), axis=0)
    sums = jnp.sum(spread_all(sums, LINE, groups).reshape(nz, nc, 2 * cap), axis=0)
    return layer_out.T, (sums[:, count : 2 * count] - jnp.log(sums[:, :count])).reshape(-1)


def solution(mesh):
    mesh = Mesh(mesh.devices.reshape(8, 2, 4, 8), ("z", "core", "x", "y"))
    placed = (
        P(LINE, PLANE),
        P(LINE, None),
        P(LINE, None),
        P(LINE, PLANE, None),
        P(LINE, PLANE, None),
        P(LINE, None, PLANE),
        P(PLANE, None),
        P(PLANE, None),
        P(None, PLANE),
        P((*LINE, *PLANE), None),
        P(),
    )
    return jax.shard_map(
        shards, mesh=mesh, in_specs=placed, out_specs=(P(LINE, PLANE), P()), check_vma=False
    )
```

```python
import jax
import jax.numpy as jnp
from jax import lax
from jax.experimental import pallas as pl
from jax.experimental.pallas import tpu as pltpu
from jax.sharding import Mesh
from jax.sharding import PartitionSpec as P

SCORE_E = 4
F32 = jnp.float32
BF16 = jnp.bfloat16
LINE = ("z", "core")
PLANE = ("x", "y")


def call(body, outs, args, scalars=0, far=(), scratch=(), limit=16):
    specs = [
        pl.BlockSpec(memory_space=pltpu.SMEM if n < scalars else pltpu.HBM if n in far else pltpu.VMEM)
        for n in range(len(args))
    ]
    moved = sum(a.size * a.dtype.itemsize for a in args)
    moved += sum(o.size * o.dtype.itemsize for o in outs)
    return pl.pallas_call(
        body,
        out_shape=outs,
        in_specs=specs,
        out_specs=[pl.BlockSpec(memory_space=pltpu.VMEM) for _ in outs],
        scratch_shapes=list(scratch),
        cost_estimate=pl.CostEstimate(flops=0, bytes_accessed=moved, transcendentals=0),
        compiler_params=pltpu.CompilerParams(vmem_limit_bytes=limit << 20),
    )(*args)


def fetch(pairs, sems):
    copies = [pltpu.make_async_copy(src, dst, sems.at[n]) for n, (src, dst) in enumerate(pairs)]
    for copy in copies:
        copy.start()
    return copies


def shape(dims, dtype=BF16):
    return jax.ShapeDtypeStruct(dims, dtype)


def nn(a, b):
    return lax.dot_general(a, b, (((1,), (0,)), ((), ())), preferred_element_type=F32)


def nt(a, b):
    return lax.dot_general(a, b, (((1,), (1,)), ((), ())), preferred_element_type=F32)


def iota(dims, axis):
    return lax.broadcasted_iota(jnp.int32, dims, axis)


def pair_low(a, b, half):
    lane = iota(a.shape, 1)
    return jnp.where(lane < half, a, pltpu.roll(b, half, 1))


def pair_high(a, b, half):
    lane = iota(a.shape, 1)
    return jnp.where(lane < half, pltpu.roll(a, half, 1), b)


def routing(routes_ref, gates_ref, experts):
    top, rows = routes_ref.shape
    expert = iota((experts, rows), 0)
    named = jnp.zeros((experts, rows), F32)
    gate = jnp.zeros((experts, rows), F32)
    for k in range(top):
        hit = expert == routes_ref[k : k + 1, :]
        named = named + jnp.where(hit, 1.0, 0.0)
        gate = gate + jnp.where(hit, gates_ref[k : k + 1, :], 0.0)
    before = jnp.where(iota((rows, rows), 0) < iota((rows, rows), 1), 1.0, 0.0).astype(BF16)
    earlier = nn(named.astype(BF16), before)
    return jnp.where(named > 0.0, earlier, -1.0).astype(jnp.int32), gate


def dispatch_body(routes_far, gates_far, tok_far, out_ref, slot_ref, gate_ref, routes_ref, gates_ref, tok_ref, sems):
    pairs = [(routes_far, routes_ref), (gates_far, gates_ref), (tok_far, tok_ref)]
    for copy in fetch(pairs, sems):
        copy.wait()
    experts, half, lanes = out_ref.shape
    rows = tok_ref.shape[1]
    cap = lanes // 2
    slot, gate = routing(routes_ref, gates_ref, experts)
    slot_ref[...] = slot
    gate_ref[...] = gate
    tok = jnp.concatenate([tok_ref[:half, :], tok_ref[half:, :]], axis=1)
    place = iota((lanes, rows), 0)
    place = jnp.where(place < cap, place, place - cap)
    low = iota((lanes, rows), 0) < cap
    for e in range(experts):
        sel = jnp.where(slot[e : e + 1, :] == place, 1.0, 0.0)
        sel = jnp.concatenate([jnp.where(low, sel, 0.0), jnp.where(low, 0.0, sel)], axis=1)
        out_ref[e] = nt(tok, sel.astype(BF16)).astype(BF16)


def spread_body(x_ref, in_ref, *refs):
    *tokens, out_ref = refs
    lanes_x, _, lanes = in_ref.shape
    width = out_ref.shape[0] // lanes_x
    half, cap = width // 2, lanes // 2
    groups = in_ref.shape[1] // half
    for x in range(lanes_x):
        top, mid, end = x * width, x * width + half, (x + 1) * width
        for q in range(groups // 2):
            a = in_ref[x, 2 * q * half : (2 * q + 1) * half, :].astype(F32)
            b = in_ref[x, (2 * q + 1) * half : (2 * q + 2) * half, :].astype(F32)
            cols = slice(q * lanes, (q + 1) * lanes)
            out_ref[top:mid, cols] = pair_low(a, b, cap).astype(BF16)
            out_ref[mid:end, cols] = pair_high(a, b, cap).astype(BF16)
    for tok, shift in zip(tokens, SHIFTS):
        at = pl.multiple_of(lax.rem(x_ref[0] + shift, lanes_x) * width, width)
        out_ref[pl.ds(at, width), groups * cap :] = tok[...]


def glu(gate, up):
    return (gate / (1.0 + jnp.exp(-gate)) * up).astype(BF16)


def hidden_body(y_ref, *refs):
    blocks = refs[: len(RING)]
    out_ref, flat_ref, weight_ref, sems = refs[-4:]
    weights = refs[len(RING) : -4]
    nx = len(weights) // 2 - 1
    units = weights[0].shape[0]
    width = blocks[0].shape[0] // nx
    ny = flat_ref.shape[0] // (nx * width)
    top = nx * units
    pairs = []
    for n, weight in enumerate(weights):
        at = n // 2 * units + (n % 2) * top if n < 2 * nx else n * units
        pairs.append((weight, weight_ref.at[at : at + units, :]))
    for block, shift in zip(blocks, RING):
        y = lax.rem(y_ref[0] + shift, ny)
        for n in range(nx):
            at = pl.multiple_of((n * ny + y) * width, width)
            pairs.append((block.at[n * width : (n + 1) * width, :], flat_ref.at[pl.ds(at, width), :]))
    for copy in fetch(pairs, sems):
        copy.wait()
    cols = out_ref.shape[2]
    both = nn(weight_ref[: 2 * top, :], flat_ref[:, :cols])
    routed = glu(both[:top], both[top:])
    both = nn(weight_ref[2 * top :, :], flat_ref[:, cols:])
    own = glu(both[:units], both[units:])
    fold = units // 2
    folded = jnp.concatenate([own[:fold], own[fold:]], axis=1)
    for y in range(ny):
        out_ref[y, :top, :] = routed
        out_ref[y, top : top + fold, :] = folded


def down_body(x_ref, hidden_ref, *refs):
    *weights, out_ref, flat_ref, down_ref, sems = refs
    nx = out_ref.shape[0]
    width = weights[0].shape[0]
    copies, at = [], 0
    for n, weight in enumerate(weights):
        copies.append((weight, down_ref.at[at : at + weight.shape[0], :]))
        at += weight.shape[0]
    copies = fetch(copies, sems)
    ny = hidden_ref.shape[0]
    units = flat_ref.shape[0] // (nx * ny)
    lanes = out_ref.shape[2]
    half, cap, fold = width // 2, lanes // 2, units // 2
    groups = (out_ref.shape[1] - ny * units) // half
    own = [lax.rem(x_ref[0] + shift, nx) for shift in SHIFTS]
    for n in range(nx):
        for y in range(ny):
            at = pl.multiple_of((own[n] * ny + y) * units, units)
            flat_ref[pl.ds(at, units), :] = hidden_ref[y, n * units : (n + 1) * units, :]
    for copy in copies:
        copy.wait()
    outs = nn(down_ref[...], flat_ref[...])
    for n in range(nx):
        out = outs[n * width : (n + 1) * width]
        for q in range(groups // 2):
            cols = slice(q * lanes, (q + 1) * lanes)
            a, b = out[:half, cols], out[half:, cols]
            out_ref[own[n], 2 * q * half : (2 * q + 1) * half, :] = pair_low(a, b, cap).astype(BF16)
            out_ref[own[n], (2 * q + 1) * half : (2 * q + 2) * half, :] = pair_high(a, b, cap).astype(BF16)
        for y in range(ny):
            at = groups * half + y * units
            both = hidden_ref[y, nx * units : nx * units + fold, :]
            out_ref[n, at : at + fold, :] = both[:, :lanes]
            out_ref[n, at + fold : at + units, :] = both[:, lanes:]


def combine_body(slot_ref, gate_ref, back_ref, tok_ref, hidden_ref, down_ref, out_ref, scored_ref):
    experts, half, lanes = back_ref.shape
    rows = tok_ref.shape[1]
    cap = lanes // 2
    place = iota((lanes, rows), 0)
    place = jnp.where(place < cap, place, place - cap)
    low = iota((lanes, rows), 0) < cap
    routed = jnp.zeros((half, 2 * rows), F32)
    for e in range(experts):
        mix = jnp.where(slot_ref[e : e + 1, :] == place, gate_ref[e : e + 1, :], 0.0)
        mix = jnp.concatenate([jnp.where(low, mix, 0.0), jnp.where(low, 0.0, mix)], axis=1)
        head = mix.astype(BF16)
        tail = (mix - head.astype(F32)).astype(BF16)
        routed = routed + nn(back_ref[e], head) + nn(back_ref[e], tail)
    depth = down_ref.shape[1] // hidden_ref.shape[0]
    skip = hidden_ref.shape[1] - depth
    shared = jnp.zeros((2 * half, rows), F32)
    for x in range(hidden_ref.shape[0]):
        shared = shared + nn(down_ref[:, x * depth : (x + 1) * depth], hidden_ref[x, skip:, :])
    routed = jnp.concatenate([routed[:, :rows], routed[:, rows:]], axis=0)
    out = (tok_ref[...].astype(F32) + shared + routed).astype(BF16)
    out_ref[...] = out
    take = iota((2 * SCORE_E, rows), 1) == rows - SCORE_E + iota((2 * SCORE_E, rows), 0)
    scored = nt(jnp.where(take, 1.0, 0.0).astype(BF16), out).astype(BF16)
    for g in range(scored_ref.shape[0]):
        scored_ref[g] = scored[:SCORE_E]


def pack_body(core_ref, rows_ref, out_ref):
    count, width = rows_ref.shape[0] // 2, rows_ref.shape[1]
    part = out_ref.shape[1]
    eye = jnp.where(iota((count, count), 0) == iota((count, count), 1), 1.0, 0.0).astype(BF16)
    mine = rows_ref[pl.ds(pl.multiple_of(core_ref[0] * count, count), count), :]
    flip = lax.dot_general(mine, eye, (((0,), (0,)), ((), ())), preferred_element_type=F32)
    packed = jnp.concatenate([flip[n : n + part] for n in range(0, width, part)], axis=1).astype(BF16)
    for n in range(out_ref.shape[0]):
        out_ref[n] = packed


def score_body(at_ref, rows_ref, vocab_ref, other_ref, targets_ref, out_ref, flat_ref):
    blocks, part, lanes = rows_ref.shape
    parts = flat_ref.shape[0] // (blocks * part)
    count = lanes // parts
    for b in range(blocks):
        block = rows_ref[b].astype(F32)
        for n in range(parts):
            at = (b * parts + n) * part
            turned = block if n == 0 else pltpu.roll(block, lanes - n * count, 1)
            flat_ref[at : at + part, :] = turned.astype(BF16)
    target = targets_ref[pl.ds(at_ref[0], 1), :]
    sums = jnp.zeros((1, lanes), F32)
    hits = jnp.zeros((1, lanes), F32)
    for n, block in enumerate((vocab_ref, other_ref)):
        logits = nn(block[...], flat_ref[...])
        entry = iota(logits.shape, 0) + at_ref[1 + n]
        sums = sums + jnp.sum(jnp.exp(logits), axis=0, keepdims=True)
        hits = hits + jnp.sum(jnp.where(entry == target, logits, 0.0), axis=0, keepdims=True)
    lane = iota(sums.shape, 1)
    out_ref[...] = jnp.broadcast_to(jnp.where(lane < count, sums, pltpu.roll(hits, count, 1)), out_ref.shape)


SHIFTS = (0, 1, 3, 2)
RING = (0, 7, 1, 6, 2, 5, 3, 4)


def exchange(value, axes):
    return lax.all_to_all(value, axes, 0, 0, tiled=True)


def spread_all(value, axes, count):
    return lax.all_to_all(
        jnp.broadcast_to(value[None], (count, *value.shape)), axes, 0, 0, tiled=True
    )


def from_shift(value, axis, shift):
    count = lax.axis_size(axis)
    return lax.ppermute(value, axis, [((i + shift) % count, i) for i in range(count)])


def around(value, axis, between):
    count = lax.axis_size(axis)
    left = right = value
    got = [value]
    for hop in range(3):
        if hop:
            left, right = between(hop, left, right)
        left = from_shift(left, axis, count - 1)
        right = from_shift(right, axis, 1)
        got += [left, right]
    left, right = between(3, left, right)
    return [*got, from_shift(left, axis, count - 1)]


def shards(tokens, routes, gates, w_gate, w_up, w_down, shared_gate, shared_up, shared_down, vocab, targets):
    nx, ny = lax.axis_size("x"), lax.axis_size("y")
    nz, nc = lax.axis_size("z"), lax.axis_size("core")
    groups, lanes = nz * nc, nx * ny
    rows, width = tokens.shape
    half, cap = width // 2, rows // 2
    near = groups // nx
    units = w_gate.shape[1]
    tok = tokens.T
    x_at = lax.axis_index("x").astype(jnp.int32).reshape(1)
    y_at = lax.axis_index("y").astype(jnp.int32).reshape(1)

    outgoing, slot, gate = call(
        dispatch_body,
        [
            shape((groups, half, 2 * cap)),
            shape((groups, rows), jnp.int32),
            shape((groups, rows), F32),
        ],
        [routes.T, gates.T, tok],
        far=range(3),
        scratch=[
            pltpu.VMEM(routes.T.shape, jnp.int32),
            pltpu.VMEM(gates.T.shape, F32),
            pltpu.VMEM(tok.shape, BF16),
            pltpu.SemaphoreType.DMA((3,)),
        ],
        limit=60,
    )
    arrived = exchange(outgoing, LINE)
    arrived, t1, t3, t2 = lax.optimization_barrier((arrived, *[from_shift(tok, "x", shift) for shift in SHIFTS[1:]]))
    quarter = exchange(arrived.reshape(nx, near * half, 2 * cap), "x")
    (spread,) = call(
        spread_body,
        [shape((nx * width, near * cap + rows))],
        [x_at, quarter, tok, t1, t3, t2],
        scalars=1,
    )
    spread, own_gate, own_up = lax.optimization_barrier((spread, w_gate[0], w_up[0]))
    after = {"own_gate": own_gate, "own_up": own_up, "down": w_down[0].T}
    after["g1"] = from_shift(own_gate, "x", 1)
    after["u3"] = from_shift(own_up, "x", nx - 1)

    def tie(left, right, *names):
        left, right, *due = lax.optimization_barrier((left, right, *[after[n] for n in names]))
        after.update(zip(names, due))
        return left, right

    def between(hop, left, right):
        if hop == 1:
            left, right = tie(left, right, "own_gate", "own_up")
            after["g3"] = from_shift(after["own_gate"], "x", nx - 1)
            after["u1"] = from_shift(after["own_up"], "x", 1)
        if hop == 2:
            left, right = tie(left, right, "g1", "u3")
            after["g2"] = from_shift(after["g1"], "x", 1)
            after["u2"] = from_shift(after["u3"], "x", nx - 1)
        if hop == 3:
            left, right = tie(left, right, "g3", "u1", "down")
            after["d1"] = from_shift(after["down"], "x", 1)
            after["d3"] = from_shift(after["down"], "x", nx - 1)
        return left, right

    blocks = around(spread, "y", between)
    near_weights = [after[n] for n in ("own_gate", "own_up", "g1", "u1", "g3", "u3", "g2", "u2")]
    (hidden,) = call(
        hidden_body,
        [shape((ny, nx * units + units // 2 + 8, near * cap))],
        [y_at, *blocks, *near_weights, shared_gate, shared_up],
        scalars=1,
        far=(*range(1, len(RING)), *range(len(RING) + 1, len(RING) + 2 * nx + 3)),
        scratch=[
            pltpu.VMEM((lanes * width, near * cap + rows), BF16),
            pltpu.VMEM((2 * (nx + 1) * units, lanes * width), BF16),
            pltpu.SemaphoreType.DMA((2 * nx + 2 + lanes,)),
        ],
        limit=56,
    )
    hidden, d1, d3 = lax.optimization_barrier((hidden, after["d1"], after["d3"]))
    d2 = [from_shift(d1[:half], "x", 1), from_shift(d3[half:], "x", nx - 1)]
    all_hidden = exchange(hidden, "y")
    (returned,) = call(
        down_body,
        [shape((nx, near * half + ny * units, 2 * cap))],
        [x_at, all_hidden, after["down"], d1, d3, *d2],
        scalars=1,
        far=range(2, 3 + nx),
        scratch=[
            pltpu.VMEM((lanes * units, near * cap), BF16),
            pltpu.VMEM((nx * width, lanes * units), BF16),
            pltpu.SemaphoreType.DMA((nx + 1,)),
        ],
        limit=40,
    )
    mixed = lax.all_to_all(returned, "x", 0, 0, tiled=True)
    back = mixed[:, : near * half].reshape(groups, half, 2 * cap)
    back = lax.all_to_all(back, LINE, 0, 0, tiled=True)
    layer_out, scored = call(
        combine_body,
        [shape((width, rows)), shape((groups, SCORE_E, width))],
        [slot, gate, back, tok, mixed, shared_down.T],
    )
    line_rows = exchange(scored, LINE).reshape(groups * SCORE_E, width)
    count = groups * SCORE_E // nc
    core = lax.axis_index("core").astype(jnp.int32)
    (packed,) = call(
        pack_body,
        [shape((lanes, width * count // (2 * cap), 2 * cap))],
        [core.reshape(1), line_rows],
        scalars=1,
    )
    every = exchange(packed, PLANE)
    other_vocab = lax.ppermute(vocab, "core", [(0, 1), (1, 0)])
    place = lax.axis_index("x") * ny + lax.axis_index("y")
    first = [
        (((lax.axis_index("z") * nc + c) * lanes + place) * vocab.shape[0]).astype(jnp.int32)
        for c in (core, 1 - core)
    ]
    (sums,) = call(
        score_body,
        [shape((8, 2 * cap), F32)],
        [
            jnp.stack([core, *first]),
            every,
            vocab,
            other_vocab,
            jnp.tile(targets.reshape(nc, count), (1, 2 * cap // count)),
        ],
        scalars=1,
        scratch=[pltpu.VMEM((lanes * width, 2 * cap), BF16)],
    )
    sums = jnp.sum(spread_all(sums[:1], PLANE, lanes), axis=0)
    sums = jnp.sum(spread_all(sums, LINE, groups).reshape(nz, nc, 2 * cap), axis=0)
    return layer_out.T, (sums[:, count : 2 * count] - jnp.log(sums[:, :count])).reshape(-1)


def solution(mesh):
    mesh = Mesh(mesh.devices.reshape(8, 2, 4, 8), ("z", "core", "x", "y"))
    placed = (
        P(LINE, PLANE),
        P(LINE, None),
        P(LINE, None),
        P(LINE, PLANE, None),
        P(LINE, PLANE, None),
        P(LINE, None, PLANE),
        P(PLANE, None),
        P(PLANE, None),
        P(None, PLANE),
        P((*LINE, *PLANE), None),
        P(),
    )
    return jax.shard_map(
        shards, mesh=mesh, in_specs=placed, out_specs=(P(LINE, PLANE), P()), check_vma=False
    )
```

```python
import jax
import jax.numpy as jnp
from jax import lax
from jax.experimental import pallas as pl
from jax.experimental.pallas import tpu as pltpu
from jax.sharding import Mesh
from jax.sharding import PartitionSpec as P

SCORE_E = 4
F32 = jnp.float32
BF16 = jnp.bfloat16
LINE = ("z", "core")
PLANE = ("x", "y")


def call(body, outs, args, scalars=0, far=(), scratch=(), limit=16, out_space=pltpu.VMEM):
    specs = [
        pl.BlockSpec(memory_space=pltpu.SMEM if n < scalars else pltpu.HBM if n in far else pltpu.VMEM)
        for n in range(len(args))
    ]
    moved = sum(a.size * a.dtype.itemsize for a in args)
    moved += sum(o.size * o.dtype.itemsize for o in outs)
    return pl.pallas_call(
        body,
        out_shape=outs,
        in_specs=specs,
        out_specs=[pl.BlockSpec(memory_space=out_space) for _ in outs],
        scratch_shapes=list(scratch),
        cost_estimate=pl.CostEstimate(flops=0, bytes_accessed=moved, transcendentals=0),
        compiler_params=pltpu.CompilerParams(vmem_limit_bytes=limit << 20),
    )(*args)


def fetch(pairs, sems):
    copies = [pltpu.make_async_copy(src, dst, sems.at[n]) for n, (src, dst) in enumerate(pairs)]
    for copy in copies:
        copy.start()
    return copies


def shape(dims, dtype=BF16):
    return jax.ShapeDtypeStruct(dims, dtype)


def nn(a, b):
    return lax.dot_general(a, b, (((1,), (0,)), ((), ())), preferred_element_type=F32)


def nt(a, b):
    return lax.dot_general(a, b, (((1,), (1,)), ((), ())), preferred_element_type=F32)


def iota(dims, axis):
    return lax.broadcasted_iota(jnp.int32, dims, axis)


def pair_low(a, b, half):
    lane = iota(a.shape, 1)
    return jnp.where(lane < half, a, pltpu.roll(b, half, 1))


def pair_high(a, b, half):
    lane = iota(a.shape, 1)
    return jnp.where(lane < half, pltpu.roll(a, half, 1), b)


def routing(routes_ref, gates_ref, experts):
    top, rows = routes_ref.shape
    expert = iota((experts, rows), 0)
    named = jnp.zeros((experts, rows), F32)
    gate = jnp.zeros((experts, rows), F32)
    for k in range(top):
        hit = expert == routes_ref[k : k + 1, :]
        named = named + jnp.where(hit, 1.0, 0.0)
        gate = gate + jnp.where(hit, gates_ref[k : k + 1, :], 0.0)
    before = jnp.where(iota((rows, rows), 0) < iota((rows, rows), 1), 1.0, 0.0).astype(BF16)
    earlier = nn(named.astype(BF16), before)
    return jnp.where(named > 0.0, earlier, -1.0).astype(jnp.int32), gate


def dispatch_body(routes_far, gates_far, tok_far, out_ref, slot_ref, gate_ref, routes_ref, gates_ref, tok_ref, sems):
    pairs = [(routes_far, routes_ref), (gates_far, gates_ref), (tok_far, tok_ref)]
    for copy in fetch(pairs, sems):
        copy.wait()
    experts, half, lanes = out_ref.shape
    rows = tok_ref.shape[1]
    cap = lanes // 2
    slot, gate = routing(routes_ref, gates_ref, experts)
    slot_ref[...] = slot
    gate_ref[...] = gate
    tok = jnp.concatenate([tok_ref[:half, :], tok_ref[half:, :]], axis=1)
    place = iota((lanes, rows), 0)
    place = jnp.where(place < cap, place, place - cap)
    low = iota((lanes, rows), 0) < cap
    for e in range(experts):
        sel = jnp.where(slot[e : e + 1, :] == place, 1.0, 0.0)
        sel = jnp.concatenate([jnp.where(low, sel, 0.0), jnp.where(low, 0.0, sel)], axis=1)
        out_ref[e] = nt(tok, sel.astype(BF16)).astype(BF16)


def spread_body(in_ref, out_ref):
    lanes_x, _, lanes = in_ref.shape
    width = out_ref.shape[0] // lanes_x
    half, cap = width // 2, lanes // 2
    for x in range(lanes_x):
        top, mid, end = x * width, x * width + half, (x + 1) * width
        for q in range(out_ref.shape[1] // lanes):
            a = in_ref[x, 2 * q * half : (2 * q + 1) * half, :].astype(F32)
            b = in_ref[x, (2 * q + 1) * half : (2 * q + 2) * half, :].astype(F32)
            cols = slice(q * lanes, (q + 1) * lanes)
            out_ref[top:mid, cols] = pair_low(a, b, cap).astype(BF16)
            out_ref[mid:end, cols] = pair_high(a, b, cap).astype(BF16)


def stack_body(gate_ref, up_ref, out_ref, sems):
    units = gate_ref.shape[0]
    for copy in fetch([(gate_ref, out_ref.at[:units, :]), (up_ref, out_ref.at[units:, :])], sems):
        copy.wait()


def glu(gate, up):
    return (gate / (1.0 + jnp.exp(-gate)) * up).astype(BF16)


def hidden_body(y_ref, *refs):
    out_ref, flat_ref, weight_ref, tok_ref, sems = refs[-5:]
    blocks = refs[: len(RING)]
    *stacked, shared_gate, shared_up, tok_far = refs[len(RING) : -5]
    nx = len(stacked)
    units = shared_gate.shape[0]
    width = blocks[0].shape[0] // nx
    ny = flat_ref.shape[0] // (nx * width)
    top = nx * units
    pairs = [
        (shared_gate, weight_ref.at[2 * top : 2 * top + units, :]),
        (shared_up, weight_ref.at[2 * top + units :, :]),
        (tok_far, tok_ref),
    ]
    for n, block in enumerate(stacked):
        pairs.append((block.at[:units, :], weight_ref.at[n * units : (n + 1) * units, :]))
        pairs.append((block.at[units:, :], weight_ref.at[top + n * units : top + (n + 1) * units, :]))
    for block, shift in zip(blocks, RING):
        y = lax.rem(y_ref[0] + shift, ny)
        for n in range(nx):
            at = pl.multiple_of((n * ny + y) * width, width)
            pairs.append((block.at[n * width : (n + 1) * width, :], flat_ref.at[pl.ds(at, width), :]))
    copies = fetch(pairs, sems)
    for copy in copies[:3]:
        copy.wait()
    both = nn(weight_ref[2 * top :, :], tok_ref[...])
    own = glu(both[:units], both[units:])
    for copy in copies[3:]:
        copy.wait()
    both = nn(weight_ref[: 2 * top, :], flat_ref[...])
    routed = glu(both[:top], both[top:])
    fold = units // 2
    folded = jnp.concatenate([own[:fold], own[fold:]], axis=1)
    for y in range(ny):
        out_ref[y, :top, :] = routed
        out_ref[y, top : top + fold, :] = folded


def down_body(x_ref, hidden_ref, *refs):
    *weights, out_ref, flat_ref, down_ref, sems = refs
    nx = out_ref.shape[0]
    width = weights[0].shape[0]
    copies, at = [], 0
    for n, weight in enumerate(weights):
        copies.append((weight, down_ref.at[at : at + weight.shape[0], :]))
        at += weight.shape[0]
    copies = fetch(copies, sems)
    ny = hidden_ref.shape[0]
    units = flat_ref.shape[0] // (nx * ny)
    lanes = out_ref.shape[2]
    half, cap, fold = width // 2, lanes // 2, units // 2
    groups = (out_ref.shape[1] - ny * units) // half
    own = [lax.rem(x_ref[0] + shift, nx) for shift in SHIFTS]
    for n in range(nx):
        for y in range(ny):
            at = pl.multiple_of((own[n] * ny + y) * units, units)
            flat_ref[pl.ds(at, units), :] = hidden_ref[y, n * units : (n + 1) * units, :]
    for copy in copies:
        copy.wait()
    outs = nn(down_ref[...], flat_ref[...])
    for n in range(nx):
        out = outs[n * width : (n + 1) * width]
        for q in range(groups // 2):
            cols = slice(q * lanes, (q + 1) * lanes)
            a, b = out[:half, cols], out[half:, cols]
            out_ref[own[n], 2 * q * half : (2 * q + 1) * half, :] = pair_low(a, b, cap).astype(BF16)
            out_ref[own[n], (2 * q + 1) * half : (2 * q + 2) * half, :] = pair_high(a, b, cap).astype(BF16)
        for y in range(ny):
            at = groups * half + y * units
            both = hidden_ref[y, nx * units : nx * units + fold, :]
            out_ref[n, at : at + fold, :] = both[:, :lanes]
            out_ref[n, at + fold : at + units, :] = both[:, lanes:]


def combine_body(slot_ref, gate_ref, back_ref, tok_ref, hidden_ref, down_ref, out_ref, scored_ref):
    experts, half, lanes = back_ref.shape
    rows = tok_ref.shape[1]
    cap = lanes // 2
    place = iota((lanes, rows), 0)
    place = jnp.where(place < cap, place, place - cap)
    low = iota((lanes, rows), 0) < cap
    routed = jnp.zeros((half, 2 * rows), F32)
    for e in range(experts):
        mix = jnp.where(slot_ref[e : e + 1, :] == place, gate_ref[e : e + 1, :], 0.0)
        mix = jnp.concatenate([jnp.where(low, mix, 0.0), jnp.where(low, 0.0, mix)], axis=1)
        head = mix.astype(BF16)
        tail = (mix - head.astype(F32)).astype(BF16)
        routed = routed + nn(back_ref[e], head) + nn(back_ref[e], tail)
    depth = down_ref.shape[1] // hidden_ref.shape[0]
    skip = hidden_ref.shape[1] - depth
    shared = jnp.zeros((2 * half, rows), F32)
    for x in range(hidden_ref.shape[0]):
        shared = shared + nn(down_ref[:, x * depth : (x + 1) * depth], hidden_ref[x, skip:, :])
    routed = jnp.concatenate([routed[:, :rows], routed[:, rows:]], axis=0)
    out = (tok_ref[...].astype(F32) + shared + routed).astype(BF16)
    out_ref[...] = out
    take = iota((2 * SCORE_E, rows), 1) == rows - SCORE_E + iota((2 * SCORE_E, rows), 0)
    scored = nt(jnp.where(take, 1.0, 0.0).astype(BF16), out).astype(BF16)
    for g in range(scored_ref.shape[0]):
        scored_ref[g] = scored[:SCORE_E]


def pack_body(core_ref, rows_ref, out_ref):
    count, width = rows_ref.shape[0] // 2, rows_ref.shape[1]
    part = out_ref.shape[1]
    eye = jnp.where(iota((count, count), 0) == iota((count, count), 1), 1.0, 0.0).astype(BF16)
    mine = rows_ref[pl.ds(pl.multiple_of(core_ref[0] * count, count), count), :]
    flip = lax.dot_general(mine, eye, (((0,), (0,)), ((), ())), preferred_element_type=F32)
    packed = jnp.concatenate([flip[n : n + part] for n in range(0, width, part)], axis=1).astype(BF16)
    for n in range(out_ref.shape[0]):
        out_ref[n] = packed


def score_body(at_ref, rows_ref, vocab_ref, other_ref, targets_ref, out_ref, flat_ref):
    blocks, part, lanes = rows_ref.shape
    parts = flat_ref.shape[0] // (blocks * part)
    count = lanes // parts
    for b in range(blocks):
        block = rows_ref[b].astype(F32)
        for n in range(parts):
            at = (b * parts + n) * part
            turned = block if n == 0 else pltpu.roll(block, lanes - n * count, 1)
            flat_ref[at : at + part, :] = turned.astype(BF16)
    target = targets_ref[pl.ds(at_ref[0], 1), :]
    sums = jnp.zeros((1, lanes), F32)
    hits = jnp.zeros((1, lanes), F32)
    for n, block in enumerate((vocab_ref, other_ref)):
        logits = nn(block[...], flat_ref[...])
        entry = iota(logits.shape, 0) + at_ref[1 + n]
        sums = sums + jnp.sum(jnp.exp(logits), axis=0, keepdims=True)
        hits = hits + jnp.sum(jnp.where(entry == target, logits, 0.0), axis=0, keepdims=True)
    lane = iota(sums.shape, 1)
    out_ref[...] = jnp.broadcast_to(jnp.where(lane < count, sums, pltpu.roll(hits, count, 1)), out_ref.shape)


SHIFTS = (0, 1, 3, 2)
RING = (0, 7, 1, 6, 2, 5, 3, 4)


def exchange(value, axes):
    return lax.all_to_all(value, axes, 0, 0, tiled=True)


def spread_all(value, axes, count):
    return lax.all_to_all(
        jnp.broadcast_to(value[None], (count, *value.shape)), axes, 0, 0, tiled=True
    )


def from_shift(value, axis, shift):
    count = lax.axis_size(axis)
    return lax.ppermute(value, axis, [((i + shift) % count, i) for i in range(count)])


def around(value, axis, between):
    count = lax.axis_size(axis)
    left = right = value
    got = [value]
    for hop in range(3):
        if hop:
            left, right = between(hop, left, right)
        left = from_shift(left, axis, count - 1)
        right = from_shift(right, axis, 1)
        got += [left, right]
    left, right = between(3, left, right)
    return [*got, from_shift(left, axis, count - 1)]


def shards(tokens, routes, gates, w_gate, w_up, w_down, shared_gate, shared_up, shared_down, vocab, targets):
    nx, ny = lax.axis_size("x"), lax.axis_size("y")
    nz, nc = lax.axis_size("z"), lax.axis_size("core")
    groups, lanes = nz * nc, nx * ny
    rows, width = tokens.shape
    half, cap = width // 2, rows // 2
    near = groups // nx
    units = w_gate.shape[1]
    tok = tokens.T
    x_at = lax.axis_index("x").astype(jnp.int32).reshape(1)
    y_at = lax.axis_index("y").astype(jnp.int32).reshape(1)

    outgoing, slot, gate = call(
        dispatch_body,
        [
            shape((groups, half, 2 * cap)),
            shape((groups, rows), jnp.int32),
            shape((groups, rows), F32),
        ],
        [routes.T, gates.T, tok],
        far=range(3),
        scratch=[
            pltpu.VMEM(routes.T.shape, jnp.int32),
            pltpu.VMEM(gates.T.shape, F32),
            pltpu.VMEM(tok.shape, BF16),
            pltpu.SemaphoreType.DMA((3,)),
        ],
        limit=60,
    )
    arrived = exchange(outgoing, LINE)
    plane_tok = lax.all_gather(tok, PLANE, axis=0, tiled=True)
    (stacked,) = call(
        stack_body,
        [shape((2 * units, lanes * width))],
        [w_gate[0], w_up[0]],
        far=range(2),
        scratch=[pltpu.SemaphoreType.DMA((2,))],
        out_space=pltpu.HBM,
    )
    arrived, stacked = lax.optimization_barrier((arrived, stacked))
    quarter = exchange(arrived.reshape(nx, near * half, 2 * cap), "x")
    (spread,) = call(spread_body, [shape((nx * width, near * cap))], [quarter])
    own_down = w_down[0].T
    d1, d3 = from_shift(own_down, "x", 1), from_shift(own_down, "x", nx - 1)
    spread, stacked, d1, d3 = lax.optimization_barrier((spread, stacked, d1, d3))
    after = {"own": stacked}
    after["g1"] = from_shift(stacked, "x", 1)
    after["g3"] = from_shift(stacked, "x", nx - 1)

    def tie(left, right, *names):
        left, right, *due = lax.optimization_barrier((left, right, *[after[n] for n in names]))
        after.update(zip(names, due))
        return left, right

    def between(hop, left, right):
        if hop == 2:
            left, right = tie(left, right, "g1", "g3")
            after["g2"] = from_shift(after["g1"], "x", 1)
        return left, right

    blocks = around(spread, "y", between)
    near_weights = [after[n] for n in ("own", "g1", "g3", "g2")]
    (hidden,) = call(
        hidden_body,
        [shape((ny, nx * units + units // 2 + 8, near * cap))],
        [y_at, *blocks, *near_weights, shared_gate, shared_up, plane_tok],
        scalars=1,
        far=range(1, len(RING) + nx + 4),
        scratch=[
            pltpu.VMEM((lanes * width, near * cap), BF16),
            pltpu.VMEM((2 * (nx + 1) * units, lanes * width), BF16),
            pltpu.VMEM((lanes * width, rows), BF16),
            pltpu.SemaphoreType.DMA((3 + 2 * nx + lanes,)),
        ],
        limit=56,
    )
    hidden, d3 = lax.optimization_barrier((hidden, d3))
    d2 = from_shift(d3, "x", nx - 1)
    all_hidden = exchange(hidden, "y")
    (returned,) = call(
        down_body,
        [shape((nx, near * half + ny * units, 2 * cap))],
        [x_at, all_hidden, own_down, d1, d3, d2],
        scalars=1,
        far=range(2, 2 + nx),
        scratch=[
            pltpu.VMEM((lanes * units, near * cap), BF16),
            pltpu.VMEM((nx * width, lanes * units), BF16),
            pltpu.SemaphoreType.DMA((nx,)),
        ],
        limit=40,
    )
    mixed = lax.all_to_all(returned, "x", 0, 0, tiled=True)
    back = mixed[:, : near * half].reshape(groups, half, 2 * cap)
    back = lax.all_to_all(back, LINE, 0, 0, tiled=True)
    layer_out, scored = call(
        combine_body,
        [shape((width, rows)), shape((groups, SCORE_E, width))],
        [slot, gate, back, tok, mixed, shared_down.T],
    )
    line_rows = exchange(scored, LINE).reshape(groups * SCORE_E, width)
    count = groups * SCORE_E // nc
    core = lax.axis_index("core").astype(jnp.int32)
    (packed,) = call(
        pack_body,
        [shape((lanes, width * count // (2 * cap), 2 * cap))],
        [core.reshape(1), line_rows],
        scalars=1,
    )
    every = exchange(packed, PLANE)
    other_vocab = lax.ppermute(vocab, "core", [(0, 1), (1, 0)])
    place = lax.axis_index("x") * ny + lax.axis_index("y")
    first = [
        (((lax.axis_index("z") * nc + c) * lanes + place) * vocab.shape[0]).astype(jnp.int32)
        for c in (core, 1 - core)
    ]
    (sums,) = call(
        score_body,
        [shape((8, 2 * cap), F32)],
        [
            jnp.stack([core, *first]),
            every,
            vocab,
            other_vocab,
            jnp.tile(targets.reshape(nc, count), (1, 2 * cap // count)),
        ],
        scalars=1,
        scratch=[pltpu.VMEM((lanes * width, 2 * cap), BF16)],
    )
    sums = jnp.sum(spread_all(sums[:1], PLANE, lanes), axis=0)
    sums = jnp.sum(spread_all(sums, LINE, groups).reshape(nz, nc, 2 * cap), axis=0)
    return layer_out.T, (sums[:, count : 2 * count] - jnp.log(sums[:, :count])).reshape(-1)


def solution(mesh):
    mesh = Mesh(mesh.devices.reshape(8, 2, 4, 8), ("z", "core", "x", "y"))
    placed = (
        P(LINE, PLANE),
        P(LINE, None),
        P(LINE, None),
        P(LINE, PLANE, None),
        P(LINE, PLANE, None),
        P(LINE, None, PLANE),
        P(PLANE, None),
        P(PLANE, None),
        P(None, PLANE),
        P((*LINE, *PLANE), None),
        P(),
    )
    return jax.shard_map(
        shards, mesh=mesh, in_specs=placed, out_specs=(P(LINE, PLANE), P()), check_vma=False
    )
```

```python
import jax
import jax.numpy as jnp
from jax import lax
from jax.experimental import pallas as pl
from jax.experimental.pallas import tpu as pltpu
from jax.sharding import Mesh
from jax.sharding import PartitionSpec as P

SCORE_E = 4
EIGHT = 8
F32 = jnp.float32
BF16 = jnp.bfloat16
LINE = ("z", "core")
PLANE = ("x", "y")
BOTH = ("z", "core", "x")


def call(body, outs, args, scalars=0, far=(), scratch=(), limit=16):
    specs = [
        pl.BlockSpec(memory_space=pltpu.SMEM if n < scalars else pltpu.HBM if n in far else pltpu.VMEM)
        for n in range(len(args))
    ]
    moved = sum(a.size * a.dtype.itemsize for a in args)
    moved += sum(o.size * o.dtype.itemsize for o in outs)
    return pl.pallas_call(
        body,
        out_shape=outs,
        in_specs=specs,
        out_specs=[pl.BlockSpec(memory_space=pltpu.VMEM) for _ in outs],
        scratch_shapes=list(scratch),
        cost_estimate=pl.CostEstimate(flops=0, bytes_accessed=moved, transcendentals=0),
        compiler_params=pltpu.CompilerParams(vmem_limit_bytes=limit << 20),
    )(*args)


def fetch(pairs, sems):
    copies = [pltpu.make_async_copy(src, dst, sems.at[n]) for n, (src, dst) in enumerate(pairs)]
    for copy in copies:
        copy.start()
    return copies


def shape(dims, dtype=BF16):
    return jax.ShapeDtypeStruct(dims, dtype)


def nn(a, b):
    return lax.dot_general(a, b, (((1,), (0,)), ((), ())), preferred_element_type=F32)


def nt(a, b):
    return lax.dot_general(a, b, (((1,), (1,)), ((), ())), preferred_element_type=F32)


def iota(dims, axis):
    return lax.broadcasted_iota(jnp.int32, dims, axis)


class Fold:
    def __init__(self, width, lanes, near):
        self.width, self.lanes, self.near = width, lanes, near
        self.rest = width - lanes
        self.parts = lanes // self.rest
        self.per = near // self.parts
        self.lines = near + EIGHT

    def to_lines(self, rows, axis):
        dims = (rows // self.near * EIGHT, rows)
        dims = dims if axis == 0 else dims[::-1]
        line, row = iota(dims, axis), iota(dims, 1 - axis)
        same = lax.div(line, EIGHT) == lax.div(row, self.near)
        hit = same & (lax.rem(line, EIGHT) == lax.rem(row, self.per))
        return hit

    def part_of(self, row):
        return lax.div(lax.rem(row, self.near), self.per)


def bf(mask):
    return jnp.where(mask, 1.0, 0.0).astype(BF16)


def tn(a, b):
    return lax.dot_general(a, b, (((0,), (0,)), ((), ())), preferred_element_type=F32)


def routing(routes_ref, gates_ref, experts):
    top, rows = routes_ref.shape
    expert = iota((experts, rows), 0)
    named = jnp.zeros((experts, rows), F32)
    gate = jnp.zeros((experts, rows), F32)
    for k in range(top):
        hit = expert == routes_ref[k : k + 1, :]
        named = named + jnp.where(hit, 1.0, 0.0)
        gate = gate + jnp.where(hit, gates_ref[k : k + 1, :], 0.0)
    before = jnp.where(iota((rows, rows), 0) < iota((rows, rows), 1), 1.0, 0.0).astype(BF16)
    earlier = nn(named.astype(BF16), before)
    return jnp.where(named > 0.0, earlier, -1.0).astype(jnp.int32), gate


def dispatch_body(routes_far, gates_far, tok_far, out_ref, slot_ref, gate_ref, routes_ref, gates_ref, tok_ref, sems):
    pairs = [(routes_far, routes_ref), (gates_far, gates_ref), (tok_far, tok_ref)]
    for copy in fetch(pairs, sems):
        copy.wait()
    experts = slot_ref.shape[0]
    width, rows = tok_ref.shape
    lanes = out_ref.shape[2]
    near = out_ref.shape[1] - EIGHT
    fold = Fold(width, lanes, near)
    cap = out_ref.shape[0] // experts * near
    slot, gate = routing(routes_ref, gates_ref, experts)
    slot_ref[...] = slot
    gate_ref[...] = gate
    tok = tok_ref[...]
    tok = jnp.concatenate([tok[:lanes]] + [tok[lanes:]] * fold.parts, axis=0)
    place = iota((cap, rows), 0)
    several = 2 * lanes // cap
    lines = bf(fold.to_lines(several * cap, 0))
    dims = (several * cap, lanes)
    own_part = fold.part_of(iota(dims, 0)) == lax.div(iota(dims, 1), fold.rest)
    for first in range(0, experts, several):
        sel = jnp.concatenate([bf(slot[e : e + 1, :] == place) for e in range(first, first + several)], axis=0)
        out = nt(sel, tok)
        rest = nn(lines, jnp.where(own_part, out[:, lanes:], 0.0).astype(BF16))
        for n in range(several * cap // near):
            piece = first * cap // near + n
            out_ref[piece, :near, :] = out[n * near : (n + 1) * near, :lanes].astype(BF16)
            out_ref[piece, near:, :] = rest[n * EIGHT : (n + 1) * EIGHT, :].astype(BF16)


def spread_body(x_ref, in_ref, *refs):
    *tokens, out_ref = refs
    nx = len(tokens)
    width, rows = tokens[0].shape
    lanes = in_ref.shape[2]
    near = in_ref.shape[1] - EIGHT
    groups = in_ref.shape[0] // nx
    fold = Fold(width, lanes, near)
    count = groups * near
    eye = bf(iota((count, count), 0) == iota((count, count), 1))
    lines = fold.to_lines(count, 0)
    part = fold.part_of(iota(lines.shape, 1))
    takes = [bf(lines & (part == q)) for q in range(fold.parts)]
    for x in range(nx):
        full = jnp.concatenate([in_ref[g * nx + x, :near, :] for g in range(groups)], axis=0)
        rest = jnp.concatenate([in_ref[g * nx + x, near:, :].astype(F32) for g in range(groups)], axis=0).astype(BF16)
        out_ref[x * width : x * width + lanes, :count] = tn(full, eye).astype(BF16)
        tail = jnp.zeros((fold.rest, count), F32)
        for q, take in enumerate(takes):
            tail = tail + tn(rest, take)[q * fold.rest : (q + 1) * fold.rest]
        out_ref[x * width + lanes : (x + 1) * width, :count] = tail.astype(BF16)
    for tok, shift in zip(tokens, SHIFTS):
        at = pl.multiple_of(lax.rem(x_ref[0] + shift, nx) * width, width)
        out_ref[pl.ds(at, width), count:] = tok[...]


def glu(gate, up):
    return (gate / (1.0 + jnp.exp(-gate)) * up).astype(BF16)


def hidden_body(y_ref, *refs):
    blocks = refs[: len(RING)]
    out_ref, flat_ref, weight_ref, sems = refs[-4:]
    weights = refs[len(RING) : -4]
    nx = len(weights) // 2 - 1
    units = weights[0].shape[0]
    width = blocks[0].shape[0] // nx
    ny = flat_ref.shape[0] // (nx * width)
    top = nx * units
    pairs = []
    for n, weight in enumerate(weights):
        at = n // 2 * units + (n % 2) * top if n < 2 * nx else n * units
        pairs.append((weight, weight_ref.at[at : at + units, :]))
    for block, shift in zip(blocks, RING):
        y = lax.rem(y_ref[0] + shift, ny)
        for n in range(nx):
            at = pl.multiple_of((n * ny + y) * width, width)
            pairs.append((block.at[n * width : (n + 1) * width, :], flat_ref.at[pl.ds(at, width), :]))
    for copy in fetch(pairs, sems):
        copy.wait()
    cols = out_ref.shape[2]
    both = nn(weight_ref[: 2 * top, :], flat_ref[:, :cols])
    routed = glu(both[:top], both[top:])
    both = nn(weight_ref[2 * top :, :], flat_ref[:, cols:])
    own = glu(both[:units], both[units:])
    fold = units // 2
    folded = jnp.concatenate([own[:fold], own[fold:]], axis=1)
    for y in range(ny):
        out_ref[y, :top, :] = routed
        out_ref[y, top : top + fold, :] = folded


def down_body(x_ref, hidden_ref, *refs):
    *weights, out_ref, shared_ref, flat_ref, down_ref, sems = refs
    nx = len(weights)
    width = weights[0].shape[0]
    lanes = out_ref.shape[2]
    near = out_ref.shape[1] - EIGHT
    fold = Fold(width, lanes, near)
    pairs = []
    for n, weight in enumerate(weights):
        pairs.append((weight.at[:lanes, :], down_ref.at[n, :lanes, :]))
        for q in range(fold.parts):
            at = lanes + q * fold.rest
            pairs.append((weight.at[lanes:, :], down_ref.at[n, at : at + fold.rest, :]))
    copies = fetch(pairs, sems)
    ny = hidden_ref.shape[0]
    units = flat_ref.shape[0] // (nx * ny)
    count = flat_ref.shape[1]
    own = [lax.rem(x_ref[0] + shift, nx) for shift in SHIFTS]
    half = units // 2
    for y in range(ny):
        for n in range(nx):
            at = pl.multiple_of((own[n] * ny + y) * units, units)
            flat_ref[pl.ds(at, units), :] = hidden_ref[y, n * units : (n + 1) * units, :]
        both = hidden_ref[y, nx * units : nx * units + half, :]
        shared_ref[y * units : y * units + half, :] = both[:, :lanes]
        shared_ref[y * units + half : (y + 1) * units, :] = both[:, lanes:]
    eye = bf(iota((count, count), 0) == iota((count, count), 1))
    lines = bf(fold.to_lines(count, 0))
    dims = (lanes, count)
    own_part = lax.div(iota(dims, 0), fold.rest) == fold.part_of(iota(dims, 1))
    for copy in copies:
        copy.wait()
    for n in range(nx):
        out = nn(down_ref[n], flat_ref[...])
        full = nt(eye, out[:lanes].astype(BF16)).astype(BF16)
        rest = nt(lines, jnp.where(own_part, out[lanes:], 0.0).astype(BF16))
        for g in range(count // near):
            out_ref[g * nx + own[n], :near, :] = full[g * near : (g + 1) * near, :]
            out_ref[g * nx + own[n], near:, :] = rest[g * EIGHT : (g + 1) * EIGHT, :].astype(BF16)


def combine_body(x_ref, slot_ref, gate_ref, back_ref, tok_ref, down_ref, *refs):
    *hidden, out_ref, scored_ref = refs
    experts, rows = slot_ref.shape
    width = tok_ref.shape[0]
    lanes = back_ref.shape[2]
    near = back_ref.shape[1] - EIGHT
    fold = Fold(width, lanes, near)
    pieces = back_ref.shape[0] // experts
    cap = pieces * near
    several = 2 * lanes // cap

    def mix(first, target):
        weigh = [
            jnp.where(slot_ref[e : e + 1, :] == target, gate_ref[e : e + 1, :], 0.0)
            for e in range(first, first + several)
        ]
        weigh = jnp.concatenate(weigh, axis=0)
        head = weigh.astype(BF16)
        return [head, (weigh - head.astype(F32)).astype(BF16)]

    place = iota((cap, rows), 0)
    line = iota((pieces * EIGHT, rows), 0)
    line, piece = lax.rem(line, EIGHT), lax.div(line, EIGHT)
    full = jnp.zeros((lanes, rows), F32)
    rest = jnp.zeros((fold.rest, rows), F32)
    for first in range(0, experts, several):
        span = range(first * pieces, (first + several) * pieces)
        block = jnp.concatenate([back_ref[n, :near, :] for n in span], axis=0)
        got = tn(block, jnp.concatenate(mix(first, place), axis=1))
        full = full + got[:, :rows] + got[:, rows:]
        block = jnp.concatenate([back_ref[n, near:, :].astype(F32) for n in span], axis=0).astype(BF16)
        terms = []
        for q in range(fold.parts):
            target = jnp.where(line < fold.per, piece * near + q * fold.per + line, -2)
            terms += mix(first, target)
        got = tn(block, jnp.concatenate(terms, axis=1))
        for q in range(fold.parts):
            part = got[q * fold.rest : (q + 1) * fold.rest]
            rest = rest + part[:, 2 * q * rows : (2 * q + 1) * rows] + part[:, (2 * q + 1) * rows : (2 * q + 2) * rows]
    routed = jnp.concatenate([full, rest], axis=0)
    shared = jnp.zeros((width, rows), F32)
    for shift, units in zip(SHIFTS, hidden):
        depth = units.shape[0]
        at = pl.multiple_of(lax.rem(x_ref[0] + shift, len(hidden)) * depth, lanes)
        shared = shared + nn(down_ref[:, pl.ds(at, depth)], units[...])
    out = (tok_ref[...].astype(F32) + shared + routed).astype(BF16)
    out_ref[...] = out
    take = iota((EIGHT, rows), 1) == rows - SCORE_E + iota((EIGHT, rows), 0)
    scored = nt(bf(take), out).astype(BF16)
    for g in range(scored_ref.shape[0]):
        scored_ref[g] = scored[:SCORE_E]


def pack_body(core_ref, rows_ref, out_ref):
    count, width = rows_ref.shape[0] // 2, rows_ref.shape[1]
    part = out_ref.shape[1]
    eye = jnp.where(iota((count, count), 0) == iota((count, count), 1), 1.0, 0.0).astype(BF16)
    mine = rows_ref[pl.ds(pl.multiple_of(core_ref[0] * count, count), count), :]
    flip = lax.dot_general(mine, eye, (((0,), (0,)), ((), ())), preferred_element_type=F32)
    packed = jnp.concatenate([flip[n : n + part] for n in range(0, width, part)], axis=1).astype(BF16)
    for n in range(out_ref.shape[0]):
        out_ref[n] = packed


def score_body(at_ref, rows_ref, vocab_ref, other_ref, targets_ref, out_ref, flat_ref):
    blocks, part, lanes = rows_ref.shape
    parts = flat_ref.shape[0] // (blocks * part)
    count = lanes // parts
    for b in range(blocks):
        block = rows_ref[b].astype(F32)
        for n in range(parts):
            at = (b * parts + n) * part
            turned = block if n == 0 else pltpu.roll(block, lanes - n * count, 1)
            flat_ref[at : at + part, :] = turned.astype(BF16)
    target = targets_ref[pl.ds(at_ref[0], 1), :]
    sums = jnp.zeros((1, lanes), F32)
    hits = jnp.zeros((1, lanes), F32)
    for n, block in enumerate((vocab_ref, other_ref)):
        logits = nn(block[...], flat_ref[...])
        entry = iota(logits.shape, 0) + at_ref[1 + n]
        sums = sums + jnp.sum(jnp.exp(logits), axis=0, keepdims=True)
        hits = hits + jnp.sum(jnp.where(entry == target, logits, 0.0), axis=0, keepdims=True)
    lane = iota(sums.shape, 1)
    out_ref[...] = jnp.broadcast_to(jnp.where(lane < count, sums, pltpu.roll(hits, count, 1)), out_ref.shape)


SHIFTS = (0, 1, 3, 2)
RING = (0, 7, 1, 6, 2, 5, 3, 4)


def exchange(value, axes):
    return lax.all_to_all(value, axes, 0, 0, tiled=True)


def spread_all(value, axes, count):
    return lax.all_to_all(
        jnp.broadcast_to(value[None], (count, *value.shape)), axes, 0, 0, tiled=True
    )


def from_shift(value, axis, shift):
    count = lax.axis_size(axis)
    return lax.ppermute(value, axis, [((i + shift) % count, i) for i in range(count)])


def around(value, axis, between):
    count = lax.axis_size(axis)
    left = right = value
    got = [value]
    for hop in range(3):
        if hop:
            left, right = between(hop, left, right)
        left = from_shift(left, axis, count - 1)
        right = from_shift(right, axis, 1)
        got += [left, right]
    left, right = between(3, left, right)
    return [*got, from_shift(left, axis, count - 1)]


def shards(tokens, routes, gates, w_gate, w_up, w_down, shared_gate, shared_up, shared_down, vocab, targets):
    nx, ny = lax.axis_size("x"), lax.axis_size("y")
    nz, nc = lax.axis_size("z"), lax.axis_size("core")
    groups, lanes = nz * nc, nx * ny
    rows, width = tokens.shape
    cap = rows // 2
    near = cap // nx
    count = groups * near
    lines = near + EIGHT
    units = w_gate.shape[1]
    tok = tokens.T
    x_at = lax.axis_index("x").astype(jnp.int32).reshape(1)
    y_at = lax.axis_index("y").astype(jnp.int32).reshape(1)

    outgoing, slot, gate = call(
        dispatch_body,
        [
            shape((groups * nx, lines, rows)),
            shape((groups, rows), jnp.int32),
            shape((groups, rows), F32),
        ],
        [routes.T, gates.T, tok],
        far=range(3),
        scratch=[
            pltpu.VMEM(routes.T.shape, jnp.int32),
            pltpu.VMEM(gates.T.shape, F32),
            pltpu.VMEM(tok.shape, BF16),
            pltpu.SemaphoreType.DMA((3,)),
        ],
        limit=60,
    )
    arrived = exchange(outgoing, BOTH)
    arrived, t1, t3, t2 = lax.optimization_barrier((arrived, *[from_shift(tok, "x", shift) for shift in SHIFTS[1:]]))
    (spread,) = call(
        spread_body,
        [shape((nx * width, count + rows))],
        [x_at, arrived, tok, t1, t3, t2],
        scalars=1,
    )
    spread, own_gate, own_up = lax.optimization_barrier((spread, w_gate[0], w_up[0]))
    after = {"own_gate": own_gate, "own_up": own_up, "down": w_down[0].T}
    after["g1"] = from_shift(own_gate, "x", 1)
    after["u3"] = from_shift(own_up, "x", nx - 1)

    def tie(left, right, *names):
        left, right, *due = lax.optimization_barrier((left, right, *[after[n] for n in names]))
        after.update(zip(names, due))
        return left, right

    def between(hop, left, right):
        if hop == 1:
            left, right = tie(left, right, "own_gate", "own_up")
            after["g3"] = from_shift(after["own_gate"], "x", nx - 1)
            after["u1"] = from_shift(after["own_up"], "x", 1)
        if hop == 2:
            left, right = tie(left, right, "g1", "u3")
            after["g2"] = from_shift(after["g1"], "x", 1)
            after["u2"] = from_shift(after["u3"], "x", nx - 1)
        if hop == 3:
            left, right = tie(left, right, "g3", "u1", "down")
            after["d1"] = from_shift(after["down"], "x", 1)
            after["d3"] = from_shift(after["down"], "x", nx - 1)
        return left, right

    blocks = around(spread, "y", between)
    near_weights = [after[n] for n in ("own_gate", "own_up", "g1", "u1", "g3", "u3", "g2", "u2")]
    (hidden,) = call(
        hidden_body,
        [shape((ny, nx * units + units // 2 + EIGHT, count))],
        [y_at, *blocks, *near_weights, shared_gate, shared_up],
        scalars=1,
        far=(*range(1, len(RING)), *range(len(RING) + 1, len(RING) + 2 * nx + 3)),
        scratch=[
            pltpu.VMEM((lanes * width, count + rows), BF16),
            pltpu.VMEM((2 * (nx + 1) * units, lanes * width), BF16),
            pltpu.SemaphoreType.DMA((2 * nx + 2 + lanes,)),
        ],
        limit=56,
    )
    hidden, d1, d3 = lax.optimization_barrier((hidden, after["d1"], after["d3"]))
    d2 = from_shift(d3, "x", nx - 1)
    all_hidden = exchange(hidden, "y")
    returned, own_shared = call(
        down_body,
        [shape((groups * nx, lines, rows)), shape((ny * units, rows))],
        [x_at, all_hidden, after["down"], d1, d3, d2],
        scalars=1,
        far=range(2, 2 + nx),
        scratch=[
            pltpu.VMEM((lanes * units, count), BF16),
            pltpu.VMEM((nx, 2 * rows, lanes * units), BF16),
            pltpu.SemaphoreType.DMA((nx * (1 + rows // (width - rows)),)),
        ],
        limit=40,
    )
    near_shared = [own_shared, *[from_shift(own_shared, "x", shift) for shift in SHIFTS[1:]]]
    back = exchange(returned, BOTH)
    layer_out, scored = call(
        combine_body,
        [shape((width, rows)), shape((groups, SCORE_E, width))],
        [x_at, slot, gate, back, tok, shared_down.T, *near_shared],
        scalars=1,
    )
    line_rows = exchange(scored, LINE).reshape(groups * SCORE_E, width)
    count = groups * SCORE_E // nc
    core = lax.axis_index("core").astype(jnp.int32)
    (packed,) = call(
        pack_body,
        [shape((lanes, width * count // (2 * cap), 2 * cap))],
        [core.reshape(1), line_rows],
        scalars=1,
    )
    every = exchange(packed, PLANE)
    other_vocab = lax.ppermute(vocab, "core", [(0, 1), (1, 0)])
    place = lax.axis_index("x") * ny + lax.axis_index("y")
    first = [
        (((lax.axis_index("z") * nc + c) * lanes + place) * vocab.shape[0]).astype(jnp.int32)
        for c in (core, 1 - core)
    ]
    (sums,) = call(
        score_body,
        [shape((8, 2 * cap), F32)],
        [
            jnp.stack([core, *first]),
            every,
            vocab,
            other_vocab,
            jnp.tile(targets.reshape(nc, count), (1, 2 * cap // count)),
        ],
        scalars=1,
        scratch=[pltpu.VMEM((lanes * width, 2 * cap), BF16)],
    )
    sums = jnp.sum(spread_all(sums[:1], PLANE, lanes), axis=0)
    sums = jnp.sum(spread_all(sums, LINE, groups).reshape(nz, nc, 2 * cap), axis=0)
    return layer_out.T, (sums[:, count : 2 * count] - jnp.log(sums[:, :count])).reshape(-1)


def solution(mesh):
    mesh = Mesh(mesh.devices.reshape(8, 2, 4, 8), ("z", "core", "x", "y"))
    placed = (
        P(LINE, PLANE),
        P(LINE, None),
        P(LINE, None),
        P(LINE, PLANE, None),
        P(LINE, PLANE, None),
        P(LINE, None, PLANE),
        P(PLANE, None),
        P(PLANE, None),
        P(None, PLANE),
        P((*LINE, *PLANE), None),
        P(),
    )
    return jax.shard_map(
        shards, mesh=mesh, in_specs=placed, out_specs=(P(LINE, PLANE), P()), check_vma=False
    )
```

```python
import jax
import jax.numpy as jnp
from jax import lax
from jax.experimental import pallas as pl
from jax.experimental.pallas import tpu as pltpu
from jax.sharding import Mesh
from jax.sharding import PartitionSpec as P

SCORE_E = 4
EIGHT = 8
F32 = jnp.float32
BF16 = jnp.bfloat16
LINE = ("z", "core")
PLANE = ("x", "y")
BOTH = ("z", "core", "x")


def call(body, outs, args, scalars=0, far=(), scratch=(), limit=16):
    specs = [
        pl.BlockSpec(memory_space=pltpu.SMEM if n < scalars else pltpu.HBM if n in far else pltpu.VMEM)
        for n in range(len(args))
    ]
    moved = sum(a.size * a.dtype.itemsize for a in args)
    moved += sum(o.size * o.dtype.itemsize for o in outs)
    return pl.pallas_call(
        body,
        out_shape=outs,
        in_specs=specs,
        out_specs=[pl.BlockSpec(memory_space=pltpu.VMEM) for _ in outs],
        scratch_shapes=list(scratch),
        cost_estimate=pl.CostEstimate(flops=0, bytes_accessed=moved, transcendentals=0),
        compiler_params=pltpu.CompilerParams(vmem_limit_bytes=limit << 20),
    )(*args)


def fetch(pairs, sems):
    copies = [pltpu.make_async_copy(src, dst, sems.at[n]) for n, (src, dst) in enumerate(pairs)]
    for copy in copies:
        copy.start()
    return copies


def shape(dims, dtype=BF16):
    return jax.ShapeDtypeStruct(dims, dtype)


def nn(a, b):
    return lax.dot_general(a, b, (((1,), (0,)), ((), ())), preferred_element_type=F32)


def nt(a, b):
    return lax.dot_general(a, b, (((1,), (1,)), ((), ())), preferred_element_type=F32)


def iota(dims, axis):
    return lax.broadcasted_iota(jnp.int32, dims, axis)


class Fold:
    def __init__(self, width, lanes, near):
        self.width, self.lanes, self.near = width, lanes, near
        self.rest = width - lanes
        self.parts = lanes // self.rest
        self.per = near // self.parts
        self.lines = near + EIGHT

    def to_lines(self, rows, axis):
        dims = (rows // self.near * EIGHT, rows)
        dims = dims if axis == 0 else dims[::-1]
        line, row = iota(dims, axis), iota(dims, 1 - axis)
        same = lax.div(line, EIGHT) == lax.div(row, self.near)
        hit = same & (lax.rem(line, EIGHT) == lax.rem(row, self.per))
        return hit

    def part_of(self, row):
        return lax.div(lax.rem(row, self.near), self.per)


def bf(mask):
    return jnp.where(mask, 1.0, 0.0).astype(BF16)


def tn(a, b):
    return lax.dot_general(a, b, (((0,), (0,)), ((), ())), preferred_element_type=F32)


def routing(routes_ref, gates_ref, experts):
    top, rows = routes_ref.shape
    expert = iota((experts, rows), 0)
    named = jnp.zeros((experts, rows), F32)
    gate = jnp.zeros((experts, rows), F32)
    for k in range(top):
        hit = expert == routes_ref[k : k + 1, :]
        named = named + jnp.where(hit, 1.0, 0.0)
        gate = gate + jnp.where(hit, gates_ref[k : k + 1, :], 0.0)
    before = jnp.where(iota((rows, rows), 0) < iota((rows, rows), 1), 1.0, 0.0).astype(BF16)
    earlier = nn(named.astype(BF16), before)
    return jnp.where(named > 0.0, earlier, -1.0).astype(jnp.int32), gate


def dispatch_body(routes_far, gates_far, tok_far, out_ref, slot_ref, gate_ref, routes_ref, gates_ref, tok_ref, sems):
    pairs = [(routes_far, routes_ref), (gates_far, gates_ref), (tok_far, tok_ref)]
    for copy in fetch(pairs, sems):
        copy.wait()
    experts = slot_ref.shape[0]
    width, rows = tok_ref.shape
    lanes = out_ref.shape[2]
    near = out_ref.shape[1] - EIGHT
    fold = Fold(width, lanes, near)
    cap = out_ref.shape[0] // experts * near
    slot, gate = routing(routes_ref, gates_ref, experts)
    slot_ref[...] = slot
    gate_ref[...] = gate
    tok = tok_ref[...]
    tok = jnp.concatenate([tok[:lanes]] + [tok[lanes:]] * fold.parts, axis=0)
    place = iota((cap, rows), 0)
    several = 2 * lanes // cap
    lines = bf(fold.to_lines(several * cap, 0))
    dims = (several * cap, lanes)
    own_part = fold.part_of(iota(dims, 0)) == lax.div(iota(dims, 1), fold.rest)
    for first in range(0, experts, several):
        sel = jnp.concatenate([bf(slot[e : e + 1, :] == place) for e in range(first, first + several)], axis=0)
        out = nt(sel, tok)
        rest = nn(lines, jnp.where(own_part, out[:, lanes:], 0.0).astype(BF16))
        for n in range(several * cap // near):
            piece = first * cap // near + n
            out_ref[piece, :near, :] = out[n * near : (n + 1) * near, :lanes].astype(BF16)
            out_ref[piece, near:, :] = rest[n * EIGHT : (n + 1) * EIGHT, :].astype(BF16)


def spread_body(x_ref, in_ref, *refs):
    *tokens, out_ref = refs
    nx = len(tokens)
    width, rows = tokens[0].shape
    lanes = in_ref.shape[2]
    near = in_ref.shape[1] - EIGHT
    groups = in_ref.shape[0] // nx
    fold = Fold(width, lanes, near)
    count = groups * near
    eye = bf(iota((count, count), 0) == iota((count, count), 1))
    lines = fold.to_lines(count, 0)
    part = fold.part_of(iota(lines.shape, 1))
    takes = [bf(lines & (part == q)) for q in range(fold.parts)]
    for x in range(nx):
        full = jnp.concatenate([in_ref[g * nx + x, :near, :] for g in range(groups)], axis=0)
        rest = jnp.concatenate([in_ref[g * nx + x, near:, :].astype(F32) for g in range(groups)], axis=0).astype(BF16)
        out_ref[x * width : x * width + lanes, :count] = tn(full, eye).astype(BF16)
        tail = jnp.zeros((fold.rest, count), F32)
        for q, take in enumerate(takes):
            tail = tail + tn(rest, take)[q * fold.rest : (q + 1) * fold.rest]
        out_ref[x * width + lanes : (x + 1) * width, :count] = tail.astype(BF16)
    for tok, shift in zip(tokens, SHIFTS):
        at = pl.multiple_of(lax.rem(x_ref[0] + shift, nx) * width, width)
        out_ref[pl.ds(at, width), count:] = tok[...]


def glu(gate, up):
    return (gate / (1.0 + jnp.exp(-gate)) * up).astype(BF16)


def hidden_body(y_ref, *refs):
    blocks = refs[: len(RING)]
    out_ref, flat_ref, weight_ref, sems = refs[-4:]
    weights = refs[len(RING) : -4]
    nx = len(weights) // 2 - 1
    units = weights[0].shape[0]
    width = blocks[0].shape[0] // nx
    ny = flat_ref.shape[0] // (nx * width)
    top = nx * units
    pairs = []
    for n, weight in enumerate(weights):
        at = n // 2 * units + (n % 2) * top if n < 2 * nx else n * units
        pairs.append((weight, weight_ref.at[at : at + units, :]))
    for block, shift in zip(blocks, RING):
        y = lax.rem(y_ref[0] + shift, ny)
        for n in range(nx):
            at = pl.multiple_of((n * ny + y) * width, width)
            pairs.append((block.at[n * width : (n + 1) * width, :], flat_ref.at[pl.ds(at, width), :]))
    for copy in fetch(pairs, sems):
        copy.wait()
    cols = out_ref.shape[2]
    both = nn(weight_ref[: 2 * top, :], flat_ref[:, :cols])
    routed = glu(both[:top], both[top:])
    both = nn(weight_ref[2 * top :, :], flat_ref[:, cols:])
    own = glu(both[:units], both[units:])
    fold = units // 2
    folded = jnp.concatenate([own[:fold], own[fold:]], axis=1)
    for y in range(ny):
        out_ref[y, :top, :] = routed
        out_ref[y, top : top + fold, :] = folded


def down_body(x_ref, hidden_ref, *refs):
    *weights, out_ref, shared_ref, flat_ref, down_ref, sems = refs
    nx = len(weights)
    width = weights[0].shape[0]
    lanes = out_ref.shape[2]
    near = out_ref.shape[1] - EIGHT
    fold = Fold(width, lanes, near)
    pairs = []
    for n, weight in enumerate(weights):
        base = 2 * n * lanes
        pairs.append((weight.at[:lanes, :], down_ref.at[base : base + lanes, :]))
        for q in range(fold.parts):
            at = base + lanes + q * fold.rest
            pairs.append((weight.at[lanes:, :], down_ref.at[at : at + fold.rest, :]))
    copies = fetch(pairs, sems)
    ny = hidden_ref.shape[0]
    units = flat_ref.shape[0] // (nx * ny)
    count = flat_ref.shape[1]
    own = [lax.rem(x_ref[0] + shift, nx) for shift in SHIFTS]
    half = units // 2
    for y in range(ny):
        for n in range(nx):
            at = pl.multiple_of((own[n] * ny + y) * units, units)
            flat_ref[pl.ds(at, units), :] = hidden_ref[y, n * units : (n + 1) * units, :]
        both = hidden_ref[y, nx * units : nx * units + half, :]
        shared_ref[y * units : y * units + half, :] = both[:, :lanes]
        shared_ref[y * units + half : (y + 1) * units, :] = both[:, lanes:]
    eye = bf(iota((count, count), 0) == iota((count, count), 1))
    lines = bf(fold.to_lines(count, 0))
    dims = (lanes, count)
    own_part = lax.div(iota(dims, 0), fold.rest) == fold.part_of(iota(dims, 1))
    for copy in copies:
        copy.wait()
    outs = nn(down_ref[...], flat_ref[...])
    for n in range(nx):
        out = outs[2 * n * lanes : 2 * (n + 1) * lanes]
        full = nt(eye, out[:lanes].astype(BF16)).astype(BF16)
        rest = nt(lines, jnp.where(own_part, out[lanes:], 0.0).astype(BF16))
        for g in range(count // near):
            out_ref[g * nx + own[n], :near, :] = full[g * near : (g + 1) * near, :]
            out_ref[g * nx + own[n], near:, :] = rest[g * EIGHT : (g + 1) * EIGHT, :].astype(BF16)


def combine_body(x_ref, down_far, slot_ref, gate_ref, back_ref, tok_ref, *refs):
    *hidden, out_ref, scored_ref, down_ref, sems = refs
    copies = fetch([(down_far, down_ref)], sems)
    experts, rows = slot_ref.shape
    width = tok_ref.shape[0]
    lanes = back_ref.shape[2]
    near = back_ref.shape[1] - EIGHT
    fold = Fold(width, lanes, near)
    pieces = back_ref.shape[0] // experts
    cap = pieces * near
    several = 2 * lanes // cap

    def mix(first, target):
        weigh = [
            jnp.where(slot_ref[e : e + 1, :] == target, gate_ref[e : e + 1, :], 0.0)
            for e in range(first, first + several)
        ]
        weigh = jnp.concatenate(weigh, axis=0)
        head = weigh.astype(BF16)
        return [head, (weigh - head.astype(F32)).astype(BF16)]

    place = iota((cap, rows), 0)
    line = iota((pieces * EIGHT, rows), 0)
    line, piece = lax.rem(line, EIGHT), lax.div(line, EIGHT)
    full = jnp.zeros((lanes, rows), F32)
    rest = jnp.zeros((fold.rest, rows), F32)
    for first in range(0, experts, several):
        span = range(first * pieces, (first + several) * pieces)
        block = jnp.concatenate([back_ref[n, :near, :] for n in span], axis=0)
        got = tn(block, jnp.concatenate(mix(first, place), axis=1))
        full = full + got[:, :rows] + got[:, rows:]
        block = jnp.concatenate([back_ref[n, near:, :].astype(F32) for n in span], axis=0).astype(BF16)
        terms = []
        for q in range(fold.parts):
            target = jnp.where(line < fold.per, piece * near + q * fold.per + line, -2)
            terms += mix(first, target)
        got = tn(block, jnp.concatenate(terms, axis=1))
        for q in range(fold.parts):
            part = got[q * fold.rest : (q + 1) * fold.rest]
            rest = rest + part[:, 2 * q * rows : (2 * q + 1) * rows] + part[:, (2 * q + 1) * rows : (2 * q + 2) * rows]
    routed = jnp.concatenate([full, rest], axis=0)
    copies[0].wait()
    shared = jnp.zeros((width, rows), F32)
    for shift, units in zip(SHIFTS, hidden):
        depth = units.shape[0]
        at = pl.multiple_of(lax.rem(x_ref[0] + shift, len(hidden)) * depth, lanes)
        shared = shared + nn(down_ref[:, pl.ds(at, depth)], units[...])
    out = (tok_ref[...].astype(F32) + shared + routed).astype(BF16)
    out_ref[...] = out
    take = iota((EIGHT, rows), 1) == rows - SCORE_E + iota((EIGHT, rows), 0)
    scored = nt(bf(take), out).astype(BF16)
    for g in range(scored_ref.shape[0]):
        scored_ref[g] = scored[:SCORE_E]


def pack_body(core_ref, rows_ref, out_ref):
    count, width = rows_ref.shape[0] // 2, rows_ref.shape[1]
    part = out_ref.shape[1]
    eye = jnp.where(iota((count, count), 0) == iota((count, count), 1), 1.0, 0.0).astype(BF16)
    mine = rows_ref[pl.ds(pl.multiple_of(core_ref[0] * count, count), count), :]
    flip = lax.dot_general(mine, eye, (((0,), (0,)), ((), ())), preferred_element_type=F32)
    packed = jnp.concatenate([flip[n : n + part] for n in range(0, width, part)], axis=1).astype(BF16)
    for n in range(out_ref.shape[0]):
        out_ref[n] = packed


def score_body(at_ref, rows_ref, vocab_ref, other_ref, targets_ref, out_ref, flat_ref):
    blocks, part, lanes = rows_ref.shape
    parts = flat_ref.shape[0] // (blocks * part)
    count = lanes // parts
    for b in range(blocks):
        block = rows_ref[b].astype(F32)
        for n in range(parts):
            at = (b * parts + n) * part
            turned = block if n == 0 else pltpu.roll(block, lanes - n * count, 1)
            flat_ref[at : at + part, :] = turned.astype(BF16)
    target = targets_ref[pl.ds(at_ref[0], 1), :]
    sums = jnp.zeros((1, lanes), F32)
    hits = jnp.zeros((1, lanes), F32)
    for n, block in enumerate((vocab_ref, other_ref)):
        logits = nn(block[...], flat_ref[...])
        entry = iota(logits.shape, 0) + at_ref[1 + n]
        sums = sums + jnp.sum(jnp.exp(logits), axis=0, keepdims=True)
        hits = hits + jnp.sum(jnp.where(entry == target, logits, 0.0), axis=0, keepdims=True)
    lane = iota(sums.shape, 1)
    out_ref[...] = jnp.broadcast_to(jnp.where(lane < count, sums, pltpu.roll(hits, count, 1)), out_ref.shape)


SHIFTS = (0, 1, 3, 2)
RING = (0, 7, 1, 6, 2, 5, 3, 4)


def exchange(value, axes):
    return lax.all_to_all(value, axes, 0, 0, tiled=True)


def spread_all(value, axes, count):
    return lax.all_to_all(
        jnp.broadcast_to(value[None], (count, *value.shape)), axes, 0, 0, tiled=True
    )


def from_shift(value, axis, shift):
    count = lax.axis_size(axis)
    return lax.ppermute(value, axis, [((i + shift) % count, i) for i in range(count)])


def around(value, axis, between):
    count = lax.axis_size(axis)
    left = right = value
    got = [value]
    for hop in range(3):
        if hop:
            left, right = between(hop, left, right)
        left = from_shift(left, axis, count - 1)
        right = from_shift(right, axis, 1)
        got += [left, right]
    left, right = between(3, left, right)
    return [*got, from_shift(left, axis, count - 1)]


def shards(tokens, routes, gates, w_gate, w_up, w_down, shared_gate, shared_up, shared_down, vocab, targets):
    nx, ny = lax.axis_size("x"), lax.axis_size("y")
    nz, nc = lax.axis_size("z"), lax.axis_size("core")
    groups, lanes = nz * nc, nx * ny
    rows, width = tokens.shape
    cap = rows // 2
    near = cap // nx
    count = groups * near
    lines = near + EIGHT
    units = w_gate.shape[1]
    tok = tokens.T
    x_at = lax.axis_index("x").astype(jnp.int32).reshape(1)
    y_at = lax.axis_index("y").astype(jnp.int32).reshape(1)

    outgoing, slot, gate = call(
        dispatch_body,
        [
            shape((groups * nx, lines, rows)),
            shape((groups, rows), jnp.int32),
            shape((groups, rows), F32),
        ],
        [routes.T, gates.T, tok],
        far=range(3),
        scratch=[
            pltpu.VMEM(routes.T.shape, jnp.int32),
            pltpu.VMEM(gates.T.shape, F32),
            pltpu.VMEM(tok.shape, BF16),
            pltpu.SemaphoreType.DMA((3,)),
        ],
        limit=60,
    )
    arrived = exchange(outgoing, BOTH)
    arrived, t1, t3, t2 = lax.optimization_barrier((arrived, *[from_shift(tok, "x", shift) for shift in SHIFTS[1:]]))
    (spread,) = call(
        spread_body,
        [shape((nx * width, count + rows))],
        [x_at, arrived, tok, t1, t3, t2],
        scalars=1,
    )
    spread, own_gate, own_up = lax.optimization_barrier((spread, w_gate[0], w_up[0]))
    after = {"own_gate": own_gate, "own_up": own_up, "down": w_down[0].T}
    after["g1"] = from_shift(own_gate, "x", 1)
    after["u3"] = from_shift(own_up, "x", nx - 1)

    def tie(left, right, *names):
        left, right, *due = lax.optimization_barrier((left, right, *[after[n] for n in names]))
        after.update(zip(names, due))
        return left, right

    def between(hop, left, right):
        if hop == 1:
            left, right = tie(left, right, "own_gate", "own_up")
            after["g3"] = from_shift(after["own_gate"], "x", nx - 1)
            after["u1"] = from_shift(after["own_up"], "x", 1)
        if hop == 2:
            left, right = tie(left, right, "g1", "u3")
            after["g2"] = from_shift(after["g1"], "x", 1)
            after["u2"] = from_shift(after["u3"], "x", nx - 1)
        if hop == 3:
            left, right = tie(left, right, "g3", "u1", "down")
            after["d1"] = from_shift(after["down"], "x", 1)
            after["d3"] = from_shift(after["down"], "x", nx - 1)
        return left, right

    blocks = around(spread, "y", between)
    near_weights = [after[n] for n in ("own_gate", "own_up", "g1", "u1", "g3", "u3", "g2", "u2")]
    (hidden,) = call(
        hidden_body,
        [shape((ny, nx * units + units // 2 + EIGHT, count))],
        [y_at, *blocks, *near_weights, shared_gate, shared_up],
        scalars=1,
        far=(*range(1, len(RING)), *range(len(RING) + 1, len(RING) + 2 * nx + 3)),
        scratch=[
            pltpu.VMEM((lanes * width, count + rows), BF16),
            pltpu.VMEM((2 * (nx + 1) * units, lanes * width), BF16),
            pltpu.SemaphoreType.DMA((2 * nx + 2 + lanes,)),
        ],
        limit=56,
    )
    hidden, d3 = lax.optimization_barrier((hidden, after["d3"]))
    d1 = after["d1"]
    d2 = from_shift(d3, "x", nx - 1)
    all_hidden = exchange(hidden, "y")
    returned, own_shared = call(
        down_body,
        [shape((groups * nx, lines, rows)), shape((ny * units, rows))],
        [x_at, all_hidden, after["down"], d1, d3, d2],
        scalars=1,
        far=range(2, 2 + nx),
        scratch=[
            pltpu.VMEM((lanes * units, count), BF16),
            pltpu.VMEM((2 * nx * rows, lanes * units), BF16),
            pltpu.SemaphoreType.DMA((nx * (1 + rows // (width - rows)),)),
        ],
        limit=40,
    )
    near_shared = [own_shared, *[from_shift(own_shared, "x", shift) for shift in SHIFTS[1:]]]
    back = exchange(returned, BOTH)
    layer_out, scored = call(
        combine_body,
        [shape((width, rows)), shape((groups, SCORE_E, width))],
        [x_at, shared_down.T, slot, gate, back, tok, *near_shared],
        scalars=1,
        far=(1,),
        scratch=[pltpu.VMEM((width, lanes * units), BF16), pltpu.SemaphoreType.DMA((1,))],
    )
    scored, moved = lax.optimization_barrier((scored, vocab))
    other_vocab = lax.ppermute(moved, "core", [(0, 1), (1, 0)])
    line_rows = exchange(scored, LINE).reshape(groups * SCORE_E, width)
    count = groups * SCORE_E // nc
    core = lax.axis_index("core").astype(jnp.int32)
    (packed,) = call(
        pack_body,
        [shape((lanes, width * count // (2 * cap), 2 * cap))],
        [core.reshape(1), line_rows],
        scalars=1,
    )
    every = exchange(packed, PLANE)
    place = lax.axis_index("x") * ny + lax.axis_index("y")
    first = [
        (((lax.axis_index("z") * nc + c) * lanes + place) * vocab.shape[0]).astype(jnp.int32)
        for c in (core, 1 - core)
    ]
    (sums,) = call(
        score_body,
        [shape((8, 2 * cap), F32)],
        [
            jnp.stack([core, *first]),
            every,
            vocab,
            other_vocab,
            jnp.tile(targets.reshape(nc, count), (1, 2 * cap // count)),
        ],
        scalars=1,
        scratch=[pltpu.VMEM((lanes * width, 2 * cap), BF16)],
    )
    sums = jnp.sum(spread_all(sums[:1], PLANE, lanes), axis=0)
    sums = jnp.sum(spread_all(sums, LINE, groups).reshape(nz, nc, 2 * cap), axis=0)
    return layer_out.T, (sums[:, count : 2 * count] - jnp.log(sums[:, :count])).reshape(-1)


def solution(mesh):
    mesh = Mesh(mesh.devices.reshape(8, 2, 4, 8), ("z", "core", "x", "y"))
    placed = (
        P(LINE, PLANE),
        P(LINE, None),
        P(LINE, None),
        P(LINE, PLANE, None),
        P(LINE, PLANE, None),
        P(LINE, None, PLANE),
        P(PLANE, None),
        P(PLANE, None),
        P(None, PLANE),
        P((*LINE, *PLANE), None),
        P(),
    )
    return jax.shard_map(
        shards, mesh=mesh, in_specs=placed, out_specs=(P(LINE, PLANE), P()), check_vma=False
    )
```

```python
import jax
import jax.numpy as jnp
from jax import lax
from jax.experimental import pallas as pl
from jax.experimental.pallas import tpu as pltpu
from jax.sharding import Mesh
from jax.sharding import PartitionSpec as P

SCORE_E = 4
EIGHT = 8
F32 = jnp.float32
BF16 = jnp.bfloat16
LINE = ("z", "core")
PLANE = ("x", "y")
BOTH = ("z", "core", "x")


def call(body, outs, args, scalars=0, far=(), scratch=(), limit=16):
    specs = [
        pl.BlockSpec(memory_space=pltpu.SMEM if n < scalars else pltpu.HBM if n in far else pltpu.VMEM)
        for n in range(len(args))
    ]
    moved = sum(a.size * a.dtype.itemsize for a in args)
    moved += sum(o.size * o.dtype.itemsize for o in outs)
    return pl.pallas_call(
        body,
        out_shape=outs,
        in_specs=specs,
        out_specs=[pl.BlockSpec(memory_space=pltpu.VMEM) for _ in outs],
        scratch_shapes=list(scratch),
        cost_estimate=pl.CostEstimate(flops=0, bytes_accessed=moved, transcendentals=0),
        compiler_params=pltpu.CompilerParams(vmem_limit_bytes=limit << 20),
    )(*args)


def fetch(pairs, sems):
    copies = [pltpu.make_async_copy(src, dst, sems.at[n]) for n, (src, dst) in enumerate(pairs)]
    for copy in copies:
        copy.start()
    return copies


def shape(dims, dtype=BF16):
    return jax.ShapeDtypeStruct(dims, dtype)


def nn(a, b):
    return lax.dot_general(a, b, (((1,), (0,)), ((), ())), preferred_element_type=F32)


def nt(a, b):
    return lax.dot_general(a, b, (((1,), (1,)), ((), ())), preferred_element_type=F32)


def iota(dims, axis):
    return lax.broadcasted_iota(jnp.int32, dims, axis)


class Fold:
    def __init__(self, width, lanes, near):
        self.width, self.lanes, self.near = width, lanes, near
        self.rest = width - lanes
        self.parts = lanes // self.rest
        self.per = near // self.parts
        self.lines = near + EIGHT

    def to_lines(self, rows, axis):
        dims = (rows // self.near * EIGHT, rows)
        dims = dims if axis == 0 else dims[::-1]
        line, row = iota(dims, axis), iota(dims, 1 - axis)
        same = lax.div(line, EIGHT) == lax.div(row, self.near)
        hit = same & (lax.rem(line, EIGHT) == lax.rem(row, self.per))
        return hit

    def part_of(self, row):
        return lax.div(lax.rem(row, self.near), self.per)


def bf(mask):
    return jnp.where(mask, 1.0, 0.0).astype(BF16)


def tn(a, b):
    return lax.dot_general(a, b, (((0,), (0,)), ((), ())), preferred_element_type=F32)


def routing(routes_ref, gates_ref, experts):
    top, rows = routes_ref.shape
    expert = iota((experts, rows), 0)
    named = jnp.zeros((experts, rows), F32)
    gate = jnp.zeros((experts, rows), F32)
    for k in range(top):
        hit = expert == routes_ref[k : k + 1, :]
        named = named + jnp.where(hit, 1.0, 0.0)
        gate = gate + jnp.where(hit, gates_ref[k : k + 1, :], 0.0)
    before = jnp.where(iota((rows, rows), 0) < iota((rows, rows), 1), 1.0, 0.0).astype(BF16)
    earlier = nn(named.astype(BF16), before)
    return jnp.where(named > 0.0, earlier, -1.0).astype(jnp.int32), gate


def dispatch_body(routes_far, gates_far, tok_far, out_ref, slot_ref, gate_ref, routes_ref, gates_ref, tok_ref, sems):
    pairs = [(routes_far, routes_ref), (gates_far, gates_ref), (tok_far, tok_ref)]
    for copy in fetch(pairs, sems):
        copy.wait()
    experts = slot_ref.shape[0]
    width, rows = tok_ref.shape
    lanes = out_ref.shape[2]
    near = out_ref.shape[1] - EIGHT
    fold = Fold(width, lanes, near)
    cap = out_ref.shape[0] // experts * near
    slot, gate = routing(routes_ref, gates_ref, experts)
    slot_ref[...] = slot
    gate_ref[...] = gate
    tok = tok_ref[...]
    tok = jnp.concatenate([tok[:lanes]] + [tok[lanes:]] * fold.parts, axis=0)
    place = iota((cap, rows), 0)
    several = 2 * lanes // cap
    lines = bf(fold.to_lines(several * cap, 0))
    dims = (several * cap, lanes)
    own_part = fold.part_of(iota(dims, 0)) == lax.div(iota(dims, 1), fold.rest)
    for first in range(0, experts, several):
        sel = jnp.concatenate([bf(slot[e : e + 1, :] == place) for e in range(first, first + several)], axis=0)
        out = nt(sel, tok)
        rest = nn(lines, jnp.where(own_part, out[:, lanes:], 0.0).astype(BF16))
        for n in range(several * cap // near):
            piece = first * cap // near + n
            out_ref[piece, :near, :] = out[n * near : (n + 1) * near, :lanes].astype(BF16)
            out_ref[piece, near:, :] = rest[n * EIGHT : (n + 1) * EIGHT, :].astype(BF16)


def spread_body(x_ref, in_ref, *refs):
    *tokens, out_ref = refs
    nx = len(tokens)
    width, rows = tokens[0].shape
    lanes = in_ref.shape[2]
    near = in_ref.shape[1] - EIGHT
    groups = in_ref.shape[0] // nx
    fold = Fold(width, lanes, near)
    count = groups * near
    eye = bf(iota((count, count), 0) == iota((count, count), 1))
    lines = fold.to_lines(count, 0)
    part = fold.part_of(iota(lines.shape, 1))
    takes = [bf(lines & (part == q)) for q in range(fold.parts)]
    for x in range(nx):
        full = jnp.concatenate([in_ref[g * nx + x, :near, :] for g in range(groups)], axis=0)
        rest = jnp.concatenate([in_ref[g * nx + x, near:, :].astype(F32) for g in range(groups)], axis=0).astype(BF16)
        out_ref[x * width : x * width + lanes, :count] = tn(full, eye).astype(BF16)
        tail = jnp.zeros((fold.rest, count), F32)
        for q, take in enumerate(takes):
            tail = tail + tn(rest, take)[q * fold.rest : (q + 1) * fold.rest]
        out_ref[x * width + lanes : (x + 1) * width, :count] = tail.astype(BF16)
    for tok, shift in zip(tokens, SHIFTS):
        at = pl.multiple_of(lax.rem(x_ref[0] + shift, nx) * width, width)
        out_ref[pl.ds(at, width), count:] = tok[...]


def glu(gate, up):
    return (gate / (1.0 + jnp.exp(-gate)) * up).astype(BF16)


def hidden_body(y_ref, *refs):
    blocks = refs[: len(RING)]
    out_ref, flat_ref, weight_ref, sems = refs[-4:]
    weights = refs[len(RING) : -4]
    nx = len(weights) // 2 - 1
    units = weights[0].shape[0]
    width = blocks[0].shape[0] // nx
    ny = flat_ref.shape[0] // (nx * width)
    top = nx * units
    depth = ny * width
    pairs = []
    for x in range(nx):
        span = slice(x * depth, (x + 1) * depth)
        for n, weight in enumerate(weights):
            at = n // 2 * units + (n % 2) * top if n < 2 * nx else n * units
            pairs.append((weight.at[:, span], weight_ref.at[at : at + units, span]))
        for block, shift in zip(blocks, RING):
            at = pl.multiple_of(x * depth + lax.rem(y_ref[0] + shift, ny) * width, width)
            pairs.append((block.at[x * width : (x + 1) * width, :], flat_ref.at[pl.ds(at, width), :]))
    copies = fetch(pairs, sems)
    cols = out_ref.shape[2]
    routed = jnp.zeros((2 * top, cols), F32)
    own = jnp.zeros((2 * units, flat_ref.shape[1] - cols), F32)
    each = len(copies) // nx
    for x in range(nx):
        for copy in copies[x * each : (x + 1) * each]:
            copy.wait()
        span = slice(x * depth, (x + 1) * depth)
        routed = routed + nn(weight_ref[: 2 * top, span], flat_ref[span, :cols])
        own = own + nn(weight_ref[2 * top :, span], flat_ref[span, cols:])
    routed = glu(routed[:top], routed[top:])
    own = glu(own[:units], own[units:])
    fold = units // 2
    folded = jnp.concatenate([own[:fold], own[fold:]], axis=1)
    for y in range(ny):
        out_ref[y, :top, :] = routed
        out_ref[y, top : top + fold, :] = folded


def down_body(x_ref, hidden_ref, *refs):
    *weights, out_ref, shared_ref, flat_ref, down_ref, sems = refs
    nx = len(weights)
    width = weights[0].shape[0]
    lanes = out_ref.shape[2]
    near = out_ref.shape[1] - EIGHT
    fold = Fold(width, lanes, near)
    pairs = []
    for n, weight in enumerate(weights):
        base = 2 * n * lanes
        pairs.append((weight.at[:lanes, :], down_ref.at[base : base + lanes, :]))
        for q in range(fold.parts):
            at = base + lanes + q * fold.rest
            pairs.append((weight.at[lanes:, :], down_ref.at[at : at + fold.rest, :]))
    copies = fetch(pairs, sems)
    ny = hidden_ref.shape[0]
    units = flat_ref.shape[0] // (nx * ny)
    count = flat_ref.shape[1]
    own = [lax.rem(x_ref[0] + shift, nx) for shift in SHIFTS]
    half = units // 2
    for y in range(ny):
        for n in range(nx):
            at = pl.multiple_of((own[n] * ny + y) * units, units)
            flat_ref[pl.ds(at, units), :] = hidden_ref[y, n * units : (n + 1) * units, :]
        both = hidden_ref[y, nx * units : nx * units + half, :]
        shared_ref[y * units : y * units + half, :] = both[:, :lanes]
        shared_ref[y * units + half : (y + 1) * units, :] = both[:, lanes:]
    eye = bf(iota((count, count), 0) == iota((count, count), 1))
    lines = bf(fold.to_lines(count, 0))
    dims = (lanes, count)
    own_part = lax.div(iota(dims, 0), fold.rest) == fold.part_of(iota(dims, 1))
    for copy in copies:
        copy.wait()
    outs = nn(down_ref[...], flat_ref[...])
    for n in range(nx):
        out = outs[2 * n * lanes : 2 * (n + 1) * lanes]
        full = nt(eye, out[:lanes].astype(BF16)).astype(BF16)
        rest = nt(lines, jnp.where(own_part, out[lanes:], 0.0).astype(BF16))
        for g in range(count // near):
            out_ref[g * nx + own[n], :near, :] = full[g * near : (g + 1) * near, :]
            out_ref[g * nx + own[n], near:, :] = rest[g * EIGHT : (g + 1) * EIGHT, :].astype(BF16)


def combine_body(x_ref, down_far, slot_ref, gate_ref, back_ref, tok_ref, *refs):
    *hidden, out_ref, scored_ref, down_ref, sems = refs
    copies = fetch([(down_far, down_ref)], sems)
    experts, rows = slot_ref.shape
    width = tok_ref.shape[0]
    lanes = back_ref.shape[2]
    near = back_ref.shape[1] - EIGHT
    fold = Fold(width, lanes, near)
    pieces = back_ref.shape[0] // experts
    cap = pieces * near
    several = 2 * lanes // cap

    def mix(first, target):
        weigh = [
            jnp.where(slot_ref[e : e + 1, :] == target, gate_ref[e : e + 1, :], 0.0)
            for e in range(first, first + several)
        ]
        weigh = jnp.concatenate(weigh, axis=0)
        head = weigh.astype(BF16)
        return [head, (weigh - head.astype(F32)).astype(BF16)]

    place = iota((cap, rows), 0)
    line = iota((pieces * EIGHT, rows), 0)
    line, piece = lax.rem(line, EIGHT), lax.div(line, EIGHT)
    full = jnp.zeros((lanes, rows), F32)
    rest = jnp.zeros((fold.rest, rows), F32)
    for first in range(0, experts, several):
        span = range(first * pieces, (first + several) * pieces)
        block = jnp.concatenate([back_ref[n, :near, :] for n in span], axis=0)
        got = tn(block, jnp.concatenate(mix(first, place), axis=1))
        full = full + got[:, :rows] + got[:, rows:]
        block = jnp.concatenate([back_ref[n, near:, :].astype(F32) for n in span], axis=0).astype(BF16)
        terms = []
        for q in range(fold.parts):
            target = jnp.where(line < fold.per, piece * near + q * fold.per + line, -2)
            terms += mix(first, target)
        got = tn(block, jnp.concatenate(terms, axis=1))
        for q in range(fold.parts):
            part = got[q * fold.rest : (q + 1) * fold.rest]
            rest = rest + part[:, 2 * q * rows : (2 * q + 1) * rows] + part[:, (2 * q + 1) * rows : (2 * q + 2) * rows]
    routed = jnp.concatenate([full, rest], axis=0)
    copies[0].wait()
    shared = jnp.zeros((width, rows), F32)
    for shift, units in zip(SHIFTS, hidden):
        depth = units.shape[0]
        at = pl.multiple_of(lax.rem(x_ref[0] + shift, len(hidden)) * depth, lanes)
        shared = shared + nn(down_ref[:, pl.ds(at, depth)], units[...])
    out = (tok_ref[...].astype(F32) + shared + routed).astype(BF16)
    out_ref[...] = out
    take = iota((EIGHT, rows), 1) == rows - SCORE_E + iota((EIGHT, rows), 0)
    scored = nt(bf(take), out).astype(BF16)
    for g in range(scored_ref.shape[0]):
        scored_ref[g] = scored[:SCORE_E]


def pack_body(core_ref, rows_ref, out_ref):
    count, width = rows_ref.shape[0] // 2, rows_ref.shape[1]
    part = out_ref.shape[1]
    eye = jnp.where(iota((count, count), 0) == iota((count, count), 1), 1.0, 0.0).astype(BF16)
    mine = rows_ref[pl.ds(pl.multiple_of(core_ref[0] * count, count), count), :]
    flip = lax.dot_general(mine, eye, (((0,), (0,)), ((), ())), preferred_element_type=F32)
    packed = jnp.concatenate([flip[n : n + part] for n in range(0, width, part)], axis=1).astype(BF16)
    for n in range(out_ref.shape[0]):
        out_ref[n] = packed


def score_body(at_ref, rows_ref, vocab_ref, other_ref, targets_ref, out_ref, flat_ref):
    blocks, part, lanes = rows_ref.shape
    parts = flat_ref.shape[0] // (blocks * part)
    count = lanes // parts
    for b in range(blocks):
        block = rows_ref[b].astype(F32)
        for n in range(parts):
            at = (b * parts + n) * part
            turned = block if n == 0 else pltpu.roll(block, lanes - n * count, 1)
            flat_ref[at : at + part, :] = turned.astype(BF16)
    target = targets_ref[pl.ds(at_ref[0], 1), :]
    sums = jnp.zeros((1, lanes), F32)
    hits = jnp.zeros((1, lanes), F32)
    for n, block in enumerate((vocab_ref, other_ref)):
        logits = nn(block[...], flat_ref[...])
        entry = iota(logits.shape, 0) + at_ref[1 + n]
        sums = sums + jnp.sum(jnp.exp(logits), axis=0, keepdims=True)
        hits = hits + jnp.sum(jnp.where(entry == target, logits, 0.0), axis=0, keepdims=True)
    lane = iota(sums.shape, 1)
    out_ref[...] = jnp.broadcast_to(jnp.where(lane < count, sums, pltpu.roll(hits, count, 1)), out_ref.shape)


SHIFTS = (0, 1, 3, 2)
RING = (0, 7, 1, 6, 2, 5, 3, 4)


def exchange(value, axes):
    return lax.all_to_all(value, axes, 0, 0, tiled=True)


def spread_all(value, axes, count):
    return lax.all_to_all(
        jnp.broadcast_to(value[None], (count, *value.shape)), axes, 0, 0, tiled=True
    )


def from_shift(value, axis, shift):
    count = lax.axis_size(axis)
    return lax.ppermute(value, axis, [((i + shift) % count, i) for i in range(count)])


def around(value, axis, between):
    count = lax.axis_size(axis)
    left = right = value
    got = [value]
    for hop in range(3):
        if hop:
            left, right = between(hop, left, right)
        left = from_shift(left, axis, count - 1)
        right = from_shift(right, axis, 1)
        got += [left, right]
    left, right = between(3, left, right)
    return [*got, from_shift(left, axis, count - 1)]


def shards(tokens, routes, gates, w_gate, w_up, w_down, shared_gate, shared_up, shared_down, vocab, targets):
    nx, ny = lax.axis_size("x"), lax.axis_size("y")
    nz, nc = lax.axis_size("z"), lax.axis_size("core")
    groups, lanes = nz * nc, nx * ny
    rows, width = tokens.shape
    cap = rows // 2
    near = cap // nx
    count = groups * near
    lines = near + EIGHT
    units = w_gate.shape[1]
    tok = tokens.T
    x_at = lax.axis_index("x").astype(jnp.int32).reshape(1)
    y_at = lax.axis_index("y").astype(jnp.int32).reshape(1)

    outgoing, slot, gate = call(
        dispatch_body,
        [
            shape((groups * nx, lines, rows)),
            shape((groups, rows), jnp.int32),
            shape((groups, rows), F32),
        ],
        [routes.T, gates.T, tok],
        far=range(3),
        scratch=[
            pltpu.VMEM(routes.T.shape, jnp.int32),
            pltpu.VMEM(gates.T.shape, F32),
            pltpu.VMEM(tok.shape, BF16),
            pltpu.SemaphoreType.DMA((3,)),
        ],
        limit=60,
    )
    arrived = exchange(outgoing, BOTH)
    arrived, t1, t3, t2 = lax.optimization_barrier((arrived, *[from_shift(tok, "x", shift) for shift in SHIFTS[1:]]))
    (spread,) = call(
        spread_body,
        [shape((nx * width, count + rows))],
        [x_at, arrived, tok, t1, t3, t2],
        scalars=1,
    )
    spread, own_gate, own_up = lax.optimization_barrier((spread, w_gate[0], w_up[0]))
    after = {"own_gate": own_gate, "own_up": own_up, "down": w_down[0].T}
    after["g1"] = from_shift(own_gate, "x", 1)
    after["u3"] = from_shift(own_up, "x", nx - 1)

    def tie(left, right, *names):
        left, right, *due = lax.optimization_barrier((left, right, *[after[n] for n in names]))
        after.update(zip(names, due))
        return left, right

    def between(hop, left, right):
        if hop == 1:
            left, right = tie(left, right, "own_gate", "own_up")
            after["g3"] = from_shift(after["own_gate"], "x", nx - 1)
            after["u1"] = from_shift(after["own_up"], "x", 1)
        if hop == 2:
            left, right = tie(left, right, "g1", "u3")
            after["g2"] = from_shift(after["g1"], "x", 1)
            after["u2"] = from_shift(after["u3"], "x", nx - 1)
        if hop == 3:
            left, right = tie(left, right, "g3", "u1", "down")
            after["d1"] = from_shift(after["down"], "x", 1)
            after["d3"] = from_shift(after["down"], "x", nx - 1)
        return left, right

    blocks = around(spread, "y", between)
    near_weights = [after[n] for n in ("own_gate", "own_up", "g1", "u1", "g3", "u3", "g2", "u2")]
    (hidden,) = call(
        hidden_body,
        [shape((ny, nx * units + units // 2 + EIGHT, count))],
        [y_at, *blocks, *near_weights, shared_gate, shared_up],
        scalars=1,
        far=(*range(1, len(RING)), *range(len(RING) + 1, len(RING) + 2 * nx + 3)),
        scratch=[
            pltpu.VMEM((lanes * width, count + rows), BF16),
            pltpu.VMEM((2 * (nx + 1) * units, lanes * width), BF16),
            pltpu.SemaphoreType.DMA((nx * (2 * nx + 2 + ny),)),
        ],
        limit=56,
    )
    hidden, d3 = lax.optimization_barrier((hidden, after["d3"]))
    d1 = after["d1"]
    d2 = from_shift(d3, "x", nx - 1)
    all_hidden = exchange(hidden, "y")
    returned, own_shared = call(
        down_body,
        [shape((groups * nx, lines, rows)), shape((ny * units, rows))],
        [x_at, all_hidden, after["down"], d1, d3, d2],
        scalars=1,
        far=range(2, 2 + nx),
        scratch=[
            pltpu.VMEM((lanes * units, count), BF16),
            pltpu.VMEM((2 * nx * rows, lanes * units), BF16),
            pltpu.SemaphoreType.DMA((nx * (1 + rows // (width - rows)),)),
        ],
        limit=40,
    )
    near_shared = [own_shared, *[from_shift(own_shared, "x", shift) for shift in SHIFTS[1:]]]
    back = exchange(returned, BOTH)
    layer_out, scored = call(
        combine_body,
        [shape((width, rows)), shape((groups, SCORE_E, width))],
        [x_at, shared_down.T, slot, gate, back, tok, *near_shared],
        scalars=1,
        far=(1,),
        scratch=[pltpu.VMEM((width, lanes * units), BF16), pltpu.SemaphoreType.DMA((1,))],
    )
    scored, moved = lax.optimization_barrier((scored, vocab))
    other_vocab = lax.ppermute(moved, "core", [(0, 1), (1, 0)])
    line_rows = exchange(scored, LINE).reshape(groups * SCORE_E, width)
    count = groups * SCORE_E // nc
    core = lax.axis_index("core").astype(jnp.int32)
    (packed,) = call(
        pack_body,
        [shape((lanes, width * count // (2 * cap), 2 * cap))],
        [core.reshape(1), line_rows],
        scalars=1,
    )
    every = exchange(packed, PLANE)
    place = lax.axis_index("x") * ny + lax.axis_index("y")
    first = [
        (((lax.axis_index("z") * nc + c) * lanes + place) * vocab.shape[0]).astype(jnp.int32)
        for c in (core, 1 - core)
    ]
    (sums,) = call(
        score_body,
        [shape((8, 2 * cap), F32)],
        [
            jnp.stack([core, *first]),
            every,
            vocab,
            other_vocab,
            jnp.tile(targets.reshape(nc, count), (1, 2 * cap // count)),
        ],
        scalars=1,
        scratch=[pltpu.VMEM((lanes * width, 2 * cap), BF16)],
    )
    sums = jnp.sum(spread_all(sums[:1], PLANE, lanes), axis=0)
    sums = jnp.sum(spread_all(sums, LINE, groups).reshape(nz, nc, 2 * cap), axis=0)
    return layer_out.T, (sums[:, count : 2 * count] - jnp.log(sums[:, :count])).reshape(-1)


def solution(mesh):
    mesh = Mesh(mesh.devices.reshape(8, 2, 4, 8), ("z", "core", "x", "y"))
    placed = (
        P(LINE, PLANE),
        P(LINE, None),
        P(LINE, None),
        P(LINE, PLANE, None),
        P(LINE, PLANE, None),
        P(LINE, None, PLANE),
        P(PLANE, None),
        P(PLANE, None),
        P(None, PLANE),
        P((*LINE, *PLANE), None),
        P(),
    )
    return jax.shard_map(
        shards, mesh=mesh, in_specs=placed, out_specs=(P(LINE, PLANE), P()), check_vma=False
    )
```

```python
import jax
import jax.numpy as jnp
from jax import lax
from jax.experimental import pallas as pl
from jax.experimental.pallas import tpu as pltpu
from jax.sharding import Mesh
from jax.sharding import PartitionSpec as P

SCORE_E = 4
EIGHT = 8
F32 = jnp.float32
BF16 = jnp.bfloat16
LINE = ("z", "core")
PLANE = ("x", "y")
BOTH = ("z", "core", "x")


def call(body, outs, args, scalars=0, far=(), scratch=(), limit=16):
    specs = [
        pl.BlockSpec(memory_space=pltpu.SMEM if n < scalars else pltpu.HBM if n in far else pltpu.VMEM)
        for n in range(len(args))
    ]
    moved = sum(a.size * a.dtype.itemsize for a in args)
    moved += sum(o.size * o.dtype.itemsize for o in outs)
    return pl.pallas_call(
        body,
        out_shape=outs,
        in_specs=specs,
        out_specs=[pl.BlockSpec(memory_space=pltpu.VMEM) for _ in outs],
        scratch_shapes=list(scratch),
        cost_estimate=pl.CostEstimate(flops=0, bytes_accessed=moved, transcendentals=0),
        compiler_params=pltpu.CompilerParams(vmem_limit_bytes=limit << 20),
    )(*args)


def fetch(pairs, sems):
    copies = [pltpu.make_async_copy(src, dst, sems.at[n]) for n, (src, dst) in enumerate(pairs)]
    for copy in copies:
        copy.start()
    return copies


def shape(dims, dtype=BF16):
    return jax.ShapeDtypeStruct(dims, dtype)


def nn(a, b):
    return lax.dot_general(a, b, (((1,), (0,)), ((), ())), preferred_element_type=F32)


def nt(a, b):
    return lax.dot_general(a, b, (((1,), (1,)), ((), ())), preferred_element_type=F32)


def iota(dims, axis):
    return lax.broadcasted_iota(jnp.int32, dims, axis)


class Fold:
    def __init__(self, width, lanes, near):
        self.width, self.lanes, self.near = width, lanes, near
        self.rest = width - lanes
        self.parts = lanes // self.rest
        self.per = near // self.parts
        self.lines = near + EIGHT

    def to_lines(self, rows, axis):
        dims = (rows // self.near * EIGHT, rows)
        dims = dims if axis == 0 else dims[::-1]
        line, row = iota(dims, axis), iota(dims, 1 - axis)
        same = lax.div(line, EIGHT) == lax.div(row, self.near)
        hit = same & (lax.rem(line, EIGHT) == lax.rem(row, self.per))
        return hit

    def part_of(self, row):
        return lax.div(lax.rem(row, self.near), self.per)


def bf(mask):
    return jnp.where(mask, 1.0, 0.0).astype(BF16)


def tn(a, b):
    return lax.dot_general(a, b, (((0,), (0,)), ((), ())), preferred_element_type=F32)


def routing(routes_ref, gates_ref, experts):
    top, rows = routes_ref.shape
    expert = iota((experts, rows), 0)
    named = jnp.zeros((experts, rows), F32)
    gate = jnp.zeros((experts, rows), F32)
    for k in range(top):
        hit = expert == routes_ref[k : k + 1, :]
        named = named + jnp.where(hit, 1.0, 0.0)
        gate = gate + jnp.where(hit, gates_ref[k : k + 1, :], 0.0)
    before = jnp.where(iota((rows, rows), 0) < iota((rows, rows), 1), 1.0, 0.0).astype(BF16)
    earlier = nn(named.astype(BF16), before)
    return jnp.where(named > 0.0, earlier, -1.0).astype(jnp.int32), gate


def dispatch_body(routes_far, gates_far, tok_far, out_ref, slot_ref, gate_ref, routes_ref, gates_ref, tok_ref, sems):
    pairs = [(routes_far, routes_ref), (gates_far, gates_ref), (tok_far, tok_ref)]
    for copy in fetch(pairs, sems):
        copy.wait()
    experts = slot_ref.shape[0]
    width, rows = tok_ref.shape
    lanes = out_ref.shape[2]
    near = out_ref.shape[1] - EIGHT
    fold = Fold(width, lanes, near)
    cap = out_ref.shape[0] // experts * near
    slot, gate = routing(routes_ref, gates_ref, experts)
    slot_ref[...] = slot
    gate_ref[...] = gate
    tok = tok_ref[...]
    tok = jnp.concatenate([tok[:lanes]] + [tok[lanes:]] * fold.parts, axis=0)
    place = iota((cap, rows), 0)
    several = 2 * lanes // cap
    lines = bf(fold.to_lines(several * cap, 0))
    dims = (several * cap, lanes)
    own_part = fold.part_of(iota(dims, 0)) == lax.div(iota(dims, 1), fold.rest)
    for first in range(0, experts, several):
        sel = jnp.concatenate([bf(slot[e : e + 1, :] == place) for e in range(first, first + several)], axis=0)
        out = nt(sel, tok)
        rest = nn(lines, jnp.where(own_part, out[:, lanes:], 0.0).astype(BF16))
        for n in range(several * cap // near):
            piece = first * cap // near + n
            out_ref[piece, :near, :] = out[n * near : (n + 1) * near, :lanes].astype(BF16)
            out_ref[piece, near:, :] = rest[n * EIGHT : (n + 1) * EIGHT, :].astype(BF16)


def spread_body(x_ref, in_ref, *refs):
    *tokens, out_ref = refs
    nx = len(tokens)
    width, rows = tokens[0].shape
    lanes = in_ref.shape[2]
    near = in_ref.shape[1] - EIGHT
    groups = in_ref.shape[0] // nx
    fold = Fold(width, lanes, near)
    count = groups * near
    eye = bf(iota((count, count), 0) == iota((count, count), 1))
    lines = fold.to_lines(count, 0)
    part = fold.part_of(iota(lines.shape, 1))
    takes = [bf(lines & (part == q)) for q in range(fold.parts)]
    for x in range(nx):
        full = jnp.concatenate([in_ref[g * nx + x, :near, :] for g in range(groups)], axis=0)
        rest = jnp.concatenate([in_ref[g * nx + x, near:, :].astype(F32) for g in range(groups)], axis=0).astype(BF16)
        out_ref[x * width : x * width + lanes, :count] = tn(full, eye).astype(BF16)
        tail = jnp.zeros((fold.rest, count), F32)
        for q, take in enumerate(takes):
            tail = tail + tn(rest, take)[q * fold.rest : (q + 1) * fold.rest]
        out_ref[x * width + lanes : (x + 1) * width, :count] = tail.astype(BF16)
    for tok, shift in zip(tokens, SHIFTS):
        at = pl.multiple_of(lax.rem(x_ref[0] + shift, nx) * width, width)
        out_ref[pl.ds(at, width), count:] = tok[...]


def glu(gate, up):
    return (gate / (1.0 + jnp.exp(-gate)) * up).astype(BF16)


def hidden_body(y_ref, *refs):
    blocks = refs[: len(RING)]
    out_ref, flat_ref, weight_ref, sems = refs[-4:]
    weights = refs[len(RING) : -4]
    nx = len(weights) // 2 - 1
    units = weights[0].shape[0]
    width = blocks[0].shape[0] // nx
    ny = flat_ref.shape[0] // (nx * width)
    top = nx * units
    pairs = []
    for n, weight in enumerate(weights):
        at = n // 2 * units + (n % 2) * top if n < 2 * nx else n * units
        pairs.append((weight, weight_ref.at[at : at + units, :]))
    for block, shift in zip(blocks, RING):
        y = lax.rem(y_ref[0] + shift, ny)
        for n in range(nx):
            at = pl.multiple_of((n * ny + y) * width, width)
            pairs.append((block.at[n * width : (n + 1) * width, :], flat_ref.at[pl.ds(at, width), :]))
    for copy in fetch(pairs, sems):
        copy.wait()
    cols = out_ref.shape[2]
    both = nn(weight_ref[: 2 * top, :], flat_ref[:, :cols])
    routed = glu(both[:top], both[top:])
    both = nn(weight_ref[2 * top :, :], flat_ref[:, cols:])
    own = glu(both[:units], both[units:])
    fold = units // 2
    folded = jnp.concatenate([own[:fold], own[fold:]], axis=1)
    for y in range(ny):
        out_ref[y, :top, :] = routed
        out_ref[y, top : top + fold, :] = folded


def down_body(x_ref, hidden_ref, *refs):
    *weights, out_ref, shared_ref, flat_ref, down_ref, sems = refs
    nx = len(weights)
    width = weights[0].shape[0]
    lanes = out_ref.shape[2]
    near = out_ref.shape[1] - EIGHT
    fold = Fold(width, lanes, near)
    pairs = []
    for n, weight in enumerate(weights):
        base = 2 * n * lanes
        pairs.append((weight.at[:lanes, :], down_ref.at[base : base + lanes, :]))
        for q in range(fold.parts):
            at = base + lanes + q * fold.rest
            pairs.append((weight.at[lanes:, :], down_ref.at[at : at + fold.rest, :]))
    copies = fetch(pairs, sems)
    ny = hidden_ref.shape[0]
    units = flat_ref.shape[0] // (nx * ny)
    count = flat_ref.shape[1]
    own = [lax.rem(x_ref[0] + shift, nx) for shift in SHIFTS]
    half = units // 2
    for y in range(ny):
        for n in range(nx):
            at = pl.multiple_of((own[n] * ny + y) * units, units)
            flat_ref[pl.ds(at, units), :] = hidden_ref[y, n * units : (n + 1) * units, :]
        both = hidden_ref[y, nx * units : nx * units + half, :]
        shared_ref[y * units : y * units + half, :] = both[:, :lanes]
        shared_ref[y * units + half : (y + 1) * units, :] = both[:, lanes:]
    eye = bf(iota((count, count), 0) == iota((count, count), 1))
    lines = bf(fold.to_lines(count, 0))
    dims = (lanes, count)
    own_part = lax.div(iota(dims, 0), fold.rest) == fold.part_of(iota(dims, 1))
    for copy in copies:
        copy.wait()
    outs = nn(down_ref[...], flat_ref[...])
    for n in range(nx):
        out = outs[2 * n * lanes : 2 * (n + 1) * lanes]
        full = nt(eye, out[:lanes].astype(BF16)).astype(BF16)
        rest = nt(lines, jnp.where(own_part, out[lanes:], 0.0).astype(BF16))
        for g in range(count // near):
            out_ref[g * nx + own[n], :near, :] = full[g * near : (g + 1) * near, :]
            out_ref[g * nx + own[n], near:, :] = rest[g * EIGHT : (g + 1) * EIGHT, :].astype(BF16)


def combine_body(x_ref, down_far, slot_ref, gate_ref, back_ref, tok_ref, *refs):
    *hidden, out_ref, scored_ref, down_ref, sems = refs
    copies = fetch([(down_far, down_ref)], sems)
    experts, rows = slot_ref.shape
    width = tok_ref.shape[0]
    lanes = back_ref.shape[2]
    near = back_ref.shape[1] - EIGHT
    fold = Fold(width, lanes, near)
    pieces = back_ref.shape[0] // experts
    cap = pieces * near
    several = 2 * lanes // cap

    def mix(first, target):
        weigh = [
            jnp.where(slot_ref[e : e + 1, :] == target, gate_ref[e : e + 1, :], 0.0)
            for e in range(first, first + several)
        ]
        weigh = jnp.concatenate(weigh, axis=0)
        head = weigh.astype(BF16)
        return [head, (weigh - head.astype(F32)).astype(BF16)]

    place = iota((cap, rows), 0)
    line = iota((pieces * EIGHT, rows), 0)
    line, piece = lax.rem(line, EIGHT), lax.div(line, EIGHT)
    full = jnp.zeros((lanes, rows), F32)
    rest = jnp.zeros((fold.rest, rows), F32)
    for first in range(0, experts, several):
        span = range(first * pieces, (first + several) * pieces)
        block = jnp.concatenate([back_ref[n, :near, :] for n in span], axis=0)
        got = tn(block, jnp.concatenate(mix(first, place), axis=1))
        full = full + got[:, :rows] + got[:, rows:]
        block = jnp.concatenate([back_ref[n, near:, :].astype(F32) for n in span], axis=0).astype(BF16)
        terms = []
        for q in range(fold.parts):
            target = jnp.where(line < fold.per, piece * near + q * fold.per + line, -2)
            terms += mix(first, target)
        got = tn(block, jnp.concatenate(terms, axis=1))
        for q in range(fold.parts):
            part = got[q * fold.rest : (q + 1) * fold.rest]
            rest = rest + part[:, 2 * q * rows : (2 * q + 1) * rows] + part[:, (2 * q + 1) * rows : (2 * q + 2) * rows]
    routed = jnp.concatenate([full, rest], axis=0)
    copies[0].wait()
    shared = jnp.zeros((width, rows), F32)
    for shift, units in zip(SHIFTS, hidden):
        depth = units.shape[0]
        at = pl.multiple_of(lax.rem(x_ref[0] + shift, len(hidden)) * depth, lanes)
        shared = shared + nn(down_ref[:, pl.ds(at, depth)], units[...])
    out = (tok_ref[...].astype(F32) + shared + routed).astype(BF16)
    out_ref[...] = out
    take = iota((EIGHT, rows), 1) == rows - SCORE_E + iota((EIGHT, rows), 0)
    scored = nt(bf(take), out).astype(BF16)
    for g in range(scored_ref.shape[0]):
        scored_ref[g] = scored[:SCORE_E]


def pack_body(core_ref, rows_ref, out_ref):
    count, width = rows_ref.shape[0] // 2, rows_ref.shape[1]
    part = out_ref.shape[1]
    eye = jnp.where(iota((count, count), 0) == iota((count, count), 1), 1.0, 0.0).astype(BF16)
    mine = rows_ref[pl.ds(pl.multiple_of(core_ref[0] * count, count), count), :]
    flip = lax.dot_general(mine, eye, (((0,), (0,)), ((), ())), preferred_element_type=F32)
    packed = jnp.concatenate([flip[n : n + part] for n in range(0, width, part)], axis=1).astype(BF16)
    for n in range(out_ref.shape[0]):
        out_ref[n] = packed


def score_body(at_ref, rows_ref, vocab_ref, other_ref, targets_ref, out_ref, flat_ref):
    blocks, part, lanes = rows_ref.shape
    parts = flat_ref.shape[0] // (blocks * part)
    count = lanes // parts
    for b in range(blocks):
        block = rows_ref[b].astype(F32)
        for n in range(parts):
            at = (b * parts + n) * part
            turned = block if n == 0 else pltpu.roll(block, lanes - n * count, 1)
            flat_ref[at : at + part, :] = turned.astype(BF16)
    target = targets_ref[pl.ds(at_ref[0], 1), :]
    sums = jnp.zeros((1, lanes), F32)
    hits = jnp.zeros((1, lanes), F32)
    for n, block in enumerate((vocab_ref, other_ref)):
        logits = nn(block[...], flat_ref[...])
        entry = iota(logits.shape, 0) + at_ref[1 + n]
        sums = sums + jnp.sum(jnp.exp(logits), axis=0, keepdims=True)
        hits = hits + jnp.sum(jnp.where(entry == target, logits, 0.0), axis=0, keepdims=True)
    lane = iota(sums.shape, 1)
    out_ref[...] = jnp.broadcast_to(jnp.where(lane < count, sums, pltpu.roll(hits, count, 1)), out_ref.shape)


SHIFTS = (0, 1, 3, 2)
RING = (0, 7, 1, 6, 2, 5, 3, 4)


def exchange(value, axes):
    return lax.all_to_all(value, axes, 0, 0, tiled=True)


def spread_all(value, axes, count):
    return lax.all_to_all(
        jnp.broadcast_to(value[None], (count, *value.shape)), axes, 0, 0, tiled=True
    )


def from_shift(value, axis, shift):
    count = lax.axis_size(axis)
    return lax.ppermute(value, axis, [((i + shift) % count, i) for i in range(count)])


def around(value, axis, between):
    count = lax.axis_size(axis)
    left = right = value
    got = [value]
    for hop in range(3):
        if hop:
            left, right = between(hop, left, right)
        left = from_shift(left, axis, count - 1)
        right = from_shift(right, axis, 1)
        got += [left, right]
    left, right = between(3, left, right)
    return [*got, from_shift(left, axis, count - 1)]


def shards(tokens, routes, gates, w_gate, w_up, w_down, shared_gate, shared_up, shared_down, vocab, targets):
    nx, ny = lax.axis_size("x"), lax.axis_size("y")
    nz, nc = lax.axis_size("z"), lax.axis_size("core")
    groups, lanes = nz * nc, nx * ny
    rows, width = tokens.shape
    cap = rows // 2
    near = cap // nx
    count = groups * near
    lines = near + EIGHT
    units = w_gate.shape[1]
    tok = tokens.T
    x_at = lax.axis_index("x").astype(jnp.int32).reshape(1)
    y_at = lax.axis_index("y").astype(jnp.int32).reshape(1)

    outgoing, slot, gate = call(
        dispatch_body,
        [
            shape((groups * nx, lines, rows)),
            shape((groups, rows), jnp.int32),
            shape((groups, rows), F32),
        ],
        [routes.T, gates.T, tok],
        far=range(3),
        scratch=[
            pltpu.VMEM(routes.T.shape, jnp.int32),
            pltpu.VMEM(gates.T.shape, F32),
            pltpu.VMEM(tok.shape, BF16),
            pltpu.SemaphoreType.DMA((3,)),
        ],
        limit=60,
    )
    arrived = exchange(outgoing, BOTH)
    arrived, t1, t3, t2 = lax.optimization_barrier((arrived, *[from_shift(tok, "x", shift) for shift in SHIFTS[1:]]))
    (spread,) = call(
        spread_body,
        [shape((nx * width, count + rows))],
        [x_at, arrived, tok, t1, t3, t2],
        scalars=1,
    )
    spread, own_gate, own_up = lax.optimization_barrier((spread, w_gate[0], w_up[0]))
    after = {"own_gate": own_gate, "own_up": own_up, "down": w_down[0].T}
    after["g1"] = from_shift(own_gate, "x", 1)
    after["u3"] = from_shift(own_up, "x", nx - 1)

    def tie(left, right, *names):
        left, right, *due = lax.optimization_barrier((left, right, *[after[n] for n in names]))
        after.update(zip(names, due))
        return left, right

    def between(hop, left, right):
        if hop == 1:
            left, right = tie(left, right, "own_gate", "own_up")
            after["g3"] = from_shift(after["own_gate"], "x", nx - 1)
            after["u1"] = from_shift(after["own_up"], "x", 1)
        if hop == 2:
            left, right = tie(left, right, "g1", "u3")
            after["g2"] = from_shift(after["g1"], "x", 1)
            after["u2"] = from_shift(after["u3"], "x", nx - 1)
        if hop == 3:
            left, right = tie(left, right, "g3", "u1", "down")
            after["d1"] = from_shift(after["down"], "x", 1)
            after["d3"] = from_shift(after["down"], "x", nx - 1)
        return left, right

    blocks = around(spread, "y", between)
    near_weights = [after[n] for n in ("own_gate", "own_up", "g1", "u1", "g3", "u3", "g2", "u2")]
    (hidden,) = call(
        hidden_body,
        [shape((ny, nx * units + units // 2 + EIGHT, count))],
        [y_at, *blocks, *near_weights, shared_gate, shared_up],
        scalars=1,
        far=(*range(1, len(RING)), *range(len(RING) + 1, len(RING) + 2 * nx + 3)),
        scratch=[
            pltpu.VMEM((lanes * width, count + rows), BF16),
            pltpu.VMEM((2 * (nx + 1) * units, lanes * width), BF16),
            pltpu.SemaphoreType.DMA((2 * nx + 2 + lanes,)),
        ],
        limit=56,
    )
    hidden, d3 = lax.optimization_barrier((hidden, after["d3"]))
    d1 = after["d1"]
    d2 = from_shift(d3, "x", nx - 1)
    all_hidden = exchange(hidden, "y")
    returned, own_shared = call(
        down_body,
        [shape((groups * nx, lines, rows)), shape((ny * units, rows))],
        [x_at, all_hidden, after["down"], d1, d3, d2],
        scalars=1,
        far=range(2, 2 + nx),
        scratch=[
            pltpu.VMEM((lanes * units, count), BF16),
            pltpu.VMEM((2 * nx * rows, lanes * units), BF16),
            pltpu.SemaphoreType.DMA((nx * (1 + rows // (width - rows)),)),
        ],
        limit=40,
    )
    near_shared = [own_shared, *[from_shift(own_shared, "x", shift) for shift in SHIFTS[1:]]]
    back = exchange(returned, BOTH)
    layer_out, scored = call(
        combine_body,
        [shape((width, rows)), shape((groups, SCORE_E, width))],
        [x_at, shared_down.T, slot, gate, back, tok, *near_shared],
        scalars=1,
        far=(1,),
        scratch=[pltpu.VMEM((width, lanes * units), BF16), pltpu.SemaphoreType.DMA((1,))],
    )
    scored, moved = lax.optimization_barrier((scored, vocab))
    other_vocab = lax.ppermute(moved, "core", [(0, 1), (1, 0)])
    line_rows = exchange(scored, LINE).reshape(groups * SCORE_E, width)
    count = groups * SCORE_E // nc
    core = lax.axis_index("core").astype(jnp.int32)
    (packed,) = call(
        pack_body,
        [shape((lanes, width * count // (2 * cap), 2 * cap))],
        [core.reshape(1), line_rows],
        scalars=1,
    )
    every = exchange(packed, PLANE)
    place = lax.axis_index("x") * ny + lax.axis_index("y")
    first = [
        (((lax.axis_index("z") * nc + c) * lanes + place) * vocab.shape[0]).astype(jnp.int32)
        for c in (core, 1 - core)
    ]
    (sums,) = call(
        score_body,
        [shape((8, 2 * cap), F32)],
        [
            jnp.stack([core, *first]),
            every,
            vocab,
            other_vocab,
            jnp.tile(targets.reshape(nc, count), (1, 2 * cap // count)),
        ],
        scalars=1,
        scratch=[pltpu.VMEM((lanes * width, 2 * cap), BF16)],
    )
    sums = jnp.sum(spread_all(sums[:1], ("z", "x"), nz * nx), axis=0)
    sums = jnp.sum(spread_all(sums, ("core", "y"), nc * ny).reshape(nc, ny, 2 * cap), axis=1)
    return layer_out.T, (sums[:, count : 2 * count] - jnp.log(sums[:, :count])).reshape(-1)


def solution(mesh):
    mesh = Mesh(mesh.devices.reshape(8, 2, 4, 8), ("z", "core", "x", "y"))
    placed = (
        P(LINE, PLANE),
        P(LINE, None),
        P(LINE, None),
        P(LINE, PLANE, None),
        P(LINE, PLANE, None),
        P(LINE, None, PLANE),
        P(PLANE, None),
        P(PLANE, None),
        P(None, PLANE),
        P((*LINE, *PLANE), None),
        P(),
    )
    return jax.shard_map(
        shards, mesh=mesh, in_specs=placed, out_specs=(P(LINE, PLANE), P()), check_vma=False
    )
```
